128 devices in a mesh: row: 16 (over x_hi, y, core), col: 8 (over x_lo, z).
Axes of the slice: x: 4 (x_hi: 2, x_lo: 2; x = x_hi * 2 + x_lo), y: 4, z: 4, core: 2. Of those that a mesh axis runs over, the one named last changes fastest.
Arguments:
- pair: bfloat16 [384, 384, 128], P('row', 'col'), may hold values from -6 to 6
- gain: float32 [128], replicated, may hold values from 0.1 to 1.9
- projections: bfloat16 [5, 128, 128], replicated, may hold values from -0.5 to 0.5
- bias_weight: bfloat16 [128, 4], replicated, as said below
- valid_len: int32 [1], replicated, may hold values from 192 to 384
- out_cotangent: bfloat16 [384, 384, 128], P('row', 'col'), may hold values from -6 to 6
Outputs:
- attended: bfloat16 [384, 384, 128], P('row', 'col')
- pair_gradient: float32 [384, 384, 128], P('row', 'col')
- projection_grad: float32 [5, 128, 128], replicated
- bias_weight_grad: float32 [128, 4], replicated
- gain_gradient: float32 [128], replicated
The draws below stay inside these ranges and needn't reach their ends.
Inputs may be any that keep to these rules, and one draw needn't show every extreme that they name: `bias_weight`: scale of the bias projection entries is free; rows are drawn independently.
All inputs are finite; a program needn't handle non-finite values.
Results may differ from the reference program's by a relative error of at most 0.0045.
The reference program's roundings to bfloat16 on the way count: a program that leaves them out, or rounds other values in their place, can miss the bound.
Values may be sent and summed in bfloat16 or wider, within the bound.
No kernel may reach another device: no remote copies, remote signals or barrier semaphores. Data moves between devices by JAX's collectives and lax.ppermute only.
A program may use at most 64 MiB of HBM per device.

```python
import jax
import jax.numpy as jnp
from jax import lax

C = 128
H = 4
QB = 384
N = 384


def draw_bias_weight(key, part):
    base = jax.random.normal(jax.random.fold_in(key, 17), (C, H), jnp.float32) * C ** (-0.5)
    return base.astype(jnp.bfloat16)


def level_of(stream_key, shape, pieces, low, high):
    def one(position, shards_of):
        steps = jax.random.uniform(jax.random.fold_in(jax.random.fold_in(stream_key, 6), position), (shards_of,), jnp.float32, low / len(pieces), high / len(pieces))
        return jnp.repeat(jnp.exp(steps), shape[position] // shards_of).reshape((-1,) + (1,) * (len(shape) - position - 1))

    factor_of = one(*pieces[0])
    for cut in pieces[1:]:
        factor_of = factor_of * one(*cut)
    return factor_of


def normal_values(rng, shape, deviation, limit, pieces=(), kind=jnp.bfloat16):
    factor_of = level_of(rng, shape, pieces, -0.22, 0.18) if pieces else 1.0
    array = jax.random.normal(rng, shape, jnp.float32) * deviation * factor_of
    return jnp.minimum(jnp.maximum(array, -limit), limit).astype(kind)


def setup_inputs(seed: int = 0) -> dict:
    key_list = jax.random.split(jax.random.key(seed), 7)
    pair = normal_values(key_list[0], (N, N, C), 1.0, 6.0, ((0, 16), (1, 8)))
    gain = jnp.clip(1.0 + 0.18 * jax.random.normal(key_list[1], (C,), jnp.float32), 0.1, 1.9)
    projections = normal_values(key_list[2], (5, C, C), C ** -0.5, 0.5)
    bias_weight = draw_bias_weight(jax.random.fold_in(key_list[6], 71), 0)
    valid_len = jax.random.randint(key_list[4], (1,), N // 2, N + 1).astype(jnp.int32)
    out_cotangent = normal_values(key_list[5], (N, N, C), 1.0, 6.0, ((0, 16), (1, 8)))
    return dict(pair=pair, gain=gain, projections=projections, bias_weight=bias_weight, valid_len=valid_len, out_cotangent=out_cotangent)


EPS = 1e-05

def dense(left, right):
    return jnp.einsum('abc,cd->abd', left.astype(jnp.float32), right.astype(jnp.float32))

def outer_sum(left, right):
    return jnp.einsum('abc,abd->cd', left.astype(jnp.float32), right.astype(jnp.float32))

def attend_forward(query, key, value, bias_blocks, keep):
    ncols, rows, heads, width = query.shape
    nblocks = bias_blocks.shape[0]
    scale = width ** (-0.5)

    def per_column(cols):
        qcol, kcol, vcol = cols

        def per_block(blk):
            qblk, bblk = blk
            scores = jnp.einsum('qhd,khd->hqk', qblk.astype(jnp.float32), kcol.astype(jnp.float32)) * scale + bblk.astype(jnp.float32)
            scores = jnp.where(keep[None, None, :], scores, -1000000000.0)
            probs = jax.nn.softmax(scores, axis=-1)
            out = jnp.einsum('hqk,khd->qhd', probs.astype(jnp.bfloat16).astype(jnp.float32), vcol.astype(jnp.float32))
            return out.astype(jnp.bfloat16)
        return lax.map(per_block, (qcol.reshape(nblocks, rows // nblocks, heads, width), bias_blocks)).reshape(rows, heads, width)
    return lax.map(per_column, (query, key, value))

def attend_backward(query, key, value, d_context, bias_blocks, keep):
    ncols, rows, heads, width = query.shape
    nblocks = bias_blocks.shape[0]
    qsize = rows // nblocks
    scale = width ** (-0.5)

    def per_column(total, cols):
        qcol, kcol, vcol, dcol = cols

        def per_block(carry, blk):
            dk_acc, dv_acc = carry
            qblk, dblk, bblk = blk
            scores = jnp.einsum('qhd,khd->hqk', qblk.astype(jnp.float32), kcol.astype(jnp.float32)) * scale + bblk.astype(jnp.float32)
            scores = jnp.where(keep[None, None, :], scores, -1000000000.0)
            probs = jax.nn.softmax(scores, axis=-1)
            weights_b = probs.astype(jnp.bfloat16).astype(jnp.float32)
            d_probs = jnp.einsum('qhd,khd->hqk', dblk.astype(jnp.float32), vcol.astype(jnp.float32))
            d_scores = probs * (d_probs - lax.optimization_barrier(jnp.sum(probs * d_probs, axis=-1, keepdims=True)))
            dsb = d_scores.astype(jnp.bfloat16).astype(jnp.float32)
            dq = (jnp.einsum('hqk,khd->qhd', dsb, kcol.astype(jnp.float32)) * scale).astype(jnp.bfloat16)
            dk_acc = dk_acc + jnp.einsum('hqk,qhd->khd', dsb, qblk.astype(jnp.float32)) * scale
            dv_acc = dv_acc + jnp.einsum('hqk,qhd->khd', weights_b, dblk.astype(jnp.float32))
            return ((dk_acc, dv_acc), (dq, d_scores))
        zeros = jnp.zeros((rows, heads, width), jnp.float32)
        (dk, dv), (dq, dscores) = lax.scan(per_block, (zeros, zeros), (qcol.reshape(nblocks, qsize, heads, width), dcol.reshape(nblocks, qsize, heads, width), bias_blocks))
        return (total + dscores, (dq.reshape(rows, heads, width), dk.astype(jnp.bfloat16), dv.astype(jnp.bfloat16)))
    start = jnp.zeros(bias_blocks.shape, jnp.float32)
    total, (dq, dk, dv) = lax.scan(per_column, start, (query, key, value, d_context))
    return (dq, dk, dv, total)

def reference(pair, gain, projections, bias_weight, valid_len, out_cotangent):
    heads = bias_weight.shape[1]
    width = pair.shape[2] // heads
    rows = pair.shape[0]
    pair_float = pair.astype(jnp.float32)
    average_value = lax.optimization_barrier(jnp.mean(pair_float, axis=-1, keepdims=True))
    var = lax.optimization_barrier(jnp.mean((pair_float - average_value) ** 2, axis=-1, keepdims=True))
    inverse_deviation = lax.rsqrt(var + EPS)
    centered_scaled = (pair_float - average_value) * inverse_deviation
    normalized_pair = (centered_scaled * gain).astype(jnp.bfloat16)
    query = dense(normalized_pair, projections[0]).astype(jnp.bfloat16)
    key = dense(normalized_pair, projections[1]).astype(jnp.bfloat16)
    value = dense(normalized_pair, projections[2]).astype(jnp.bfloat16)
    gate = jax.nn.sigmoid(dense(normalized_pair, projections[3]))
    pair_bias = dense(normalized_pair, bias_weight)
    bias_t = jnp.transpose(pair_bias, (2, 1, 0))
    bias_blocks = bias_t.reshape(heads, rows // QB, QB, rows).transpose(1, 0, 2, 3)
    keep = jnp.arange(rows, dtype=jnp.int32) < valid_len[0]

    def split(tensor):
        return jnp.moveaxis(tensor, 1, 0).reshape(rows, rows, heads, width)

    def join(tensor):
        return jnp.moveaxis(tensor.reshape(rows, rows, heads * width), 0, 1)
    context = join(attend_forward(split(query), split(key), split(value), bias_blocks, keep))
    gated = (gate * context.astype(jnp.float32)).astype(jnp.bfloat16)
    attended = dense(gated, projections[4]).astype(jnp.bfloat16)
    d_gated = dense(out_cotangent, projections[4].T)
    d_context = (d_gated * gate).astype(jnp.bfloat16)
    d_gate_pre = (d_gated * context.astype(jnp.float32) * gate * (1.0 - gate)).astype(jnp.bfloat16)
    dq, dk, dv, total = attend_backward(split(query), split(key), split(value), split(d_context), bias_blocks, keep)
    dq, dk, dv = (join(dq), join(dk), join(dv))
    d_bias_t = total.transpose(1, 0, 2, 3).reshape(heads, rows, rows)
    d_bias = jnp.transpose(d_bias_t, (2, 1, 0)).astype(jnp.bfloat16)
    normalized_gradient = dense(dq, projections[0].T) + dense(dk, projections[1].T) + dense(dv, projections[2].T)
    normalized_gradient = normalized_gradient + dense(d_gate_pre, projections[3].T) + dense(d_bias, bias_weight.T)
    projection_grad = jnp.stack([outer_sum(normalized_pair, dq), outer_sum(normalized_pair, dk), outer_sum(normalized_pair, dv), outer_sum(normalized_pair, d_gate_pre), outer_sum(gated, out_cotangent)])
    bias_weight_grad = outer_sum(normalized_pair, d_bias)
    gain_gradient = lax.optimization_barrier(jnp.sum(normalized_gradient * centered_scaled, axis=(0, 1)))
    scaled_output = normalized_gradient * gain
    pair_gradient = inverse_deviation * (scaled_output - lax.optimization_barrier(jnp.mean(scaled_output, axis=-1, keepdims=True)) - centered_scaled * lax.optimization_barrier(jnp.mean(scaled_output * centered_scaled, axis=-1, keepdims=True)))
    return (attended, pair_gradient, projection_grad, bias_weight_grad, gain_gradient)
```

```python
import functools

import jax
import jax.numpy as jnp
from jax import lax
from jax.experimental import pallas as pl
from jax.experimental.pallas import tpu as pltpu
from jax.sharding import Mesh
from jax.sharding import PartitionSpec as P

ROW = ("row_0", "row_1", "row_2")
COL = ("col_0", "col_1")
ALL = ROW + COL
EPS = 1e-05
MASKED = -1000000000.0
CHUNK = 128
F32 = jnp.float32
BF16 = jnp.bfloat16


def nn(left, right):
    return lax.dot_general(left, right, (((1,), (0,)), ((), ())), preferred_element_type=F32)


def nt(left, right):
    return lax.dot_general(left, right, (((1,), (1,)), ((), ())), preferred_element_type=F32)


def turned(value):
    return jnp.transpose(value.astype(F32)).astype(value.dtype)


def exchange(value, axes):
    return lax.all_to_all(value, axes, split_axis=0, concat_axis=0, tiled=True)


def attention_kernel(
    heads, valid_ref, normed_ref, cot_ref, bias_ref, w_ref, wt_ref,
    out_ref, dbias_ref, grads_ref, total, ctx_t, dq_t, dk_acc, dv_acc,
):
    column = pl.program_id(0)
    columns = pl.num_programs(0)
    rows, channels = normed_ref.shape
    width = channels // heads
    scale = width ** (-0.5)
    normed = normed_ref[...]
    cot = cot_ref[...]

    @pl.when(column == 0)
    def _():
        total[...] = jnp.zeros_like(total)
        grads_ref[...] = jnp.zeros_like(grads_ref)

    query = nn(normed, w_ref[0]).astype(BF16)
    key = nn(normed, w_ref[1]).astype(BF16)
    value = nn(normed, w_ref[2]).astype(BF16)
    query_t = nt(wt_ref[0], normed).astype(BF16)
    key_t = nt(wt_ref[1], normed).astype(BF16)
    value_t = nt(wt_ref[2], normed).astype(BF16)
    gate_t = jax.nn.sigmoid(nt(wt_ref[3], normed))
    d_gated_t = nt(w_ref[4], cot)
    d_context_t = (d_gated_t * gate_t).astype(BF16)
    d_context = turned(d_context_t)
    keep = lax.broadcasted_iota(jnp.int32, (rows, CHUNK), 0) < valid_ref[0]
    lane = lax.broadcasted_iota(jnp.int32, (rows, channels), 1)
    dk_acc[...] = jnp.zeros_like(dk_acc)
    dv_acc[...] = jnp.zeros_like(dv_acc)
    for head in range(heads):
        mine = (lane >= head * width) & (lane < (head + 1) * width)
        zero = jnp.zeros((rows, channels), BF16)
        key_h = jnp.where(mine, key, zero)
        value_h = jnp.where(mine, value, zero)
        query_h = jnp.where(mine, query, zero)
        d_context_h = jnp.where(mine, d_context, zero)
        part = slice(head * width, (head + 1) * width)
        for at in range(0, rows, CHUNK):
            here = slice(at, at + CHUNK)
            scores = nn(key_h, query_t[:, here]) * scale + bias_ref[head, :, here]
            scores = jnp.where(keep, scores, MASKED)
            top = jnp.max(scores, axis=0, keepdims=True)
            grown = jnp.exp(scores - top)
            probs = grown * (1.0 / jnp.sum(grown, axis=0, keepdims=True))
            weights_b = probs.astype(BF16)
            ctx_t[part, here] = nn(value_t[part, :], weights_b).astype(BF16)
            d_probs = nn(value_h, d_context_t[:, here])
            delta = jnp.sum(probs * d_probs, axis=0, keepdims=True)
            d_scores = probs * (d_probs - delta)
            total[head, :, here] += d_scores
            d_scores_b = d_scores.astype(BF16)
            dq_t[part, here] = (nn(key_t[part, :], d_scores_b) * scale).astype(BF16)
            dk_acc[...] += nn(d_scores_b, query_h[here, :])
            dv_acc[...] += nn(weights_b, d_context_h[here, :])
    context_t = ctx_t[...].astype(F32)
    gated_t = (gate_t * context_t).astype(BF16)
    d_gate_t = (d_gated_t * context_t * gate_t * (1.0 - gate_t)).astype(BF16)
    gated = turned(gated_t)
    d_gate = turned(d_gate_t)
    d_query = turned(dq_t[...])
    d_key = (dk_acc[...] * scale).astype(BF16)
    d_value = dv_acc[...].astype(BF16)
    attended = nn(gated, w_ref[4]).astype(BF16)
    d_normed = nt(d_query, w_ref[0]) + nt(d_key, w_ref[1]) + nt(d_value, w_ref[2])
    d_normed = d_normed + nt(d_gate, w_ref[3])
    out_ref[:, pl.ds(pl.multiple_of(column * channels, channels), channels)] = attended
    second = pl.multiple_of((columns + column) * channels, channels)
    out_ref[:, pl.ds(second, channels)] = d_normed.astype(BF16)
    normed_t = turned(normed)
    grads_ref[0] += nn(normed_t, d_query)
    grads_ref[1] += nn(normed_t, d_key)
    grads_ref[2] += nn(normed_t, d_value)
    grads_ref[3] += nn(normed_t, d_gate)
    grads_ref[4] += nn(gated_t, cot)

    @pl.when(column == columns - 1)
    def _():
        dbias_ref[...] = total[...].astype(BF16)


def attend(valid_len, both, bias, projections, projections_t, columns):
    rows = both.shape[0]
    heads = bias.shape[0]
    channels = projections.shape[-1]
    whole3 = lambda j: (0, 0, 0)
    return pl.pallas_call(
        functools.partial(attention_kernel, heads),
        grid=(columns,),
        in_specs=[
            pl.BlockSpec(memory_space=pltpu.SMEM),
            pl.BlockSpec((rows, channels), lambda j: (0, j)),
            pl.BlockSpec((rows, channels), lambda j: (0, columns + j)),
            pl.BlockSpec(bias.shape, whole3),
            pl.BlockSpec(projections.shape, whole3),
            pl.BlockSpec(projections.shape, whole3),
        ],
        out_specs=[
            pl.BlockSpec((rows, 2 * columns * channels), lambda j: (0, 0)),
            pl.BlockSpec(bias.shape, whole3),
            pl.BlockSpec(projections.shape, whole3),
        ],
        out_shape=[
            jax.ShapeDtypeStruct((rows, 2 * columns * channels), BF16),
            jax.ShapeDtypeStruct(bias.shape, BF16),
            jax.ShapeDtypeStruct(projections.shape, F32),
        ],
        scratch_shapes=[
            pltpu.VMEM(bias.shape, F32),
            pltpu.VMEM((channels, rows), BF16),
            pltpu.VMEM((channels, rows), BF16),
            pltpu.VMEM((rows, channels), F32),
            pltpu.VMEM((rows, channels), F32),
        ],
        compiler_params=pltpu.CompilerParams(vmem_limit_bytes=56 << 20),
        name="attention",
    )(valid_len, both, both, bias, projections, projections_t)


def shards(pair, gain, projections, bias_weight, valid_len, out_cotangent):
    n_row = lax.axis_size(ROW)
    n_col = lax.axis_size(COL)
    n_all = n_row * n_col
    tile_rows, tile_cols, channels = pair.shape
    rows = tile_rows * n_row
    heads = bias_weight.shape[1]
    ncols = tile_cols // n_row
    pair_float = pair.astype(F32)
    average_value = jnp.mean(pair_float, axis=-1, keepdims=True)
    var = jnp.mean((pair_float - average_value) ** 2, axis=-1, keepdims=True)
    inverse_deviation = lax.rsqrt(var + EPS)
    centered_scaled = (pair_float - average_value) * inverse_deviation
    normalized_pair = (centered_scaled * gain).astype(BF16)
    bias_tile = jnp.einsum("abc,ch->hab", normalized_pair, bias_weight, preferred_element_type=F32)
    bias_tile = bias_tile.reshape(1, 1, heads * tile_rows * tile_cols)
    spread = jnp.broadcast_to(bias_tile, (n_all, 1, bias_tile.shape[-1]))
    grid = exchange(spread, ALL).reshape(n_row, n_col, heads, tile_rows, tile_cols)
    bias = jnp.transpose(grid, (2, 0, 3, 1, 4)).reshape(heads, rows, rows)

    def by_owner(tile):
        return jnp.moveaxis(tile.reshape(tile_rows, n_row, ncols * channels), 1, 0)

    both = jnp.concatenate([by_owner(normalized_pair), by_owner(out_cotangent)], axis=2)
    both = exchange(both, ROW).reshape(rows, 2 * ncols * channels)
    out, d_bias_part, grads = attend(
        valid_len, both, bias, projections, jnp.swapaxes(projections, 1, 2), ncols
    )
    part = d_bias_part.reshape(heads, n_row, tile_rows, n_col, tile_cols)
    part = jnp.transpose(part, (1, 3, 0, 2, 4)).reshape(n_all, heads * tile_rows * tile_cols)
    grads = grads.reshape(n_all, -1)
    share = grads.shape[1]
    coarse = grads.astype(BF16)
    fine = (grads - coarse.astype(F32)).astype(BF16)
    sent = jnp.concatenate([part, coarse, fine], axis=1)[:, None, :]
    summed = jnp.sum(exchange(sent, ALL).astype(F32), axis=(0, 1))
    at = heads * tile_rows * tile_cols
    d_bias = summed[:at].reshape(heads, tile_rows, tile_cols).astype(BF16)
    grad_share = summed[at : at + share] + summed[at + share :]

    back = exchange(out.reshape(n_row, tile_rows, 2 * ncols * channels), ROW)
    back = jnp.moveaxis(back.reshape(n_row, tile_rows, 2, ncols, channels), 0, 2)
    back = jnp.moveaxis(back, 1, 0).reshape(2, tile_rows, tile_cols, channels)
    attended = back[0]
    bias_term = jnp.einsum("hab,ch->abc", d_bias, bias_weight, preferred_element_type=F32)
    bias_weight_part = jnp.einsum("abc,hab->ch", normalized_pair, d_bias, preferred_element_type=F32)
    normalized_gradient = back[1].astype(F32) + bias_term
    gain_part = jnp.sum(normalized_gradient * centered_scaled, axis=(0, 1))
    last = jnp.concatenate([grad_share, bias_weight_part.reshape(-1), gain_part])
    everyone = exchange(jnp.broadcast_to(last[None, None], (n_all, 1, last.shape[0])), ALL)[:, 0]
    projection_grad = everyone[:, :share].reshape(projections.shape)
    small = jnp.sum(everyone[:, share:], axis=0)
    bias_weight_grad = small[: channels * heads].reshape(channels, heads)
    gain_gradient = small[channels * heads :]
    scaled_output = normalized_gradient * gain
    pair_gradient = inverse_deviation * (
        scaled_output
        - jnp.mean(scaled_output, axis=-1, keepdims=True)
        - centered_scaled * jnp.mean(scaled_output * centered_scaled, axis=-1, keepdims=True)
    )
    return (attended, pair_gradient, projection_grad, bias_weight_grad, gain_gradient)


def solution(mesh):
    torus = Mesh(mesh.devices.reshape(2, 4, 2, 2, 4), ALL)
    in_specs = (P(ROW, COL, None), P(), P(), P(), P(), P(ROW, COL, None))
    out_specs = (P(ROW, COL, None), P(ROW, COL, None), P(), P(), P())
    return jax.shard_map(
        shards, mesh=torus, in_specs=in_specs, out_specs=out_specs, check_vma=False
    )
```

```python
import functools

import jax
import jax.numpy as jnp
from jax import lax
from jax.experimental import pallas as pl
from jax.experimental.pallas import tpu as pltpu
from jax.sharding import Mesh
from jax.sharding import PartitionSpec as P

ROW = ("row_0", "row_1", "row_2")
COL = ("col_0", "col_1")
ALL = ROW + COL
CORE = "row_2"
EPS = 1e-05
MASKED = -1000000000.0
PARTS = 4
F32 = jnp.float32
BF16 = jnp.bfloat16


def nn(left, right):
    return lax.dot_general(left, right, (((1,), (0,)), ((), ())), preferred_element_type=F32)


def nt(left, right):
    return lax.dot_general(left, right, (((1,), (1,)), ((), ())), preferred_element_type=F32)


def turned(value):
    return jnp.transpose(value.astype(F32)).astype(value.dtype)


def exchange(value, axes):
    return lax.all_to_all(value, axes, split_axis=0, concat_axis=0, tiled=True)


def call(kernel, out_shape, scratch, name, *operands):
    return pl.pallas_call(
        kernel,
        out_shape=out_shape,
        scratch_shapes=scratch,
        compiler_params=pltpu.CompilerParams(vmem_limit_bytes=56 << 20),
        name=name,
    )(*operands)


def coarse_fine(value):
    coarse = value.astype(BF16)
    return coarse, (value - coarse.astype(F32)).astype(BF16)


def normalize(pair_ref, gain_ref):
    rows, cols, channels = pair_ref.shape
    pair = pair_ref[...].astype(F32).reshape(rows * cols, channels)
    average = jnp.mean(pair, axis=-1, keepdims=True)
    var = jnp.mean((pair - average) ** 2, axis=-1, keepdims=True)
    inverse = lax.rsqrt(var + EPS)
    xhat = (pair - average) * inverse
    return xhat, inverse, (xhat * gain_ref[...]).astype(BF16)


def pack_kernel(pair_ref, cot_ref, gain_ref, bias_weight_ref, out_ref, normed_s, cot_s, bias_s):
    rows, cols, channels = pair_ref.shape
    owners = out_ref.shape[0]
    ncols = cols // owners
    heads = bias_weight_ref.shape[0]
    normed = normalize(pair_ref, gain_ref)[2]
    normed_s[...] = normed.astype(F32)
    cot_s[...] = cot_ref[...].astype(F32).reshape(rows * cols, channels)
    for a in range(rows):
        bias = nt(bias_weight_ref[...], normed[a * cols : (a + 1) * cols])
        bias_s[pl.ds(a, heads, stride=rows), :] = bias
    pad = jnp.zeros((rows, 256 - 4 * cols), BF16)
    for core in range(2):
        first = 2 * core * rows
        bias = jnp.concatenate([bias_s[first : first + rows], bias_s[first + rows : first + 2 * rows]], axis=1)
        bias = jnp.concatenate([*coarse_fine(bias), pad], axis=1)
        for owner in range(core, owners, 2):
            out_ref[owner, :, 2 * ncols * channels :] = bias
    for owner in range(owners):
        for k in range(ncols):
            column = pl.ds(owner * ncols + k, rows, stride=cols)
            at = k * channels
            out_ref[owner, :, at : at + channels] = normed_s[column, :].astype(BF16)
            at = (ncols + k) * channels
            out_ref[owner, :, at : at + channels] = cot_s[column, :].astype(BF16)


def bias_out_kernel(parts_ref, out_ref):
    rows = parts_ref.shape[0]
    width = out_ref.shape[2] // PARTS
    bias = parts_ref[:, :width].astype(F32) + parts_ref[:, width : 2 * width].astype(F32)
    high = rows // PARTS
    packed = jnp.concatenate([bias[k * high : (k + 1) * high] for k in range(PARTS)], axis=1)
    for c in range(out_ref.shape[0]):
        out_ref[c] = packed


def project_kernel(
    normed_ref, twin_normed_ref, cot_ref, twin_cot_ref, w_ref, wt_ref, w_out_ref,
    query_ref, key_ref, value_ref, d_context_ref,
    query_t_ref, key_t_ref, value_t_ref, d_context_t_ref, gate_t_ref, d_gated_t_ref,
):
    normed = jnp.concatenate([normed_ref[...], twin_normed_ref[...]], axis=1)
    cot = jnp.concatenate([cot_ref[...], twin_cot_ref[...]], axis=1)
    for m, ref, ref_t in ((0, query_ref, query_t_ref), (1, key_ref, key_t_ref), (2, value_ref, value_t_ref)):
        ref[0] = nn(normed, w_ref[m]).astype(BF16)
        ref_t[0] = nt(wt_ref[m], normed).astype(BF16)
    gate_t = jax.nn.sigmoid(nt(wt_ref[3], normed))
    d_gated_t = nt(w_out_ref[...], cot)
    d_context_t = (d_gated_t * gate_t).astype(BF16)
    gate_t_ref[0] = gate_t
    d_gated_t_ref[0] = d_gated_t
    d_context_t_ref[0] = d_context_t
    d_context_ref[0] = turned(d_context_t)


def project(both, twin, w, wt, w_out, columns):
    rows = both.shape[0]
    channels = w.shape[-1]
    normed = pl.BlockSpec((rows, channels), lambda j: (0, j))
    cot = pl.BlockSpec((rows, channels), lambda j: (0, columns + j))
    flat = pl.BlockSpec((1, rows, channels), lambda j: (j, 0, 0))
    flat_t = pl.BlockSpec((1, channels, rows), lambda j: (j, 0, 0))
    upright = jax.ShapeDtypeStruct((columns, rows, channels), BF16)
    lying = jax.ShapeDtypeStruct((columns, channels, rows), BF16)
    wide = jax.ShapeDtypeStruct((columns, channels, rows), F32)
    return pl.pallas_call(
        project_kernel,
        grid=(columns,),
        in_specs=[
            normed, normed, cot, cot,
            pl.BlockSpec(w.shape, lambda j: (0, 0, 0)),
            pl.BlockSpec(wt.shape, lambda j: (0, 0, 0)),
            pl.BlockSpec(w_out.shape, lambda j: (0, 0)),
        ],
        out_specs=[flat] * 4 + [flat_t] * 6,
        out_shape=[upright] * 4 + [lying] * 4 + [wide] * 2,
        compiler_params=pltpu.CompilerParams(vmem_limit_bytes=56 << 20),
        name="project",
    )(both, twin, both, twin, w, wt, w_out)


def attention_kernel(
    valid_ref, got_ref, normed_ref, twin_normed_ref, cot_ref, twin_cot_ref,
    query_ref, key_ref, value_ref, d_context_ref,
    query_t_ref, key_t_ref, value_t_ref, d_context_t_ref, gate_t_ref, d_gated_t_ref,
    acts_ref, sent_ref, bias_s, total, grads_s, ctx_t, dq_t, d_scores_s, weights_s, query_s, d_context_s,
):
    step = pl.program_id(0)
    steps = pl.num_programs(0)
    blocks, high, lanes = got_ref.shape
    rows, channels = normed_ref.shape
    slots = 4
    width = channels // slots
    half = channels // 2
    cols = rows // blocks
    scale = width ** (-0.5)

    @pl.when(step == 0)
    def _():
        for k in range(PARTS):
            for h in range(2):
                at = (2 * k + h) * cols
                pieces = [got_ref[c, :, at : at + cols] for c in range(blocks)]
                bias_s[h, k * high : (k + 1) * high, :] = jnp.concatenate(pieces, axis=1)
        total[...] = jnp.zeros_like(total)
        grads_s[...] = jnp.zeros_like(grads_s)

    query = query_ref[0]
    key = key_ref[0]
    value = value_ref[0]
    d_context = d_context_ref[0]
    lane = lax.broadcasted_iota(jnp.int32, (rows, channels), 1)
    keep = lax.broadcasted_iota(jnp.int32, (rows, rows), 0) < valid_ref[0]
    zero = jnp.zeros((rows, channels), BF16)
    for slot in range(slots):
        mine = (lane >= slot * width) & (lane < (slot + 1) * width)
        key_h = jnp.where(mine, key, zero)
        value_h = jnp.where(mine, value, zero)
        here = slice(slot * rows, (slot + 1) * rows)
        part = slice(slot * width, (slot + 1) * width)
        query_s[here, :] = jnp.where(mine, query, zero)
        d_context_s[here, :] = jnp.where(mine, d_context, zero)
        scores = nn(key_h, query_t_ref[0]) * scale + bias_s[slot % 2]
        scores = jnp.where(keep, scores, MASKED)
        top = jnp.max(scores, axis=0, keepdims=True)
        grown = jnp.exp(scores - top)
        probs = grown * (1.0 / jnp.sum(grown, axis=0, keepdims=True))
        weights_b = probs.astype(BF16)
        weights_s[:, here] = weights_b
        ctx_t[part, :] = nn(value_t_ref[0, part, :], weights_b).astype(BF16)
        d_probs = nn(value_h, d_context_t_ref[0])
        delta = jnp.sum(probs * d_probs, axis=0, keepdims=True)
        d_scores = probs * (d_probs - delta)
        total[slot % 2] += d_scores
        d_scores_b = d_scores.astype(BF16)
        d_scores_s[:, here] = d_scores_b
        dq_t[part, :] = (nn(key_t_ref[0, part, :], d_scores_b) * scale).astype(BF16)
    d_key = (nn(d_scores_s[...], query_s[...]) * scale).astype(BF16)
    d_value = nn(weights_s[...], d_context_s[...]).astype(BF16)
    gate_t = gate_t_ref[0]
    context_t = ctx_t[...].astype(F32)
    gated_t = (gate_t * context_t).astype(BF16)
    d_gate_t = (d_gated_t_ref[0] * context_t * gate_t * (1.0 - gate_t)).astype(BF16)
    acts = [turned(gated_t), turned(dq_t[...]), d_key, d_value, turned(d_gate_t)]
    for m in range(5):
        acts_ref[0, :, m * channels : (m + 1) * channels] = acts[m]
    right = jnp.concatenate(acts[1:], axis=1)
    own = nn(turned(normed_ref[...]), right)
    other = nn(turned(twin_normed_ref[...]), right)
    for m in range(4):
        at = slice(m * channels, (m + 1) * channels)
        grads_s[:channels, at] += jnp.where(lane[:channels] < half, own[:, at], other[:, at])
    last = nn(gated_t[:half], cot_ref[...]) + nn(gated_t[half:], twin_cot_ref[...])
    grads_s[channels:, :channels] += last

    @pl.when(step == steps - 1)
    def _():
        for c in range(blocks):
            pieces = [
                total[h, k * high : (k + 1) * high, c * cols : (c + 1) * cols]
                for k in range(PARTS)
                for h in range(2)
            ]
            sent_ref[c, :high, :] = jnp.concatenate(pieces, axis=1).astype(BF16)
        sums = []
        for m in range(4):
            at = slice(m * channels, (m + 1) * channels)
            both = grads_s[:channels, at]
            sums.append(both + pltpu.roll(both, half, 1))
        left = lane[:channels] < half
        grads = [
            jnp.where(left, sums[0], sums[1]),
            jnp.where(left, sums[2], sums[3]),
            grads_s[channels:, :channels],
        ]
        grads = jnp.concatenate(grads, axis=0)
        share = grads.shape[0] // blocks
        rest = sent_ref.shape[1] - high
        spare = jnp.zeros((3 * rest - share, channels), F32)
        for c in range(blocks):
            mine = jnp.concatenate([grads[c * share : (c + 1) * share], spare], axis=0)
            pieces = [mine[k * rest : (k + 1) * rest] for k in range(3)]
            sent_ref[c, high:, :] = jnp.concatenate(pieces, axis=1).astype(BF16)


def attend(valid_len, got, both, twin, inner, columns):
    rows = both.shape[0]
    channels = inner[0].shape[-1]
    blocks, high, lanes = got.shape
    normed = pl.BlockSpec((rows, channels), lambda j: (0, j))
    cot = pl.BlockSpec((rows, channels), lambda j: (0, columns + j))
    flat = pl.BlockSpec((1, rows, channels), lambda j: (j, 0, 0))
    flat_t = pl.BlockSpec((1, channels, rows), lambda j: (j, 0, 0))
    return pl.pallas_call(
        attention_kernel,
        grid=(columns,),
        in_specs=[
            pl.BlockSpec(memory_space=pltpu.SMEM),
            pl.BlockSpec(got.shape, lambda j: (0, 0, 0)),
            normed, normed, cot, cot,
        ]
        + [flat] * 4
        + [flat_t] * 6,
        out_specs=[
            pl.BlockSpec((1, rows, 5 * channels), lambda j: (j, 0, 0)),
            pl.BlockSpec((blocks, high + 16, lanes), lambda j: (0, 0, 0)),
        ],
        out_shape=[
            jax.ShapeDtypeStruct((columns, rows, 5 * channels), BF16),
            jax.ShapeDtypeStruct((blocks, high + 16, lanes), BF16),
        ],
        scratch_shapes=[
            pltpu.VMEM((2, rows, rows), F32),
            pltpu.VMEM((2, rows, rows), F32),
            pltpu.VMEM((channels + channels // 2, 4 * channels), F32),
            pltpu.VMEM((channels, rows), BF16),
            pltpu.VMEM((channels, rows), BF16),
            pltpu.VMEM((rows, 4 * rows), BF16),
            pltpu.VMEM((rows, 4 * rows), BF16),
            pltpu.VMEM((4 * rows, channels), BF16),
            pltpu.VMEM((4 * rows, channels), BF16),
        ],
        compiler_params=pltpu.CompilerParams(vmem_limit_bytes=56 << 20),
        name="attention",
    )(valid_len, got, both, twin, both, twin, *inner)


def merge_kernel(acts_ref, came_ref, w_ref, out_ref):
    column = pl.program_id(0)
    columns = pl.num_programs(0)
    channels = w_ref.shape[-1]
    parts = []
    for m in range(5):
        at = slice(m * channels, (m + 1) * channels)
        parts.append(nn(jnp.concatenate([acts_ref[0, :, at], came_ref[0, :, at]], axis=1), w_ref[m]))
    d_normed = parts[1] + parts[2] + parts[3] + parts[4]
    out_ref[:, pl.ds(pl.multiple_of(column * channels, channels), channels)] = parts[0].astype(BF16)
    second = pl.multiple_of((columns + column) * channels, channels)
    out_ref[:, pl.ds(second, channels)] = d_normed.astype(BF16)


def merge(acts, came, w):
    columns, rows, lanes = acts.shape
    channels = w.shape[-1]
    block = pl.BlockSpec((1, rows, lanes), lambda j: (j, 0, 0))
    return pl.pallas_call(
        merge_kernel,
        grid=(columns,),
        in_specs=[block, block, pl.BlockSpec(w.shape, lambda j: (0, 0, 0))],
        out_specs=pl.BlockSpec((rows, 2 * columns * channels), lambda j: (0, 0)),
        out_shape=jax.ShapeDtypeStruct((rows, 2 * columns * channels), BF16),
        compiler_params=pltpu.CompilerParams(vmem_limit_bytes=56 << 20),
        name="merge",
    )(acts, came, w)


def sum_kernel(got_ref, main_ref, out_ref):
    blocks, high, lanes = got_ref.shape
    owners, rows, wide = out_ref.shape
    main = main_ref.shape[1]
    part = lanes // PARTS
    rest = high - part
    total = got_ref[0].astype(F32)
    for c in range(1, blocks):
        total = total + got_ref[c].astype(F32)
    grads = jnp.concatenate([total[part:, k * 128 : (k + 1) * 128] for k in range(lanes // 128)], axis=0)
    share = 5
    pad = jnp.zeros((rows, 256 - 2 * part), BF16)
    gap = jnp.zeros((8 - share, 128), F32)
    for owner in range(owners):
        across, down = divmod(owner, part // rows)
        block = total[down * rows : (down + 1) * rows, across * part : (across + 1) * part]
        out_ref[owner, :, :main] = main_ref[owner * rows : (owner + 1) * rows, :]
        out_ref[owner, :, main : main + 256] = jnp.concatenate([*coarse_fine(block), pad], axis=1)
        mine = grads[owner // 2 * share : (owner // 2 + 1) * share]
        coarse = mine.astype(BF16).astype(F32)
        stack = jnp.concatenate([coarse, gap, mine - coarse, gap, jnp.zeros((8, 128), F32)], axis=0)
        out_ref[owner, :, main + 256 :] = stack.astype(BF16)


def finish_kernel(
    core_ref, got_ref, pair_ref, gain_ref, bias_weight_ref, repeated_ref,
    attended_ref, gradient_ref, last_ref, moved_s, d_normed_s, d_bias_s,
):
    owners, rows, wide = got_ref.shape
    cols, channels = pair_ref.shape[1:]
    heads = bias_weight_ref.shape[0]
    ncols = cols // owners
    main = 2 * ncols * channels
    xhat, inverse, normed = normalize(pair_ref, gain_ref)
    for owner in range(owners):
        for k in range(ncols):
            column = pl.ds(owner * ncols + k, rows, stride=cols)
            at = k * channels
            moved_s[column, :] = got_ref[owner, :, at : at + channels].astype(F32)
            at = (ncols + k) * channels
            d_normed_s[column, :] = got_ref[owner, :, at : at + channels].astype(F32)
    attended_ref[...] = moved_s[...].astype(BF16).reshape(attended_ref.shape)
    grads = [jnp.zeros((rows, 128), F32), jnp.zeros((rows, 128), F32)]
    for owner in range(owners):
        grads[owner % 2] = grads[owner % 2] + got_ref[owner, :, main + 256 :].astype(F32)
    grads = jnp.where(core_ref[0] == 0, grads[0], grads[1])
    for core in range(2):
        block = jnp.zeros((rows, 2 * cols), F32)
        for owner in range(core, owners, 2):
            block = block + got_ref[owner, :, main : main + 2 * cols].astype(F32)
            block = block + got_ref[owner, :, main + 2 * cols : main + 4 * cols].astype(F32)
        block = block.astype(BF16).astype(F32)
        for h in range(2):
            at = pl.ds(2 * core + h, rows, stride=heads)
            d_bias_s[at, :] = block[:, h * cols : (h + 1) * cols]
    d_bias_t = jnp.transpose(d_bias_s[...]).astype(BF16)
    row = lax.broadcasted_iota(jnp.int32, (rows * heads, channels), 0)
    weight_part = jnp.zeros((heads, channels), F32)
    for a in range(rows):
        here = slice(a * cols, (a + 1) * cols)
        mine = (row >= a * heads) & (row < (a + 1) * heads)
        weight = jnp.where(mine, repeated_ref[...], jnp.zeros((rows * heads, channels), BF16))
        d_normed_s[here, :] += nn(d_bias_t, weight)
        d_bias_a = d_bias_s[a * heads : (a + 1) * heads, :].astype(BF16)
        weight_part = weight_part + nn(d_bias_a, normed[here])
    d_normed = d_normed_s[...]
    gain_part = jnp.sum(d_normed * xhat, axis=0, keepdims=True)
    last = jnp.concatenate([grads[:5] + grads[8:13], weight_part, gain_part], axis=0)
    last_ref[...] = jnp.broadcast_to(last[None], last_ref.shape)
    scaled = d_normed * gain_ref[...]
    gradient = inverse * (
        scaled
        - jnp.mean(scaled, axis=-1, keepdims=True)
        - xhat * jnp.mean(scaled * xhat, axis=-1, keepdims=True)
    )
    gradient_ref[...] = gradient.reshape(gradient_ref.shape)


def shards(pair, gain, projections, bias_weight, valid_len, out_cotangent):
    n_row = lax.axis_size(ROW)
    n_col = lax.axis_size(COL)
    n_all = n_row * n_col
    tile_rows, tile_cols, channels = pair.shape
    rows = tile_rows * n_row
    heads = bias_weight.shape[1]
    ncols = tile_cols // n_row
    tile = tile_rows * tile_cols
    main = 2 * ncols * channels
    half = channels // 2
    shape = jax.ShapeDtypeStruct
    gain_row = gain[None, :]
    weight_t = bias_weight.T
    swap = [(0, 1), (1, 0)]
    core = lax.axis_index(CORE).astype(jnp.int32)
    repeated = jnp.tile(weight_t, (tile_rows, 1))
    halves = projections[:4].reshape(4, channels, 2, half)
    rows_out = projections[4].reshape(2, half, channels)
    own = lax.dynamic_index_in_dim(halves, core, 2, keepdims=False)
    other = lax.dynamic_index_in_dim(halves, 1 - core, 2, keepdims=False)
    own_out = lax.dynamic_index_in_dim(rows_out, core, 0, keepdims=False)
    other_out = lax.dynamic_index_in_dim(rows_out, 1 - core, 0, keepdims=False)
    zero = jnp.zeros_like(own)
    w = jnp.concatenate(
        [jnp.concatenate([own, zero], axis=2), jnp.concatenate([zero, own], axis=2)], axis=1
    )
    zero_out = jnp.zeros_like(own_out)
    w_out = jnp.concatenate(
        [jnp.concatenate([own_out, zero_out], axis=1), jnp.concatenate([zero_out, own_out], axis=1)],
        axis=0,
    )
    mine = jnp.concatenate([own_out[None], jnp.swapaxes(own, 1, 2)], axis=0)
    theirs = jnp.concatenate([other_out[None], jnp.swapaxes(other, 1, 2)], axis=0)
    gap = jnp.zeros((5, channels, channels), BF16)
    w_merge = jnp.concatenate([mine, gap, theirs], axis=1)

    packed = call(
        pack_kernel, shape((n_row, tile_rows, main + 256), BF16),
        [pltpu.VMEM((tile, channels), F32), pltpu.VMEM((tile, channels), F32),
         pltpu.VMEM((heads * tile_rows, tile_cols), F32)],
        "pack", pair, out_cotangent, gain_row, weight_t,
    )
    both = exchange(packed, ROW).reshape(rows, main + 256)
    high = rows // PARTS
    lanes = PARTS * 2 * tile_cols
    spread = pl.pallas_call(
        bias_out_kernel,
        grid=(1,),
        in_specs=[pl.BlockSpec((rows, 256), lambda i: (0, main // 256))],
        out_specs=pl.BlockSpec((n_col, high, lanes), lambda i: (0, 0, 0)),
        out_shape=shape((n_col, high, lanes), F32),
        name="bias_out",
    )(both)
    got = exchange(spread, COL)
    twin = lax.ppermute(both, CORE, swap)
    inner = project(both, twin, w, jnp.swapaxes(w, 1, 2), w_out, ncols)
    acts, sent = attend(valid_len, got, both, twin, inner, ncols)
    summed = exchange(sent, COL)
    out = merge(acts, lax.ppermute(acts, CORE, swap), w_merge)
    back = call(
        sum_kernel, shape((n_row, tile_rows, main + 384), BF16), [], "sum", summed, out
    )
    attended, pair_gradient, last = pl.pallas_call(
        finish_kernel,
        in_specs=[pl.BlockSpec(memory_space=pltpu.SMEM)] + [pl.BlockSpec(memory_space=pltpu.VMEM)] * 5,
        out_shape=[shape(pair.shape, BF16), shape(pair.shape, F32), shape((n_all, 10, channels), F32)],
        scratch_shapes=[
            pltpu.VMEM((tile, channels), F32), pltpu.VMEM((tile, channels), F32),
            pltpu.VMEM((heads * tile_rows, tile_cols), F32),
        ],
        compiler_params=pltpu.CompilerParams(vmem_limit_bytes=56 << 20),
        name="finish",
    )(core[None], exchange(back, ROW), pair, gain_row, weight_t, repeated)
    everyone = exchange(last, ALL)
    shares = everyone[:, :5].reshape(n_row // 2, 2, n_col, 5, channels)
    shares = jnp.transpose(shares, (1, 2, 0, 3, 4)).reshape(2, 5 * half, channels)
    inward = shares[:, : 2 * channels].reshape(2, 2, channels, 2, half)
    inward = jnp.transpose(inward, (1, 3, 2, 0, 4)).reshape(4, channels, channels)
    outward = shares[:, 2 * channels :].reshape(1, channels, channels)
    projection_grad = jnp.concatenate([inward, outward], axis=0)
    small = jnp.sum(everyone[:, 5:], axis=0)
    return (attended, pair_gradient, projection_grad, small[:4].T, small[4])


def solution(mesh):
    torus = Mesh(mesh.devices.reshape(2, 4, 2, 2, 4), ALL)
    in_specs = (P(ROW, COL, None), P(), P(), P(), P(), P(ROW, COL, None))
    out_specs = (P(ROW, COL, None), P(ROW, COL, None), P(), P(), P())
    return jax.shard_map(
        shards, mesh=torus, in_specs=in_specs, out_specs=out_specs, check_vma=False
    )
```

```python
import functools

import jax
import jax.numpy as jnp
from jax import lax
from jax.experimental import pallas as pl
from jax.experimental.pallas import tpu as pltpu
from jax.sharding import Mesh
from jax.sharding import PartitionSpec as P

ROW = ("row_0", "row_1", "row_2")
COL = ("col_0", "col_1")
ALL = ROW + COL
CORE = "row_2"
EPS = 1e-05
MASKED = -1000000000.0
LOG2E = 1.4426950408889634
PARTS = 4
F32 = jnp.float32
BF16 = jnp.bfloat16


def nn(left, right):
    return lax.dot_general(left, right, (((1,), (0,)), ((), ())), preferred_element_type=F32)


def nt(left, right):
    return lax.dot_general(left, right, (((1,), (1,)), ((), ())), preferred_element_type=F32)


def turned(value):
    return jnp.transpose(value.astype(F32)).astype(value.dtype)


def exchange(value, axes):
    return lax.all_to_all(value, axes, split_axis=0, concat_axis=0, tiled=True)


def call(kernel, out_shape, scratch, name, *operands):
    return pl.pallas_call(
        kernel,
        out_shape=out_shape,
        scratch_shapes=scratch,
        compiler_params=pltpu.CompilerParams(vmem_limit_bytes=56 << 20),
        name=name,
    )(*operands)


def coarse_fine(value):
    coarse = value.astype(BF16)
    return coarse, (value - coarse.astype(F32)).astype(BF16)


def normalize(pair_ref, gain_ref):
    rows, cols, channels = pair_ref.shape
    pair = pair_ref[...].astype(F32).reshape(rows * cols, channels)
    average = jnp.mean(pair, axis=-1, keepdims=True)
    var = jnp.mean((pair - average) ** 2, axis=-1, keepdims=True)
    inverse = lax.rsqrt(var + EPS)
    xhat = (pair - average) * inverse
    return xhat, inverse, (xhat * gain_ref[...]).astype(BF16)


def pack_kernel(pair_ref, cot_ref, gain_ref, bias_weight_ref, out_ref, normed_s, cot_s, bias_s):
    rows, cols, channels = pair_ref.shape
    owners = out_ref.shape[0]
    ncols = cols // owners
    heads = bias_weight_ref.shape[0]
    normed = normalize(pair_ref, gain_ref)[2]
    normed_s[...] = normed.astype(F32)
    cot_s[...] = cot_ref[...].astype(F32).reshape(rows * cols, channels)
    for a in range(rows):
        bias = nt(bias_weight_ref[...], normed[a * cols : (a + 1) * cols])
        bias_s[pl.ds(a, heads, stride=rows), :] = bias
    pad = jnp.zeros((rows, 256 - 4 * cols), BF16)
    for core in range(2):
        first = 2 * core * rows
        bias = jnp.concatenate([bias_s[first : first + rows], bias_s[first + rows : first + 2 * rows]], axis=1)
        bias = jnp.concatenate([*coarse_fine(bias), pad], axis=1)
        for owner in range(core, owners, 2):
            out_ref[owner, :, 2 * ncols * channels :] = bias
    for owner in range(owners):
        for k in range(ncols):
            column = pl.ds(owner * ncols + k, rows, stride=cols)
            at = k * channels
            out_ref[owner, :, at : at + channels] = normed_s[column, :].astype(BF16)
            at = (ncols + k) * channels
            out_ref[owner, :, at : at + channels] = cot_s[column, :].astype(BF16)


def bias_out_kernel(parts_ref, out_ref):
    rows = parts_ref.shape[0]
    width = out_ref.shape[2] // PARTS
    bias = parts_ref[:, :width].astype(F32) + parts_ref[:, width : 2 * width].astype(F32)
    high = rows // PARTS
    packed = jnp.concatenate([bias[k * high : (k + 1) * high] for k in range(PARTS)], axis=1)
    for c in range(out_ref.shape[0]):
        out_ref[c] = packed


def project_kernel(
    normed_ref, twin_normed_ref, cot_ref, twin_cot_ref, w_ref, wt_ref, w_out_ref,
    query_ref, key_ref, value_ref, d_context_ref,
    query_t_ref, key_t_ref, value_t_ref, d_context_t_ref, gate_t_ref, d_gated_t_ref,
):
    normed = jnp.concatenate([normed_ref[...], twin_normed_ref[...]], axis=1)
    cot = jnp.concatenate([cot_ref[...], twin_cot_ref[...]], axis=1)
    for m, ref, ref_t in ((0, query_ref, query_t_ref), (1, key_ref, key_t_ref), (2, value_ref, value_t_ref)):
        ref[0] = nn(normed, w_ref[m]).astype(BF16)
        ref_t[0] = nt(wt_ref[m], normed).astype(BF16)
    gate_t = jax.nn.sigmoid(nt(wt_ref[3], normed))
    d_gated_t = nt(w_out_ref[...], cot)
    d_context_t = (d_gated_t * gate_t).astype(BF16)
    gate_t_ref[0] = gate_t
    d_gated_t_ref[0] = d_gated_t
    d_context_t_ref[0] = d_context_t
    d_context_ref[0] = turned(d_context_t)


def project(both, twin, w, wt, w_out, columns):
    rows = both.shape[0]
    channels = w.shape[-1]
    normed = pl.BlockSpec((rows, channels), lambda j: (0, j))
    cot = pl.BlockSpec((rows, channels), lambda j: (0, columns + j))
    flat = pl.BlockSpec((1, rows, channels), lambda j: (j, 0, 0))
    flat_t = pl.BlockSpec((1, channels, rows), lambda j: (j, 0, 0))
    upright = jax.ShapeDtypeStruct((columns, rows, channels), BF16)
    lying = jax.ShapeDtypeStruct((columns, channels, rows), BF16)
    wide = jax.ShapeDtypeStruct((columns, channels, rows), F32)
    return pl.pallas_call(
        project_kernel,
        grid=(columns,),
        in_specs=[
            normed, normed, cot, cot,
            pl.BlockSpec(w.shape, lambda j: (0, 0, 0)),
            pl.BlockSpec(wt.shape, lambda j: (0, 0, 0)),
            pl.BlockSpec(w_out.shape, lambda j: (0, 0)),
        ],
        out_specs=[flat] * 4 + [flat_t] * 6,
        out_shape=[upright] * 4 + [lying] * 4 + [wide] * 2,
        compiler_params=pltpu.CompilerParams(vmem_limit_bytes=56 << 20),
        name="project",
    )(both, twin, both, twin, w, wt, w_out)


def attention_kernel(
    valid_ref, got_ref, normed_ref, twin_normed_ref, cot_ref, twin_cot_ref,
    query_ref, key_ref, value_ref, d_context_ref,
    query_t_ref, key_t_ref, value_t_ref, d_context_t_ref, gate_t_ref, d_gated_t_ref,
    acts_ref, sent_ref, bias_s, total, grads_s, d_scores_s, weights_s, right_s,
):
    step = pl.program_id(0)
    steps = pl.num_programs(0)
    blocks, high, lanes = got_ref.shape
    rows, channels = normed_ref.shape
    slots = 4
    width = channels // slots
    half = channels // 2
    cols = rows // blocks
    scale = width ** (-0.5)

    @pl.when(step == 0)
    def _():
        for k in range(PARTS):
            for h in range(2):
                at = (2 * k + h) * cols
                pieces = [got_ref[c, :, at : at + cols] for c in range(blocks)]
                bias_s[h, k * high : (k + 1) * high, :] = jnp.concatenate(pieces, axis=1) * LOG2E
        total[...] = jnp.zeros_like(total)
        grads_s[...] = jnp.zeros_like(grads_s)

    query = query_ref[0]
    d_context = d_context_ref[0]
    lane = lax.broadcasted_iota(jnp.int32, (rows, channels), 1)
    sure = rows // 2
    keep = lax.broadcasted_iota(jnp.int32, (rows - sure, rows), 0) + sure < valid_ref[0]
    zero = jnp.zeros((rows, channels), BF16)
    for slot in range(slots):
        mine = (lane >= slot * width) & (lane < (slot + 1) * width)
        here = slice(slot * rows, (slot + 1) * rows)
        part = slice(slot * width, (slot + 1) * width)
        right_s[here, :channels] = jnp.where(mine, query, zero)
        right_s[here, channels:] = jnp.where(mine, d_context, zero)
        scores = nn(key_ref[0, :, part], query_t_ref[0, part]) * (scale * LOG2E) + bias_s[slot % 2]
        masked = jnp.where(keep, scores[sure:], MASKED * LOG2E)
        scores = jnp.concatenate([scores[:sure], masked], axis=0)
        top = jnp.max(scores, axis=0, keepdims=True)
        grown = jnp.exp2(scores - top)
        inverse = 1.0 / jnp.sum(grown, axis=0, keepdims=True)
        probs = grown * inverse
        weights_s[:, here] = probs.astype(BF16)
        d_probs = nn(value_ref[0, :, part], d_context_t_ref[0, part])
        delta = jnp.sum(grown * d_probs, axis=0, keepdims=True) * inverse
        d_scores = probs * (d_probs - delta)
        total[slot % 2] += d_scores
        d_scores_s[:, here] = d_scores.astype(BF16)
    blocks_t = [
        (nn(value_t_ref[0, s * width : (s + 1) * width], weights_s[:, s * rows : (s + 1) * rows]),
         nn(key_t_ref[0, s * width : (s + 1) * width], d_scores_s[:, s * rows : (s + 1) * rows]))
        for s in range(slots)
    ]
    context_t = jnp.concatenate([one for one, _ in blocks_t], axis=0).astype(BF16).astype(F32)
    d_query_t = (jnp.concatenate([two for _, two in blocks_t], axis=0) * scale).astype(BF16)
    d_key = (nn(d_scores_s[...], right_s[:, :channels]) * scale).astype(BF16)
    d_value = nn(weights_s[...], right_s[:, channels:]).astype(BF16)
    gate_t = gate_t_ref[0]
    gated_t = (gate_t * context_t).astype(BF16)
    d_gate_t = (d_gated_t_ref[0] * context_t * gate_t * (1.0 - gate_t)).astype(BF16)
    acts = [turned(gated_t), turned(d_query_t), d_key, d_value, turned(d_gate_t)]
    for m in range(5):
        acts_ref[0, :, m * channels : (m + 1) * channels] = acts[m]
    left = jnp.concatenate([d_query_t, turned(d_key), turned(d_value), d_gate_t], axis=0)
    normed = jnp.concatenate([normed_ref[...], twin_normed_ref[...]], axis=1)
    products = nn(left, normed)
    for m in range(4):
        near = products[m * channels : m * channels + half, :channels]
        far = products[m * channels + half : (m + 1) * channels, channels:]
        grads_s[m * half : (m + 1) * half, :] += near + far
    last = nn(gated_t[:half], cot_ref[...]) + nn(gated_t[half:], twin_cot_ref[...])
    grads_s[4 * half :, :] += last

    @pl.when(step == steps - 1)
    def _():
        for c in range(blocks):
            pieces = [
                total[h, k * high : (k + 1) * high, c * cols : (c + 1) * cols]
                for k in range(PARTS)
                for h in range(2)
            ]
            sent_ref[c, :high, :] = jnp.concatenate(pieces, axis=1).astype(BF16)
        grads = grads_s[...]
        share = grads.shape[0] // blocks
        rest = sent_ref.shape[1] - high
        spare = jnp.zeros((3 * rest - share, channels), F32)
        for c in range(blocks):
            mine = jnp.concatenate([grads[c * share : (c + 1) * share], spare], axis=0)
            pieces = [mine[k * rest : (k + 1) * rest] for k in range(3)]
            sent_ref[c, high:, :] = jnp.concatenate(pieces, axis=1).astype(BF16)


def attend(valid_len, got, both, twin, inner, columns):
    rows = both.shape[0]
    channels = inner[0].shape[-1]
    blocks, high, lanes = got.shape
    normed = pl.BlockSpec((rows, channels), lambda j: (0, j))
    cot = pl.BlockSpec((rows, channels), lambda j: (0, columns + j))
    flat = pl.BlockSpec((1, rows, channels), lambda j: (j, 0, 0))
    flat_t = pl.BlockSpec((1, channels, rows), lambda j: (j, 0, 0))
    return pl.pallas_call(
        attention_kernel,
        grid=(columns,),
        in_specs=[
            pl.BlockSpec(memory_space=pltpu.SMEM),
            pl.BlockSpec(got.shape, lambda j: (0, 0, 0)),
            normed, normed, cot, cot,
        ]
        + [flat] * 4
        + [flat_t] * 6,
        out_specs=[
            pl.BlockSpec((1, rows, 5 * channels), lambda j: (j, 0, 0)),
            pl.BlockSpec((blocks, high + 16, lanes), lambda j: (0, 0, 0)),
        ],
        out_shape=[
            jax.ShapeDtypeStruct((columns, rows, 5 * channels), BF16),
            jax.ShapeDtypeStruct((blocks, high + 16, lanes), BF16),
        ],
        scratch_shapes=[
            pltpu.VMEM((2, rows, rows), F32),
            pltpu.VMEM((2, rows, rows), F32),
            pltpu.VMEM((5 * channels // 2, channels), F32),
            pltpu.VMEM((rows, 4 * rows), BF16),
            pltpu.VMEM((rows, 4 * rows), BF16),
            pltpu.VMEM((4 * rows, 2 * channels), BF16),
        ],
        compiler_params=pltpu.CompilerParams(vmem_limit_bytes=56 << 20),
        name="attention",
    )(valid_len, got, both, twin, both, twin, *inner)


def merge_kernel(acts_ref, came_ref, w_ref, out_ref):
    column = pl.program_id(0)
    columns = pl.num_programs(0)
    channels = w_ref.shape[-1]
    parts = []
    for m in range(5):
        at = slice(m * channels, (m + 1) * channels)
        parts.append(nn(jnp.concatenate([acts_ref[0, :, at], came_ref[0, :, at]], axis=1), w_ref[m]))
    d_normed = parts[1] + parts[2] + parts[3] + parts[4]
    out_ref[:, pl.ds(pl.multiple_of(column * channels, channels), channels)] = parts[0].astype(BF16)
    second = pl.multiple_of((columns + column) * channels, channels)
    out_ref[:, pl.ds(second, channels)] = d_normed.astype(BF16)


def merge(acts, came, w):
    columns, rows, lanes = acts.shape
    channels = w.shape[-1]
    block = pl.BlockSpec((1, rows, lanes), lambda j: (j, 0, 0))
    return pl.pallas_call(
        merge_kernel,
        grid=(columns,),
        in_specs=[block, block, pl.BlockSpec(w.shape, lambda j: (0, 0, 0))],
        out_specs=pl.BlockSpec((rows, 2 * columns * channels), lambda j: (0, 0)),
        out_shape=jax.ShapeDtypeStruct((rows, 2 * columns * channels + 256), BF16),
        compiler_params=pltpu.CompilerParams(vmem_limit_bytes=56 << 20),
        name="merge",
    )(acts, came, w)


def sum_kernel(got_ref, main_ref, out_ref):
    blocks, high, lanes = got_ref.shape
    owners, rows, wide = out_ref.shape
    part = lanes // PARTS
    total = got_ref[0].astype(F32)
    for c in range(1, blocks):
        total = total + got_ref[c].astype(F32)
    grads = jnp.concatenate([total[part:, k * 128 : (k + 1) * 128] for k in range(3)], axis=0)
    share = 5
    gap = jnp.zeros((rows - 4 * share, 64), F32)
    for owner in range(owners):
        across, down = divmod(owner, part // rows)
        block = total[down * rows : (down + 1) * rows, across * part : (across + 1) * part]
        coarse = block.astype(BF16).astype(F32)
        mine = grads[owner // 2 * share : (owner // 2 + 1) * share]
        near = mine.astype(BF16).astype(F32)
        far = mine - near
        stack = jnp.concatenate([near[:, :64], near[:, 64:], far[:, :64], far[:, 64:], gap], axis=0)
        out_ref[owner] = jnp.concatenate([coarse, block - coarse, stack], axis=1).astype(BF16)


def add_sums(got, main, n_row):
    rows, wide = main.shape
    blocked = main.reshape(n_row, rows // n_row, wide)
    spec = pl.BlockSpec((n_row, rows // n_row, 256), lambda i: (0, 0, wide // 256 - 1))
    return pl.pallas_call(
        sum_kernel,
        grid=(1,),
        in_specs=[pl.BlockSpec(got.shape, lambda i: (0, 0, 0)), pl.BlockSpec(memory_space=pl.ANY)],
        out_specs=spec,
        out_shape=jax.ShapeDtypeStruct(blocked.shape, BF16),
        input_output_aliases={1: 0},
        compiler_params=pltpu.CompilerParams(vmem_limit_bytes=56 << 20),
        name="sum",
    )(got, blocked)


def finish_kernel(
    core_ref, got_ref, pair_ref, gain_ref, bias_weight_ref,
    d_normed_ref, last_ref, d_bias_s,
):
    owners, rows, wide = got_ref.shape
    cols, channels = pair_ref.shape[1:]
    heads = bias_weight_ref.shape[0]
    ncols = cols // owners
    main = 2 * ncols * channels
    xhat, inverse, normed = normalize(pair_ref, gain_ref)
    for owner in range(owners):
        for k in range(ncols):
            column = pl.ds(owner * ncols + k, rows, stride=cols)
            at = (ncols + k) * channels
            d_normed_ref[column, :] = got_ref[owner, :, at : at + channels].astype(F32)
    sums = [jnp.zeros((rows, 256), F32), jnp.zeros((rows, 256), F32)]
    for owner in range(owners):
        sums[owner % 2] = sums[owner % 2] + got_ref[owner, :, main:].astype(F32)
    for core in range(2):
        block = sums[core][:, : 2 * cols] + sums[core][:, 2 * cols : 4 * cols]
        block = block.astype(BF16).astype(F32)
        for h in range(2):
            at = pl.ds(2 * core + h, rows, stride=heads)
            d_bias_s[at, :] = block[:, h * cols : (h + 1) * cols]
    grads = jnp.where(core_ref[0] == 0, sums[0], sums[1])[:, 4 * cols :]
    grads = jnp.concatenate([grads[:5] + grads[10:15], grads[5:10] + grads[15:20]], axis=1)
    d_bias_t = jnp.transpose(d_bias_s[...]).astype(BF16)
    row = lax.broadcasted_iota(jnp.int32, (rows * heads, channels), 0)
    repeated = jnp.concatenate([bias_weight_ref[...].astype(F32)] * rows, axis=0).astype(BF16)
    weight_part = jnp.zeros((heads, channels), F32)
    for a in range(rows):
        here = slice(a * cols, (a + 1) * cols)
        mine = (row >= a * heads) & (row < (a + 1) * heads)
        weight = jnp.where(mine, repeated, jnp.zeros((rows * heads, channels), BF16))
        d_normed_ref[here, :] += nn(d_bias_t, weight)
        d_bias_a = d_bias_s[a * heads : (a + 1) * heads, :].astype(BF16)
        weight_part = weight_part + nn(d_bias_a, normed[here])
    gain_part = jnp.sum(d_normed_ref[...] * xhat, axis=0, keepdims=True)
    small = jnp.concatenate([weight_part, gain_part], axis=0)
    for t in range(5):
        pair = jnp.concatenate([grads[t : t + 1], small[t : t + 1]], axis=0)
        last_ref[:, t] = jnp.broadcast_to(pair[None], (last_ref.shape[0], 2, channels))


def output_kernel(got_ref, d_normed_ref, pair_ref, gain_ref, attended_ref, gradient_ref, moved_s):
    owners, rows, wide = got_ref.shape
    cols, channels = pair_ref.shape[1:]
    ncols = cols // owners
    xhat, inverse, normed = normalize(pair_ref, gain_ref)
    for owner in range(owners):
        for k in range(ncols):
            column = pl.ds(owner * ncols + k, rows, stride=cols)
            moved_s[column, :] = got_ref[owner, :, k * channels : (k + 1) * channels].astype(F32)
    attended_ref[...] = moved_s[...].astype(BF16).reshape(attended_ref.shape)
    scaled = d_normed_ref[...] * gain_ref[...]
    gradient = inverse * (
        scaled
        - jnp.mean(scaled, axis=-1, keepdims=True)
        - xhat * jnp.mean(scaled * xhat, axis=-1, keepdims=True)
    )
    gradient_ref[...] = gradient.reshape(gradient_ref.shape)


def gather_kernel(n_row, n_col, got_ref, grad_ref, weight_ref, gain_ref, halves_s):
    channels = got_ref.shape[-1]
    share = got_ref.shape[1]
    half = channels // 2
    for r in range(n_row):
        for c in range(n_col):
            at = (c * (n_row // 2) + r // 2) * share
            halves_s[r % 2, at : at + share, :] = got_ref[r * n_col + c, :, 0, :]
    small = jnp.sum(got_ref[:, :, 1, :], axis=0)
    heads = weight_ref.shape[0]
    weight_ref[...] = small[:heads]
    gain_ref[...] = small[heads : heads + 1]
    for m in range(5):
        both = [halves_s[core, m * half : (m + 1) * half, :] for core in range(2)]
        both = jnp.concatenate(both, axis=0)
        grad_ref[m] = jnp.transpose(both) if m < 4 else both


def shards(pair, gain, projections, bias_weight, valid_len, out_cotangent):
    n_row = lax.axis_size(ROW)
    n_col = lax.axis_size(COL)
    n_all = n_row * n_col
    tile_rows, tile_cols, channels = pair.shape
    rows = tile_rows * n_row
    heads = bias_weight.shape[1]
    ncols = tile_cols // n_row
    tile = tile_rows * tile_cols
    main = 2 * ncols * channels
    half = channels // 2
    shape = jax.ShapeDtypeStruct
    gain_row = gain[None, :]
    weight_t = bias_weight.T
    swap = [(0, 1), (1, 0)]
    core = lax.axis_index(CORE).astype(jnp.int32)
    halves = projections[:4].reshape(4, channels, 2, half)
    rows_out = projections[4].reshape(2, half, channels)
    own = lax.dynamic_index_in_dim(halves, core, 2, keepdims=False)
    other = lax.dynamic_index_in_dim(halves, 1 - core, 2, keepdims=False)
    own_out = lax.dynamic_index_in_dim(rows_out, core, 0, keepdims=False)
    other_out = lax.dynamic_index_in_dim(rows_out, 1 - core, 0, keepdims=False)
    zero = jnp.zeros_like(own)
    w = jnp.concatenate(
        [jnp.concatenate([own, zero], axis=2), jnp.concatenate([zero, own], axis=2)], axis=1
    )
    zero_out = jnp.zeros_like(own_out)
    w_out = jnp.concatenate(
        [jnp.concatenate([own_out, zero_out], axis=1), jnp.concatenate([zero_out, own_out], axis=1)],
        axis=0,
    )
    mine = jnp.concatenate([own_out[None], jnp.swapaxes(own, 1, 2)], axis=0)
    theirs = jnp.concatenate([other_out[None], jnp.swapaxes(other, 1, 2)], axis=0)
    gap = jnp.zeros((5, channels, channels), BF16)
    w_merge = jnp.concatenate([mine, gap, theirs], axis=1)

    packed = call(
        pack_kernel, shape((n_row, tile_rows, main + 256), BF16),
        [pltpu.VMEM((tile, channels), F32), pltpu.VMEM((tile, channels), F32),
         pltpu.VMEM((heads * tile_rows, tile_cols), F32)],
        "pack", pair, out_cotangent, gain_row, weight_t,
    )
    both = exchange(packed, ROW).reshape(rows, main + 256)
    high = rows // PARTS
    lanes = PARTS * 2 * tile_cols
    spread = pl.pallas_call(
        bias_out_kernel,
        grid=(1,),
        in_specs=[pl.BlockSpec((rows, 256), lambda i: (0, main // 256))],
        out_specs=pl.BlockSpec((n_col, high, lanes), lambda i: (0, 0, 0)),
        out_shape=shape((n_col, high, lanes), F32),
        name="bias_out",
    )(both)
    got = exchange(spread, COL)
    twin = lax.ppermute(both, CORE, swap)
    inner = project(both, twin, w, jnp.swapaxes(w, 1, 2), w_out, ncols)
    acts, sent = attend(valid_len, got, both, twin, inner, ncols)
    summed = exchange(sent, COL)
    out = merge(acts, lax.ppermute(acts, CORE, swap), w_merge)
    back = exchange(add_sums(summed, out, n_row), ROW)
    smem = pl.BlockSpec(memory_space=pltpu.SMEM)
    vmem = pl.BlockSpec(memory_space=pltpu.VMEM)
    d_normed, last = pl.pallas_call(
        finish_kernel,
        in_specs=[smem] + [vmem] * 4,
        out_shape=[shape((tile, channels), F32), shape((n_all, 5, 2, channels), F32)],
        scratch_shapes=[pltpu.VMEM((heads * tile_rows, tile_cols), F32)],
        compiler_params=pltpu.CompilerParams(vmem_limit_bytes=56 << 20),
        name="finish",
    )(core[None], back, pair, gain_row, weight_t)
    everyone = exchange(last, ALL)
    attended, pair_gradient = call(
        output_kernel, [shape(pair.shape, BF16), shape(pair.shape, F32)],
        [pltpu.VMEM((tile, channels), F32)], "output", back, d_normed, pair, gain_row,
    )
    projection_grad, bias_weight_grad, gain_gradient = call(
        functools.partial(gather_kernel, n_row, n_col),
        [shape(projections.shape, F32), shape((heads, channels), F32), shape((1, channels), F32)],
        [pltpu.VMEM((2, 5 * half, channels), F32)], "gather", everyone,
    )
    return (attended, pair_gradient, projection_grad, bias_weight_grad.T, gain_gradient[0])


def solution(mesh):
    torus = Mesh(mesh.devices.reshape(2, 4, 2, 2, 4), ALL)
    in_specs = (P(ROW, COL, None), P(), P(), P(), P(), P(ROW, COL, None))
    out_specs = (P(ROW, COL, None), P(ROW, COL, None), P(), P(), P())
    return jax.shard_map(
        shards, mesh=torus, in_specs=in_specs, out_specs=out_specs, check_vma=False
    )
```

```python
import functools

import jax
import jax.numpy as jnp
from jax import lax
from jax.experimental import pallas as pl
from jax.experimental.pallas import tpu as pltpu
from jax.sharding import Mesh
from jax.sharding import PartitionSpec as P

ROW = ("row_0", "row_1", "row_2")
COL = ("col_0", "col_1")
ALL = ROW + COL
CORE = "row_2"
EPS = 1e-05
MASKED = -1000000000.0
LOG2E = 1.4426950408889634
PARTS = 4
F32 = jnp.float32
BF16 = jnp.bfloat16


def nn(left, right):
    return lax.dot_general(left, right, (((1,), (0,)), ((), ())), preferred_element_type=F32)


def nt(left, right):
    return lax.dot_general(left, right, (((1,), (1,)), ((), ())), preferred_element_type=F32)


def turned(value):
    return jnp.transpose(value.astype(F32)).astype(value.dtype)


def exchange(value, axes):
    return lax.all_to_all(value, axes, split_axis=0, concat_axis=0, tiled=True)


def call(kernel, out_shape, scratch, name, *operands):
    return pl.pallas_call(
        kernel,
        out_shape=out_shape,
        scratch_shapes=scratch,
        compiler_params=pltpu.CompilerParams(vmem_limit_bytes=56 << 20),
        name=name,
    )(*operands)


def coarse_fine(value):
    coarse = value.astype(BF16)
    return coarse, (value - coarse.astype(F32)).astype(BF16)


def normalize(pair_ref, gain_ref):
    rows, cols, channels = pair_ref.shape
    pair = pair_ref[...].astype(F32).reshape(rows * cols, channels)
    average = jnp.mean(pair, axis=-1, keepdims=True)
    var = jnp.mean((pair - average) ** 2, axis=-1, keepdims=True)
    inverse = lax.rsqrt(var + EPS)
    xhat = (pair - average) * inverse
    return xhat, inverse, (xhat * gain_ref[...]).astype(BF16)


def pack_kernel(pair_ref, cot_ref, gain_ref, bias_weight_ref, out_ref, normed_s, cot_s, bias_s):
    rows, cols, channels = pair_ref.shape
    owners = out_ref.shape[0]
    ncols = cols // owners
    heads = bias_weight_ref.shape[0]
    normed = normalize(pair_ref, gain_ref)[2]
    normed_s[...] = normed.astype(F32)
    cot_s[...] = cot_ref[...].astype(F32).reshape(rows * cols, channels)
    for a in range(rows):
        bias = nt(bias_weight_ref[...], normed[a * cols : (a + 1) * cols])
        bias_s[pl.ds(a, heads, stride=rows), :] = bias
    pad = jnp.zeros((rows, 256 - 4 * cols), BF16)
    for core in range(2):
        first = 2 * core * rows
        bias = jnp.concatenate([bias_s[first : first + rows], bias_s[first + rows : first + 2 * rows]], axis=1)
        bias = jnp.concatenate([*coarse_fine(bias), pad], axis=1)
        for owner in range(core, owners, 2):
            out_ref[owner, :, 2 * ncols * channels :] = bias
    for owner in range(owners):
        for k in range(ncols):
            column = pl.ds(owner * ncols + k, rows, stride=cols)
            at = k * channels
            out_ref[owner, :, at : at + channels] = normed_s[column, :].astype(BF16)
            at = (ncols + k) * channels
            out_ref[owner, :, at : at + channels] = cot_s[column, :].astype(BF16)


def bias_out_kernel(parts_ref, out_ref):
    rows = parts_ref.shape[0]
    width = out_ref.shape[2] // PARTS
    bias = parts_ref[:, :width].astype(F32) + parts_ref[:, width : 2 * width].astype(F32)
    high = rows // PARTS
    packed = jnp.concatenate([bias[k * high : (k + 1) * high] for k in range(PARTS)], axis=1)
    for c in range(out_ref.shape[0]):
        out_ref[c] = packed


def project_kernel(
    normed_ref, twin_normed_ref, cot_ref, twin_cot_ref, w_ref, wt_ref, w_out_ref,
    query_ref, key_ref, value_ref, d_context_ref,
    query_t_ref, key_t_ref, value_t_ref, d_context_t_ref, gate_t_ref, d_gated_t_ref,
):
    normed = jnp.concatenate([normed_ref[...], twin_normed_ref[...]], axis=1)
    cot = jnp.concatenate([cot_ref[...], twin_cot_ref[...]], axis=1)
    for m, ref, ref_t in ((0, query_ref, query_t_ref), (1, key_ref, key_t_ref), (2, value_ref, value_t_ref)):
        ref[0] = nn(normed, w_ref[m]).astype(BF16)
        ref_t[0] = nt(wt_ref[m], normed).astype(BF16)
    gate_t = jax.nn.sigmoid(nt(wt_ref[3], normed))
    d_gated_t = nt(w_out_ref[...], cot)
    d_context_t = (d_gated_t * gate_t).astype(BF16)
    gate_t_ref[0] = gate_t
    d_gated_t_ref[0] = d_gated_t
    d_context_t_ref[0] = d_context_t
    d_context_ref[0] = turned(d_context_t)


def project(both, twin, w, wt, w_out, columns):
    rows = both.shape[0]
    channels = w.shape[-1]
    normed = pl.BlockSpec((rows, channels), lambda j: (0, j))
    cot = pl.BlockSpec((rows, channels), lambda j: (0, columns + j))
    flat = pl.BlockSpec((1, rows, channels), lambda j: (j, 0, 0))
    flat_t = pl.BlockSpec((1, channels, rows), lambda j: (j, 0, 0))
    upright = jax.ShapeDtypeStruct((columns, rows, channels), BF16)
    lying = jax.ShapeDtypeStruct((columns, channels, rows), BF16)
    wide = jax.ShapeDtypeStruct((columns, channels, rows), F32)
    return pl.pallas_call(
        project_kernel,
        grid=(columns,),
        in_specs=[
            normed, normed, cot, cot,
            pl.BlockSpec(w.shape, lambda j: (0, 0, 0)),
            pl.BlockSpec(wt.shape, lambda j: (0, 0, 0)),
            pl.BlockSpec(w_out.shape, lambda j: (0, 0)),
        ],
        out_specs=[flat] * 4 + [flat_t] * 6,
        out_shape=[upright] * 4 + [lying] * 4 + [wide] * 2,
        compiler_params=pltpu.CompilerParams(vmem_limit_bytes=56 << 20),
        name="project",
    )(both, twin, both, twin, w, wt, w_out)


def attention_kernel(
    valid_ref, got_ref, normed_ref, twin_normed_ref, cot_ref, twin_cot_ref,
    query_ref, key_ref, value_ref, d_context_ref,
    query_t_ref, key_t_ref, value_t_ref, d_context_t_ref, gate_t_ref, d_gated_t_ref,
    acts_ref, sent_ref, bias_s, total, grads_s, d_scores_s, weights_s, right_s,
):
    step = pl.program_id(0)
    steps = pl.num_programs(0)
    blocks, high, lanes = got_ref.shape
    rows, channels = normed_ref.shape
    slots = 4
    width = channels // slots
    half = channels // 2
    cols = rows // blocks
    scale = width ** (-0.5)

    @pl.when(step == 0)
    def _():
        for k in range(PARTS):
            for h in range(2):
                at = (2 * k + h) * cols
                pieces = [got_ref[c, :, at : at + cols] for c in range(blocks)]
                bias_s[h, k * high : (k + 1) * high, :] = jnp.concatenate(pieces, axis=1) * LOG2E
        total[...] = jnp.zeros_like(total)
        grads_s[...] = jnp.zeros_like(grads_s)

    query = query_ref[0]
    d_context = d_context_ref[0]
    lane = lax.broadcasted_iota(jnp.int32, (rows, channels), 1)
    sure = rows // 2
    keep = lax.broadcasted_iota(jnp.int32, (rows - sure, rows), 0) + sure < valid_ref[0]
    zero = jnp.zeros((rows, channels), BF16)
    for slot in range(slots):
        mine = (lane >= slot * width) & (lane < (slot + 1) * width)
        here = slice(slot * rows, (slot + 1) * rows)
        part = slice(slot * width, (slot + 1) * width)
        right_s[here, :channels] = jnp.where(mine, query, zero)
        right_s[here, channels:] = jnp.where(mine, d_context, zero)
        scores = nn(key_ref[0, :, part], query_t_ref[0, part]) * (scale * LOG2E) + bias_s[slot % 2]
        masked = jnp.where(keep, scores[sure:], MASKED * LOG2E)
        scores = jnp.concatenate([scores[:sure], masked], axis=0)
        top = jnp.max(scores, axis=0, keepdims=True)
        grown = jnp.exp2(scores - top)
        inverse = 1.0 / jnp.sum(grown, axis=0, keepdims=True)
        probs = grown * inverse
        weights_s[:, here] = probs.astype(BF16)
        d_probs = nn(value_ref[0, :, part], d_context_t_ref[0, part])
        delta = jnp.sum(grown * d_probs, axis=0, keepdims=True) * inverse
        d_scores = probs * (d_probs - delta)
        total[slot % 2] += d_scores
        d_scores_s[:, here] = d_scores.astype(BF16)
    blocks_t = [
        (nn(value_t_ref[0, s * width : (s + 1) * width], weights_s[:, s * rows : (s + 1) * rows]),
         nn(key_t_ref[0, s * width : (s + 1) * width], d_scores_s[:, s * rows : (s + 1) * rows]))
        for s in range(slots)
    ]
    context_t = jnp.concatenate([one for one, _ in blocks_t], axis=0).astype(BF16).astype(F32)
    d_query_t = (jnp.concatenate([two for _, two in blocks_t], axis=0) * scale).astype(BF16)
    d_key = (nn(d_scores_s[...], right_s[:, :channels]) * scale).astype(BF16)
    d_value = nn(weights_s[...], right_s[:, channels:]).astype(BF16)
    gate_t = gate_t_ref[0]
    gated_t = (gate_t * context_t).astype(BF16)
    d_gate_t = (d_gated_t_ref[0] * context_t * gate_t * (1.0 - gate_t)).astype(BF16)
    acts = [turned(gated_t), turned(d_query_t), d_key, d_value, turned(d_gate_t)]
    for m in range(5):
        acts_ref[0, :, m * channels : (m + 1) * channels] = acts[m]
    left = jnp.concatenate([d_query_t, turned(d_key), turned(d_value), d_gate_t], axis=0)
    normed = jnp.concatenate([normed_ref[...], twin_normed_ref[...]], axis=1)
    products = nn(left, normed)
    for m in range(4):
        near = products[m * channels : m * channels + half, :channels]
        far = products[m * channels + half : (m + 1) * channels, channels:]
        grads_s[m * half : (m + 1) * half, :] += near + far
    last = nn(gated_t[:half], cot_ref[...]) + nn(gated_t[half:], twin_cot_ref[...])
    grads_s[4 * half :, :] += last

    @pl.when(step == steps - 1)
    def _():
        for c in range(blocks):
            pieces = [
                total[h, k * high : (k + 1) * high, c * cols : (c + 1) * cols]
                for k in range(PARTS)
                for h in range(2)
            ]
            sent_ref[c, :high, :] = jnp.concatenate(pieces, axis=1).astype(BF16)
        grads = grads_s[...]
        share = grads.shape[0] // blocks
        rest = sent_ref.shape[1] - high
        spare = jnp.zeros((3 * rest - share, channels), F32)
        for c in range(blocks):
            mine = jnp.concatenate([grads[c * share : (c + 1) * share], spare], axis=0)
            pieces = [mine[k * rest : (k + 1) * rest] for k in range(3)]
            sent_ref[c, high:, :] = jnp.concatenate(pieces, axis=1).astype(BF16)


def attend(valid_len, got, both, twin, inner, columns):
    rows = both.shape[0]
    channels = inner[0].shape[-1]
    blocks, high, lanes = got.shape
    normed = pl.BlockSpec((rows, channels), lambda j: (0, j))
    cot = pl.BlockSpec((rows, channels), lambda j: (0, columns + j))
    flat = pl.BlockSpec((1, rows, channels), lambda j: (j, 0, 0))
    flat_t = pl.BlockSpec((1, channels, rows), lambda j: (j, 0, 0))
    return pl.pallas_call(
        attention_kernel,
        grid=(columns,),
        in_specs=[
            pl.BlockSpec(memory_space=pltpu.SMEM),
            pl.BlockSpec(memory_space=pltpu.VMEM),
            normed, normed, cot, cot,
        ]
        + [flat] * 4
        + [flat_t] * 6,
        out_specs=[
            pl.BlockSpec((1, rows, 5 * channels), lambda j: (j, 0, 0)),
            pl.BlockSpec((blocks, high + 16, lanes), lambda j: (0, 0, 0)),
        ],
        out_shape=[
            jax.ShapeDtypeStruct((columns, rows, 5 * channels), BF16),
            jax.ShapeDtypeStruct((blocks, high + 16, lanes), BF16),
        ],
        scratch_shapes=[
            pltpu.VMEM((2, rows, rows), F32),
            pltpu.VMEM((2, rows, rows), F32),
            pltpu.VMEM((5 * channels // 2, channels), F32),
            pltpu.VMEM((rows, 4 * rows), BF16),
            pltpu.VMEM((rows, 4 * rows), BF16),
            pltpu.VMEM((4 * rows, 2 * channels), BF16),
        ],
        compiler_params=pltpu.CompilerParams(vmem_limit_bytes=56 << 20),
        name="attention",
    )(valid_len, got, both, twin, both, twin, *inner)


def merge_kernel(acts_ref, came_ref, w_ref, out_ref):
    column = pl.program_id(0)
    columns = pl.num_programs(0)
    channels = w_ref.shape[-1]
    parts = []
    for m in range(5):
        at = slice(m * channels, (m + 1) * channels)
        parts.append(nn(jnp.concatenate([acts_ref[0, :, at], came_ref[0, :, at]], axis=1), w_ref[m]))
    d_normed = parts[1] + parts[2] + parts[3] + parts[4]
    out_ref[:, pl.ds(pl.multiple_of(column * channels, channels), channels)] = parts[0].astype(BF16)
    second = pl.multiple_of((columns + column) * channels, channels)
    out_ref[:, pl.ds(second, channels)] = d_normed.astype(BF16)


def merge(acts, came, w):
    columns, rows, lanes = acts.shape
    channels = w.shape[-1]
    block = pl.BlockSpec((1, rows, lanes), lambda j: (j, 0, 0))
    return pl.pallas_call(
        merge_kernel,
        grid=(columns,),
        in_specs=[block, block, pl.BlockSpec(w.shape, lambda j: (0, 0, 0))],
        out_specs=pl.BlockSpec((rows, 2 * columns * channels), lambda j: (0, 0)),
        out_shape=jax.ShapeDtypeStruct((rows, 2 * columns * channels + 256), BF16),
        compiler_params=pltpu.CompilerParams(vmem_limit_bytes=56 << 20),
        name="merge",
    )(acts, came, w)


def sum_kernel(got_ref, main_ref, out_ref):
    blocks, high, lanes = got_ref.shape
    owners, rows, wide = out_ref.shape
    part = lanes // PARTS
    total = got_ref[0].astype(F32)
    for c in range(1, blocks):
        total = total + got_ref[c].astype(F32)
    grads = jnp.concatenate([total[part:, k * 128 : (k + 1) * 128] for k in range(3)], axis=0)
    share = 5
    gap = jnp.zeros((rows - 4 * share, 64), F32)
    for owner in range(owners):
        across, down = divmod(owner, part // rows)
        block = total[down * rows : (down + 1) * rows, across * part : (across + 1) * part]
        coarse = block.astype(BF16).astype(F32)
        mine = grads[owner // 2 * share : (owner // 2 + 1) * share]
        near = mine.astype(BF16).astype(F32)
        far = mine - near
        stack = jnp.concatenate([near[:, :64], near[:, 64:], far[:, :64], far[:, 64:], gap], axis=0)
        out_ref[owner] = jnp.concatenate([coarse, block - coarse, stack], axis=1).astype(BF16)


def add_sums(got, main, n_row):
    rows, wide = main.shape
    blocked = main.reshape(n_row, rows // n_row, wide)
    spec = pl.BlockSpec((n_row, rows // n_row, 256), lambda i: (0, 0, wide // 256 - 1))
    return pl.pallas_call(
        sum_kernel,
        grid=(1,),
        in_specs=[pl.BlockSpec(memory_space=pltpu.VMEM), pl.BlockSpec(memory_space=pl.ANY)],
        out_specs=spec,
        out_shape=jax.ShapeDtypeStruct(blocked.shape, BF16),
        input_output_aliases={1: 0},
        compiler_params=pltpu.CompilerParams(vmem_limit_bytes=56 << 20),
        name="sum",
    )(got, blocked)


def finish_kernel(
    core_ref, got_ref, pair_ref, gain_ref, bias_weight_ref,
    d_normed_ref, last_ref, d_bias_s,
):
    owners, rows, wide = got_ref.shape
    cols, channels = pair_ref.shape[1:]
    heads = bias_weight_ref.shape[0]
    ncols = cols // owners
    main = 2 * ncols * channels
    xhat, inverse, normed = normalize(pair_ref, gain_ref)
    for owner in range(owners):
        for k in range(ncols):
            column = pl.ds(owner * ncols + k, rows, stride=cols)
            at = (ncols + k) * channels
            d_normed_ref[column, :] = got_ref[owner, :, at : at + channels].astype(F32)
    sums = [jnp.zeros((rows, 256), F32), jnp.zeros((rows, 256), F32)]
    for owner in range(owners):
        sums[owner % 2] = sums[owner % 2] + got_ref[owner, :, main:].astype(F32)
    for core in range(2):
        block = sums[core][:, : 2 * cols] + sums[core][:, 2 * cols : 4 * cols]
        block = block.astype(BF16).astype(F32)
        for h in range(2):
            at = pl.ds(2 * core + h, rows, stride=heads)
            d_bias_s[at, :] = block[:, h * cols : (h + 1) * cols]
    grads = jnp.where(core_ref[0] == 0, sums[0], sums[1])[:, 4 * cols :]
    grads = jnp.concatenate([grads[:5] + grads[10:15], grads[5:10] + grads[15:20]], axis=1)
    d_bias_t = jnp.transpose(d_bias_s[...]).astype(BF16)
    row = lax.broadcasted_iota(jnp.int32, (rows * heads, channels), 0)
    repeated = jnp.concatenate([bias_weight_ref[...].astype(F32)] * rows, axis=0).astype(BF16)
    weight_part = jnp.zeros((heads, channels), F32)
    for a in range(rows):
        here = slice(a * cols, (a + 1) * cols)
        mine = (row >= a * heads) & (row < (a + 1) * heads)
        weight = jnp.where(mine, repeated, jnp.zeros((rows * heads, channels), BF16))
        d_normed_ref[here, :] += nn(d_bias_t, weight)
        d_bias_a = d_bias_s[a * heads : (a + 1) * heads, :].astype(BF16)
        weight_part = weight_part + nn(d_bias_a, normed[here])
    gain_part = jnp.sum(d_normed_ref[...] * xhat, axis=0, keepdims=True)
    small = jnp.concatenate([weight_part, gain_part], axis=0)
    for t in range(5):
        pair = jnp.concatenate([grads[t : t + 1], small[t : t + 1]], axis=0)
        last_ref[:, t] = jnp.broadcast_to(pair[None], (last_ref.shape[0], 2, channels))


def output_kernel(got_ref, d_normed_ref, pair_ref, gain_ref, attended_ref, gradient_ref, moved_s):
    owners, rows, wide = got_ref.shape
    cols, channels = pair_ref.shape[1:]
    ncols = cols // owners
    xhat, inverse, normed = normalize(pair_ref, gain_ref)
    for owner in range(owners):
        for k in range(ncols):
            column = pl.ds(owner * ncols + k, rows, stride=cols)
            moved_s[column, :] = got_ref[owner, :, k * channels : (k + 1) * channels].astype(F32)
    attended_ref[...] = moved_s[...].astype(BF16).reshape(attended_ref.shape)
    scaled = d_normed_ref[...] * gain_ref[...]
    gradient = inverse * (
        scaled
        - jnp.mean(scaled, axis=-1, keepdims=True)
        - xhat * jnp.mean(scaled * xhat, axis=-1, keepdims=True)
    )
    gradient_ref[...] = gradient.reshape(gradient_ref.shape)


def gather_kernel(n_row, n_col, got_ref, grad_ref, weight_ref, gain_ref, halves_s):
    channels = got_ref.shape[-1]
    share = got_ref.shape[1]
    half = channels // 2
    for r in range(n_row):
        for c in range(n_col):
            at = (c * (n_row // 2) + r // 2) * share
            halves_s[r % 2, at : at + share, :] = got_ref[r * n_col + c, :, 0, :]
    small = jnp.sum(got_ref[:, :, 1, :], axis=0)
    heads = weight_ref.shape[0]
    weight_ref[...] = small[:heads]
    gain_ref[...] = small[heads : heads + 1]
    for m in range(5):
        both = [halves_s[core, m * half : (m + 1) * half, :] for core in range(2)]
        both = jnp.concatenate(both, axis=0)
        grad_ref[m] = jnp.transpose(both) if m < 4 else both


def shards(pair, gain, projections, bias_weight, valid_len, out_cotangent):
    n_row = lax.axis_size(ROW)
    n_col = lax.axis_size(COL)
    n_all = n_row * n_col
    tile_rows, tile_cols, channels = pair.shape
    rows = tile_rows * n_row
    heads = bias_weight.shape[1]
    ncols = tile_cols // n_row
    tile = tile_rows * tile_cols
    main = 2 * ncols * channels
    half = channels // 2
    shape = jax.ShapeDtypeStruct
    gain_row = gain[None, :]
    weight_t = bias_weight.T
    swap = [(0, 1), (1, 0)]
    core = lax.axis_index(CORE).astype(jnp.int32)
    halves = projections[:4].reshape(4, channels, 2, half)
    rows_out = projections[4].reshape(2, half, channels)
    own = lax.dynamic_index_in_dim(halves, core, 2, keepdims=False)
    other = lax.dynamic_index_in_dim(halves, 1 - core, 2, keepdims=False)
    own_out = lax.dynamic_index_in_dim(rows_out, core, 0, keepdims=False)
    other_out = lax.dynamic_index_in_dim(rows_out, 1 - core, 0, keepdims=False)
    zero = jnp.zeros_like(own)
    w = jnp.concatenate(
        [jnp.concatenate([own, zero], axis=2), jnp.concatenate([zero, own], axis=2)], axis=1
    )
    zero_out = jnp.zeros_like(own_out)
    w_out = jnp.concatenate(
        [jnp.concatenate([own_out, zero_out], axis=1), jnp.concatenate([zero_out, own_out], axis=1)],
        axis=0,
    )
    mine = jnp.concatenate([own_out[None], jnp.swapaxes(own, 1, 2)], axis=0)
    theirs = jnp.concatenate([other_out[None], jnp.swapaxes(other, 1, 2)], axis=0)
    gap = jnp.zeros((5, channels, channels), BF16)
    w_merge = jnp.concatenate([mine, gap, theirs], axis=1)

    packed = call(
        pack_kernel, shape((n_row, tile_rows, main + 256), BF16),
        [pltpu.VMEM((tile, channels), F32), pltpu.VMEM((tile, channels), F32),
         pltpu.VMEM((heads * tile_rows, tile_cols), F32)],
        "pack", pair, out_cotangent, gain_row, weight_t,
    )
    both = exchange(packed, ROW).reshape(rows, main + 256)
    high = rows // PARTS
    lanes = PARTS * 2 * tile_cols
    spread = pl.pallas_call(
        bias_out_kernel,
        grid=(1,),
        in_specs=[pl.BlockSpec((rows, 256), lambda i: (0, main // 256))],
        out_specs=pl.BlockSpec((n_col, high, lanes), lambda i: (0, 0, 0)),
        out_shape=shape((n_col, high, lanes), F32),
        name="bias_out",
    )(both)
    got = pltpu.with_memory_space_constraint(exchange(spread, COL), pltpu.VMEM)
    twin = lax.ppermute(both, CORE, swap)
    inner = project(both, twin, w, jnp.swapaxes(w, 1, 2), w_out, ncols)
    acts, sent = attend(valid_len, got, both, twin, inner, ncols)
    summed = pltpu.with_memory_space_constraint(exchange(sent, COL), pltpu.VMEM)
    out = merge(acts, lax.ppermute(acts, CORE, swap), w_merge)
    back = pltpu.with_memory_space_constraint(exchange(add_sums(summed, out, n_row), ROW), pltpu.VMEM)
    smem = pl.BlockSpec(memory_space=pltpu.SMEM)
    vmem = pl.BlockSpec(memory_space=pltpu.VMEM)
    d_normed, last = pl.pallas_call(
        finish_kernel,
        in_specs=[smem] + [vmem] * 4,
        out_shape=[shape((tile, channels), F32), shape((n_all, 5, 2, channels), F32)],
        scratch_shapes=[pltpu.VMEM((heads * tile_rows, tile_cols), F32)],
        compiler_params=pltpu.CompilerParams(vmem_limit_bytes=56 << 20),
        name="finish",
    )(core[None], back, pair, gain_row, weight_t)
    everyone = pltpu.with_memory_space_constraint(exchange(last, ALL), pltpu.VMEM)
    attended, pair_gradient = pl.pallas_call(
        output_kernel,
        in_specs=[vmem] * 4,
        out_shape=[shape(pair.shape, BF16), shape(pair.shape, F32)],
        scratch_shapes=[pltpu.VMEM((tile, channels), F32)],
        compiler_params=pltpu.CompilerParams(vmem_limit_bytes=56 << 20),
        name="output",
    )(back, d_normed, pair, gain_row)
    projection_grad, bias_weight_grad, gain_gradient = pl.pallas_call(
        functools.partial(gather_kernel, n_row, n_col),
        in_specs=[vmem],
        out_shape=[shape(projections.shape, F32), shape((heads, channels), F32), shape((1, channels), F32)],
        scratch_shapes=[pltpu.VMEM((2, 5 * half, channels), F32)],
        name="gather",
    )(everyone)
    return (attended, pair_gradient, projection_grad, bias_weight_grad.T, gain_gradient[0])


def solution(mesh):
    torus = Mesh(mesh.devices.reshape(2, 4, 2, 2, 4), ALL)
    in_specs = (P(ROW, COL, None), P(), P(), P(), P(), P(ROW, COL, None))
    out_specs = (P(ROW, COL, None), P(ROW, COL, None), P(), P(), P())
    return jax.shard_map(
        shards, mesh=torus, in_specs=in_specs, out_specs=out_specs, check_vma=False
    )
```

```python
import functools

import jax
import jax.numpy as jnp
from jax import lax
from jax.experimental import pallas as pl
from jax.experimental.pallas import tpu as pltpu
from jax.sharding import Mesh
from jax.sharding import PartitionSpec as P

ROW = ("row_0", "row_1", "row_2")
COL = ("col_0", "col_1")
ALL = ROW + COL
CORE = "row_2"
EPS = 1e-05
MASKED = -1000000000.0
LOG2E = 1.4426950408889634
PARTS = 4
F32 = jnp.float32
BF16 = jnp.bfloat16


def nn(left, right):
    return lax.dot_general(left, right, (((1,), (0,)), ((), ())), preferred_element_type=F32)


def nt(left, right):
    return lax.dot_general(left, right, (((1,), (1,)), ((), ())), preferred_element_type=F32)


def turned(value):
    return jnp.transpose(value.astype(F32)).astype(value.dtype)


def exchange(value, axes):
    return lax.all_to_all(value, axes, split_axis=0, concat_axis=0, tiled=True)


def call(kernel, out_shape, scratch, name, *operands):
    return pl.pallas_call(
        kernel,
        out_shape=out_shape,
        scratch_shapes=scratch,
        compiler_params=pltpu.CompilerParams(vmem_limit_bytes=24 << 20),
        name=name,
    )(*operands)


def resident(value):
    return pltpu.with_memory_space_constraint(value, pltpu.VMEM)


def distant(value):
    return pltpu.with_memory_space_constraint(value, pltpu.HBM)


def fetched(sources, targets, sem):
    copies = [pltpu.make_async_copy(a, b, sem.at[k]) for k, (a, b) in enumerate(zip(sources, targets))]
    for copy in copies:
        copy.start()
    return copies


def coarse_fine(value):
    coarse = value.astype(BF16)
    return coarse, (value - coarse.astype(F32)).astype(BF16)


def normalize(pair_ref, gain_ref):
    rows, cols, channels = pair_ref.shape
    pair = pair_ref[...].astype(F32).reshape(rows * cols, channels)
    average = jnp.mean(pair, axis=-1, keepdims=True)
    var = jnp.mean((pair - average) ** 2, axis=-1, keepdims=True)
    inverse = lax.rsqrt(var + EPS)
    xhat = (pair - average) * inverse
    return xhat, inverse, (xhat * gain_ref[...]).astype(BF16)


def pack_kernel(
    pair_at, cot_at, gain_at, bias_weight_at,
    out_ref, pair_ref, cot_ref, gain_ref, bias_weight_ref, sem, normed_s, cot_s, bias_s,
):
    copies = fetched(
        (pair_at, gain_at, bias_weight_at, cot_at), (pair_ref, gain_ref, bias_weight_ref, cot_ref), sem
    )
    for copy in copies[:3]:
        copy.wait()
    rows, cols, channels = pair_ref.shape
    owners = out_ref.shape[0]
    ncols = cols // owners
    heads = bias_weight_ref.shape[0]
    normed = normalize(pair_ref, gain_ref)[2]
    normed_s[...] = normed.astype(F32)
    copies[3].wait()
    cot_s[...] = cot_ref[...].astype(F32).reshape(rows * cols, channels)
    for a in range(rows):
        bias = nt(bias_weight_ref[...], normed[a * cols : (a + 1) * cols])
        bias_s[pl.ds(a, heads, stride=rows), :] = bias
    pad = jnp.zeros((rows, 256 - 4 * cols), BF16)
    for core in range(2):
        first = 2 * core * rows
        bias = jnp.concatenate([bias_s[first : first + rows], bias_s[first + rows : first + 2 * rows]], axis=1)
        bias = jnp.concatenate([*coarse_fine(bias), pad], axis=1)
        for owner in range(core, owners, 2):
            out_ref[owner, :, 2 * ncols * channels :] = bias
    for owner in range(owners):
        for k in range(ncols):
            column = pl.ds(owner * ncols + k, rows, stride=cols)
            at = k * channels
            out_ref[owner, :, at : at + channels] = normed_s[column, :].astype(BF16)
            at = (ncols + k) * channels
            out_ref[owner, :, at : at + channels] = cot_s[column, :].astype(BF16)


def bias_out_kernel(both_ref, out_ref):
    rows, wide = both_ref.shape
    width = out_ref.shape[2] // PARTS
    parts = both_ref[:, wide - 256 :].astype(F32)
    bias = parts[:, :width] + parts[:, width : 2 * width]
    high = rows // PARTS
    packed = jnp.concatenate([bias[k * high : (k + 1) * high] for k in range(PARTS)], axis=1)
    for c in range(out_ref.shape[0]):
        out_ref[c] = packed


def project_kernel(
    normed_ref, twin_normed_ref, cot_ref, twin_cot_ref, w_ref, wt_ref, w_out_ref,
    upright_ref, lying_ref, gates_ref,
):
    channels = w_ref.shape[-1]
    normed = jnp.concatenate([normed_ref[...], twin_normed_ref[...]], axis=1)
    cot = jnp.concatenate([cot_ref[...], twin_cot_ref[...]], axis=1)
    for m in range(3):
        at = slice(m * channels, (m + 1) * channels)
        upright_ref[0, :, at] = nn(normed, w_ref[m]).astype(BF16)
        lying_ref[0, at, :] = nt(wt_ref[m], normed).astype(BF16)
    gate_t = jax.nn.sigmoid(nt(wt_ref[3], normed))
    d_gated_t = nt(w_out_ref[...], cot)
    d_context_t = (d_gated_t * gate_t).astype(BF16)
    gates_ref[0, :channels, :] = gate_t
    gates_ref[0, channels:, :] = d_gated_t
    lying_ref[0, 3 * channels :, :] = d_context_t
    upright_ref[0, :, 3 * channels : 4 * channels] = turned(d_context_t)
    upright_ref[0, :, 4 * channels : 6 * channels] = normed
    upright_ref[0, :, 6 * channels :] = cot


def inner_specs(columns, rows, channels):
    sizes = ((rows, 8 * channels, BF16), (4 * channels, rows, BF16), (2 * channels, rows, F32))
    specs = [pl.BlockSpec((1, high, wide), lambda j: (j, 0, 0)) for high, wide, _ in sizes]
    shapes = [jax.ShapeDtypeStruct((columns, high, wide), kind) for high, wide, kind in sizes]
    return specs, shapes


def project(both, twin, w, wt, w_out, columns):
    rows = both.shape[0]
    channels = w.shape[-1]
    normed = pl.BlockSpec((rows, channels), lambda j: (0, j))
    cot = pl.BlockSpec((rows, channels), lambda j: (0, columns + j))
    specs, shapes = inner_specs(columns, rows, channels)
    return pl.pallas_call(
        project_kernel,
        grid=(columns,),
        in_specs=[
            normed, normed, cot, cot,
            pl.BlockSpec(w.shape, lambda j: (0, 0, 0)),
            pl.BlockSpec(wt.shape, lambda j: (0, 0, 0)),
            pl.BlockSpec(w_out.shape, lambda j: (0, 0)),
        ],
        out_specs=specs,
        out_shape=shapes,
        compiler_params=pltpu.CompilerParams(vmem_limit_bytes=24 << 20),
        name="project",
    )(both, twin, both, twin, w, wt, w_out)


def attention_kernel(
    valid_ref, got_ref, upright_at, lying_at, gates_at,
    acts_ref, sent_ref, upright_ref, lying_ref, gates_ref, sem, bias_s, total, grads_s, d_scores_s, weights_s, right_s,
):
    step = pl.program_id(0)
    steps = pl.num_programs(0)
    blocks, high, lanes = got_ref.shape
    rows = lying_ref.shape[2]
    channels = lying_ref.shape[1] // 4
    slots = 4
    width = channels // slots
    half = channels // 2
    cols = rows // blocks
    scale = width ** (-0.5)

    sources = (upright_at, lying_at, gates_at)
    targets = (upright_ref, lying_ref, gates_ref)

    def block(m, j):
        return pltpu.make_async_copy(sources[m].at[j], targets[m].at[j], sem.at[m, j])

    @pl.when(step == 0)
    def _():
        for j in range(upright_ref.shape[0]):
            for m in range(3):
                block(m, j).start()
        for k in range(PARTS):
            for h in range(2):
                at = (2 * k + h) * cols
                pieces = [got_ref[c, :, at : at + cols] for c in range(blocks)]
                bias_s[h, k * high : (k + 1) * high, :] = jnp.concatenate(pieces, axis=1) * LOG2E
        total[...] = jnp.zeros_like(total)
        grads_s[...] = jnp.zeros_like(grads_s)

    for m in range(3):
        block(m, step).wait()
    query = upright_ref[step, :, :channels]
    d_context = upright_ref[step, :, 3 * channels : 4 * channels]
    key = upright_ref[step, :, channels : 2 * channels]
    value = upright_ref[step, :, 2 * channels : 3 * channels]
    lane = lax.broadcasted_iota(jnp.int32, (rows, channels), 1)
    sure = rows // 2
    keep = lax.broadcasted_iota(jnp.int32, (rows - sure, rows), 0) + sure < valid_ref[0]
    zero = jnp.zeros((rows, channels), BF16)
    for slot in range(slots):
        mine = (lane >= slot * width) & (lane < (slot + 1) * width)
        here = slice(slot * rows, (slot + 1) * rows)
        part = slice(slot * width, (slot + 1) * width)
        right_s[here, :channels] = jnp.where(mine, query, zero)
        right_s[here, channels:] = jnp.where(mine, d_context, zero)
        scores = nn(key[:, part], lying_ref[step, part]) * (scale * LOG2E) + bias_s[slot % 2]
        masked = jnp.where(keep, scores[sure:], MASKED * LOG2E)
        scores = jnp.concatenate([scores[:sure], masked], axis=0)
        top = jnp.max(scores, axis=0, keepdims=True)
        grown = jnp.exp2(scores - top)
        inverse = 1.0 / jnp.sum(grown, axis=0, keepdims=True)
        probs = grown * inverse
        weights_s[:, here] = probs.astype(BF16)
        d_probs = nn(value[:, part], lying_ref[step, 3 * channels + slot * width : 3 * channels + (slot + 1) * width])
        delta = jnp.sum(grown * d_probs, axis=0, keepdims=True) * inverse
        d_scores = probs * (d_probs - delta)
        total[slot % 2] += d_scores
        d_scores_s[:, here] = d_scores.astype(BF16)
    blocks_t = [
        (nn(lying_ref[step, 2 * channels + s * width : 2 * channels + (s + 1) * width], weights_s[:, s * rows : (s + 1) * rows]),
         nn(lying_ref[step, channels + s * width : channels + (s + 1) * width], d_scores_s[:, s * rows : (s + 1) * rows]))
        for s in range(slots)
    ]
    context_t = jnp.concatenate([one for one, _ in blocks_t], axis=0).astype(BF16).astype(F32)
    d_query_t = (jnp.concatenate([two for _, two in blocks_t], axis=0) * scale).astype(BF16)
    d_key = (nn(d_scores_s[...], right_s[:, :channels]) * scale).astype(BF16)
    d_value = nn(weights_s[...], right_s[:, channels:]).astype(BF16)
    gate_t = gates_ref[step, :channels]
    gated_t = (gate_t * context_t).astype(BF16)
    d_gate_t = (gates_ref[step, channels:] * context_t * gate_t * (1.0 - gate_t)).astype(BF16)
    acts = [turned(gated_t), turned(d_query_t), d_key, d_value, turned(d_gate_t)]
    for m in range(5):
        acts_ref[0, :, m * channels : (m + 1) * channels] = acts[m]
    left = jnp.concatenate([d_query_t, turned(d_key), turned(d_value), d_gate_t], axis=0)
    products = nn(left, upright_ref[step, :, 4 * channels : 6 * channels])
    for m in range(4):
        near = products[m * channels : m * channels + half, :channels]
        far = products[m * channels + half : (m + 1) * channels, channels:]
        grads_s[m * half : (m + 1) * half, :] += near + far
    last = nn(gated_t[:half], upright_ref[step, :, 6 * channels : 7 * channels])
    last = last + nn(gated_t[half:], upright_ref[step, :, 7 * channels :])
    grads_s[4 * half :, :] += last

    @pl.when(step == steps - 1)
    def _():
        for c in range(blocks):
            pieces = [
                total[h, k * high : (k + 1) * high, c * cols : (c + 1) * cols]
                for k in range(PARTS)
                for h in range(2)
            ]
            sent_ref[c, :high, :] = jnp.concatenate(pieces, axis=1).astype(BF16)
        grads = grads_s[...]
        share = grads.shape[0] // blocks
        rest = sent_ref.shape[1] - high
        spare = jnp.zeros((3 * rest - share, channels), F32)
        for c in range(blocks):
            mine = jnp.concatenate([grads[c * share : (c + 1) * share], spare], axis=0)
            pieces = [mine[k * rest : (k + 1) * rest] for k in range(3)]
            sent_ref[c, high:, :] = jnp.concatenate(pieces, axis=1).astype(BF16)


def attend(valid_len, got, inner, columns):
    rows = inner[1].shape[2]
    channels = inner[1].shape[1] // 4
    blocks, high, lanes = got.shape
    return pl.pallas_call(
        attention_kernel,
        grid=(columns,),
        in_specs=[pl.BlockSpec(memory_space=pltpu.SMEM), pl.BlockSpec(memory_space=pltpu.VMEM)]
        + [pl.BlockSpec(memory_space=pl.ANY)] * 3,
        out_specs=[
            pl.BlockSpec((1, rows, 5 * channels), lambda j: (j, 0, 0)),
            pl.BlockSpec((blocks, high + 16, lanes), lambda j: (0, 0, 0)),
        ],
        out_shape=[
            jax.ShapeDtypeStruct((columns, rows, 5 * channels), BF16),
            jax.ShapeDtypeStruct((blocks, high + 16, lanes), BF16),
        ],
        scratch_shapes=[
            *[pltpu.VMEM(one.shape, one.dtype) for one in inner],
            pltpu.SemaphoreType.DMA((3, columns)),
            pltpu.VMEM((2, rows, rows), F32),
            pltpu.VMEM((2, rows, rows), F32),
            pltpu.VMEM((5 * channels // 2, channels), F32),
            pltpu.VMEM((rows, 4 * rows), BF16),
            pltpu.VMEM((rows, 4 * rows), BF16),
            pltpu.VMEM((4 * rows, 2 * channels), BF16),
        ],
        compiler_params=pltpu.CompilerParams(vmem_limit_bytes=24 << 20),
        name="attention",
    )(valid_len, got, *[distant(one) for one in inner])


def merge_kernel(acts_ref, came_ref, w_ref, out_ref):
    column = pl.program_id(0)
    columns = pl.num_programs(0)
    channels = w_ref.shape[-1]
    parts = []
    for m in range(5):
        at = slice(m * channels, (m + 1) * channels)
        parts.append(nn(jnp.concatenate([acts_ref[0, :, at], came_ref[0, :, at]], axis=1), w_ref[m]))
    d_normed = parts[1] + parts[2] + parts[3] + parts[4]
    out_ref[:, pl.ds(pl.multiple_of(column * channels, channels), channels)] = parts[0].astype(BF16)
    second = pl.multiple_of((columns + column) * channels, channels)
    out_ref[:, pl.ds(second, channels)] = d_normed.astype(BF16)


def merge(acts, came, w):
    columns, rows, lanes = acts.shape
    channels = w.shape[-1]
    block = pl.BlockSpec((1, rows, lanes), lambda j: (j, 0, 0))
    return pl.pallas_call(
        merge_kernel,
        grid=(columns,),
        in_specs=[block, block, pl.BlockSpec(w.shape, lambda j: (0, 0, 0))],
        out_specs=pl.BlockSpec((rows, 2 * columns * channels), lambda j: (0, 0)),
        out_shape=jax.ShapeDtypeStruct((rows, 2 * columns * channels + 256), BF16),
        compiler_params=pltpu.CompilerParams(vmem_limit_bytes=24 << 20),
        name="merge",
    )(acts, came, w)


def sum_kernel(got_ref, main_ref, out_ref):
    blocks, high, lanes = got_ref.shape
    owners, rows, wide = out_ref.shape
    part = lanes // PARTS
    total = got_ref[0].astype(F32)
    for c in range(1, blocks):
        total = total + got_ref[c].astype(F32)
    grads = jnp.concatenate([total[part:, k * 128 : (k + 1) * 128] for k in range(3)], axis=0)
    share = 5
    gap = jnp.zeros((rows - 4 * share, 64), F32)
    for owner in range(owners):
        across, down = divmod(owner, part // rows)
        block = total[down * rows : (down + 1) * rows, across * part : (across + 1) * part]
        coarse = block.astype(BF16).astype(F32)
        mine = grads[owner // 2 * share : (owner // 2 + 1) * share]
        near = mine.astype(BF16).astype(F32)
        far = mine - near
        stack = jnp.concatenate([near[:, :64], near[:, 64:], far[:, :64], far[:, 64:], gap], axis=0)
        out_ref[owner] = jnp.concatenate([coarse, block - coarse, stack], axis=1).astype(BF16)


def add_sums(got, main, n_row):
    rows, wide = main.shape
    blocked = main.reshape(n_row, rows // n_row, wide)
    spec = pl.BlockSpec((n_row, rows // n_row, 256), lambda i: (0, 0, wide // 256 - 1))
    return pl.pallas_call(
        sum_kernel,
        grid=(1,),
        in_specs=[pl.BlockSpec(memory_space=pltpu.VMEM), pl.BlockSpec(memory_space=pl.ANY)],
        out_specs=spec,
        out_shape=jax.ShapeDtypeStruct(blocked.shape, BF16),
        input_output_aliases={1: 0},
        compiler_params=pltpu.CompilerParams(vmem_limit_bytes=24 << 20),
        name="sum",
    )(got, blocked)


def finish_kernel(
    core_ref, got_ref, pair_at, gain_at, bias_weight_at,
    d_normed_ref, last_ref, pair_ref, gain_ref, bias_weight_ref, sem, d_bias_s,
):
    copies = fetched((pair_at, gain_at, bias_weight_at), (pair_ref, gain_ref, bias_weight_ref), sem)
    owners, rows, wide = got_ref.shape
    cols, channels = pair_ref.shape[1:]
    heads = bias_weight_ref.shape[0]
    ncols = cols // owners
    main = 2 * ncols * channels
    for owner in range(owners):
        for k in range(ncols):
            column = pl.ds(owner * ncols + k, rows, stride=cols)
            at = (ncols + k) * channels
            d_normed_ref[column, :] = got_ref[owner, :, at : at + channels].astype(F32)
    sums = [jnp.zeros((rows, 256), F32), jnp.zeros((rows, 256), F32)]
    for owner in range(owners):
        sums[owner % 2] = sums[owner % 2] + got_ref[owner, :, main:].astype(F32)
    for core in range(2):
        block = sums[core][:, : 2 * cols] + sums[core][:, 2 * cols : 4 * cols]
        block = block.astype(BF16).astype(F32)
        for h in range(2):
            at = pl.ds(2 * core + h, rows, stride=heads)
            d_bias_s[at, :] = block[:, h * cols : (h + 1) * cols]
    grads = jnp.where(core_ref[0] == 0, sums[0], sums[1])[:, 4 * cols :]
    grads = jnp.concatenate([grads[:5] + grads[10:15], grads[5:10] + grads[15:20]], axis=1)
    for copy in copies:
        copy.wait()
    xhat, inverse, normed = normalize(pair_ref, gain_ref)
    d_bias_t = jnp.transpose(d_bias_s[...]).astype(BF16)
    row = lax.broadcasted_iota(jnp.int32, (rows * heads, channels), 0)
    repeated = jnp.concatenate([bias_weight_ref[...].astype(F32)] * rows, axis=0).astype(BF16)
    weight_part = jnp.zeros((heads, channels), F32)
    for a in range(rows):
        here = slice(a * cols, (a + 1) * cols)
        mine = (row >= a * heads) & (row < (a + 1) * heads)
        weight = jnp.where(mine, repeated, jnp.zeros((rows * heads, channels), BF16))
        d_normed_ref[here, :] += nn(d_bias_t, weight)
        d_bias_a = d_bias_s[a * heads : (a + 1) * heads, :].astype(BF16)
        weight_part = weight_part + nn(d_bias_a, normed[here])
    gain_part = jnp.sum(d_normed_ref[...] * xhat, axis=0, keepdims=True)
    small = jnp.concatenate([weight_part, gain_part], axis=0)
    for t in range(5):
        pair = jnp.concatenate([grads[t : t + 1], small[t : t + 1]], axis=0)
        last_ref[:, t] = jnp.broadcast_to(pair[None], (last_ref.shape[0], 2, channels))


def output_kernel(got_ref, d_normed_ref, pair_ref, gain_ref, attended_ref, gradient_ref, moved_s):
    owners, rows, wide = got_ref.shape
    cols, channels = pair_ref.shape[1:]
    ncols = cols // owners
    xhat, inverse, normed = normalize(pair_ref, gain_ref)
    for owner in range(owners):
        for k in range(ncols):
            column = pl.ds(owner * ncols + k, rows, stride=cols)
            moved_s[column, :] = got_ref[owner, :, k * channels : (k + 1) * channels].astype(F32)
    attended_ref[...] = moved_s[...].astype(BF16).reshape(attended_ref.shape)
    scaled = d_normed_ref[...] * gain_ref[...]
    gradient = inverse * (
        scaled
        - jnp.mean(scaled, axis=-1, keepdims=True)
        - xhat * jnp.mean(scaled * xhat, axis=-1, keepdims=True)
    )
    gradient_ref[...] = gradient.reshape(gradient_ref.shape)


def gather_kernel(n_row, n_col, got_ref, grad_ref, weight_ref, gain_ref, halves_s):
    channels = got_ref.shape[-1]
    share = got_ref.shape[1]
    half = channels // 2
    for r in range(n_row):
        for c in range(n_col):
            at = (c * (n_row // 2) + r // 2) * share
            halves_s[r % 2, at : at + share, :] = got_ref[r * n_col + c, :, 0, :]
    small = jnp.sum(got_ref[:, :, 1, :], axis=0)
    heads = weight_ref.shape[0]
    weight_ref[...] = small[:heads]
    gain_ref[...] = small[heads : heads + 1]
    for m in range(5):
        both = [halves_s[core, m * half : (m + 1) * half, :] for core in range(2)]
        both = jnp.concatenate(both, axis=0)
        grad_ref[m] = jnp.transpose(both) if m < 4 else both


def shards(pair, gain, projections, bias_weight, valid_len, out_cotangent):
    n_row = lax.axis_size(ROW)
    n_col = lax.axis_size(COL)
    n_all = n_row * n_col
    tile_rows, tile_cols, channels = pair.shape
    rows = tile_rows * n_row
    heads = bias_weight.shape[1]
    ncols = tile_cols // n_row
    tile = tile_rows * tile_cols
    main = 2 * ncols * channels
    half = channels // 2
    shape = jax.ShapeDtypeStruct
    gain_row = gain[None, :]
    weight_t = bias_weight.T
    swap = [(0, 1), (1, 0)]
    core = lax.axis_index(CORE).astype(jnp.int32)
    halves = projections[:4].reshape(4, channels, 2, half)
    rows_out = projections[4].reshape(2, half, channels)
    own = lax.dynamic_index_in_dim(halves, core, 2, keepdims=False)
    other = lax.dynamic_index_in_dim(halves, 1 - core, 2, keepdims=False)
    own_out = lax.dynamic_index_in_dim(rows_out, core, 0, keepdims=False)
    other_out = lax.dynamic_index_in_dim(rows_out, 1 - core, 0, keepdims=False)
    zero = jnp.zeros_like(own)
    w = jnp.concatenate(
        [jnp.concatenate([own, zero], axis=2), jnp.concatenate([zero, own], axis=2)], axis=1
    )
    zero_out = jnp.zeros_like(own_out)
    w_out = jnp.concatenate(
        [jnp.concatenate([own_out, zero_out], axis=1), jnp.concatenate([zero_out, own_out], axis=1)],
        axis=0,
    )
    mine = jnp.concatenate([own_out[None], jnp.swapaxes(own, 1, 2)], axis=0)
    theirs = jnp.concatenate([other_out[None], jnp.swapaxes(other, 1, 2)], axis=0)
    gap = jnp.zeros((5, channels, channels), BF16)
    w_merge = jnp.concatenate([mine, gap, theirs], axis=1)

    anywhere = pl.BlockSpec(memory_space=pl.ANY)
    inputs = [pltpu.VMEM(pair.shape, BF16), pltpu.VMEM(gain_row.shape, F32), pltpu.VMEM(weight_t.shape, BF16)]
    packed = pl.pallas_call(
        pack_kernel,
        in_specs=[anywhere] * 4,
        out_shape=shape((n_row, tile_rows, main + 256), BF16),
        scratch_shapes=[
            inputs[0], *inputs, pltpu.SemaphoreType.DMA((4,)),
            pltpu.VMEM((tile, channels), F32), pltpu.VMEM((tile, channels), F32),
            pltpu.VMEM((heads * tile_rows, tile_cols), F32),
        ],
        compiler_params=pltpu.CompilerParams(vmem_limit_bytes=24 << 20),
        name="pack",
    )(distant(pair), distant(out_cotangent), distant(gain_row), distant(weight_t))
    both = exchange(packed, ROW).reshape(rows, main + 256)
    high = rows // PARTS
    lanes = PARTS * 2 * tile_cols
    smem = pl.BlockSpec(memory_space=pltpu.SMEM)
    vmem = pl.BlockSpec(memory_space=pltpu.VMEM)
    spread = pl.pallas_call(
        bias_out_kernel,
        in_specs=[vmem],
        out_shape=shape((n_col, high, lanes), F32),
        name="bias_out",
    )(resident(both))
    got = pltpu.with_memory_space_constraint(exchange(spread, COL), pltpu.VMEM)
    twin = lax.ppermute(both, CORE, swap)
    inner = project(both, twin, w, jnp.swapaxes(w, 1, 2), w_out, ncols)
    acts, sent = attend(valid_len, got, inner, ncols)
    summed = pltpu.with_memory_space_constraint(exchange(sent, COL), pltpu.VMEM)
    out = merge(acts, lax.ppermute(acts, CORE, swap), w_merge)
    back = pltpu.with_memory_space_constraint(exchange(add_sums(summed, out, n_row), ROW), pltpu.VMEM)
    d_normed, last = pl.pallas_call(
        finish_kernel,
        in_specs=[smem, vmem] + [anywhere] * 3,
        out_shape=[shape((tile, channels), F32), shape((n_all, 5, 2, channels), F32)],
        scratch_shapes=[*inputs, pltpu.SemaphoreType.DMA((3,)), pltpu.VMEM((heads * tile_rows, tile_cols), F32)],
        compiler_params=pltpu.CompilerParams(vmem_limit_bytes=24 << 20),
        name="finish",
    )(core[None], back, pair, gain_row, weight_t)
    everyone = pltpu.with_memory_space_constraint(exchange(last, ALL), pltpu.VMEM)
    attended, pair_gradient = pl.pallas_call(
        output_kernel,
        in_specs=[vmem] * 4,
        out_shape=[shape(pair.shape, BF16), shape(pair.shape, F32)],
        scratch_shapes=[pltpu.VMEM((tile, channels), F32)],
        compiler_params=pltpu.CompilerParams(vmem_limit_bytes=24 << 20),
        name="output",
    )(back, d_normed, pair, gain_row)
    projection_grad, bias_weight_grad, gain_gradient = pl.pallas_call(
        functools.partial(gather_kernel, n_row, n_col),
        in_specs=[vmem],
        out_shape=[shape(projections.shape, F32), shape((heads, channels), F32), shape((1, channels), F32)],
        scratch_shapes=[pltpu.VMEM((2, 5 * half, channels), F32)],
        name="gather",
    )(everyone)
    return (attended, pair_gradient, projection_grad, bias_weight_grad.T, gain_gradient[0])


def solution(mesh):
    torus = Mesh(mesh.devices.reshape(2, 4, 2, 2, 4), ALL)
    in_specs = (P(ROW, COL, None), P(), P(), P(), P(), P(ROW, COL, None))
    out_specs = (P(ROW, COL, None), P(ROW, COL, None), P(), P(), P())
    return jax.shard_map(
        shards, mesh=torus, in_specs=in_specs, out_specs=out_specs, check_vma=False
    )
```

```python
import functools

import jax
import jax.numpy as jnp
from jax import lax
from jax.experimental import pallas as pl
from jax.experimental.pallas import tpu as pltpu
from jax.sharding import Mesh
from jax.sharding import PartitionSpec as P

ROW = ("row_0", "row_1", "row_2")
COL = ("col_0", "col_1")
ALL = ROW + COL
CORE = "row_2"
EPS = 1e-05
MASKED = -1000000000.0
LOG2E = 1.4426950408889634
PARTS = 4
F32 = jnp.float32
BF16 = jnp.bfloat16


def nn(left, right):
    return lax.dot_general(left, right, (((1,), (0,)), ((), ())), preferred_element_type=F32)


def nt(left, right):
    return lax.dot_general(left, right, (((1,), (1,)), ((), ())), preferred_element_type=F32)


def turned(value):
    return jnp.transpose(value.astype(F32)).astype(value.dtype)


def exchange(value, axes):
    return lax.all_to_all(value, axes, split_axis=0, concat_axis=0, tiled=True)


def call(kernel, out_shape, scratch, name, *operands):
    return pl.pallas_call(
        kernel,
        out_shape=out_shape,
        scratch_shapes=scratch,
        compiler_params=pltpu.CompilerParams(vmem_limit_bytes=24 << 20),
        name=name,
    )(*operands)


def resident(value):
    return pltpu.with_memory_space_constraint(value, pltpu.VMEM)


def distant(value):
    return pltpu.with_memory_space_constraint(value, pltpu.HBM)


def fetched(sources, targets, sem):
    copies = [pltpu.make_async_copy(a, b, sem.at[k]) for k, (a, b) in enumerate(zip(sources, targets))]
    for copy in copies:
        copy.start()
    return copies


def coarse_fine(value):
    coarse = value.astype(BF16)
    return coarse, (value - coarse.astype(F32)).astype(BF16)


def normalize(pair_ref, gain_ref):
    rows, cols, channels = pair_ref.shape
    pair = pair_ref[...].astype(F32).reshape(rows * cols, channels)
    average = jnp.mean(pair, axis=-1, keepdims=True)
    var = jnp.mean((pair - average) ** 2, axis=-1, keepdims=True)
    inverse = lax.rsqrt(var + EPS)
    xhat = (pair - average) * inverse
    return xhat, inverse, (xhat * gain_ref[...]).astype(BF16)


def pack_kernel(
    pair_at, cot_at, gain_at, bias_weight_at,
    out_ref, pair_ref, cot_ref, gain_ref, bias_weight_ref, sem, normed_s, cot_s, bias_s,
):
    copies = fetched(
        (pair_at, gain_at, bias_weight_at, cot_at), (pair_ref, gain_ref, bias_weight_ref, cot_ref), sem
    )
    for copy in copies[:3]:
        copy.wait()
    rows, cols, channels = pair_ref.shape
    owners = out_ref.shape[0]
    ncols = cols // owners
    heads = bias_weight_ref.shape[0]
    normed = normalize(pair_ref, gain_ref)[2]
    normed_s[...] = normed.astype(F32)
    copies[3].wait()
    cot_s[...] = cot_ref[...].astype(F32).reshape(rows * cols, channels)
    for a in range(rows):
        bias = nt(bias_weight_ref[...], normed[a * cols : (a + 1) * cols])
        bias_s[pl.ds(a, heads, stride=rows), :] = bias
    pad = jnp.zeros((rows, 256 - 4 * cols), BF16)
    for core in range(2):
        first = 2 * core * rows
        bias = jnp.concatenate([bias_s[first : first + rows], bias_s[first + rows : first + 2 * rows]], axis=1)
        bias = jnp.concatenate([*coarse_fine(bias), pad], axis=1)
        for owner in range(core, owners, 2):
            out_ref[owner, :, 2 * ncols * channels :] = bias
    for owner in range(owners):
        for k in range(ncols):
            column = pl.ds(owner * ncols + k, rows, stride=cols)
            at = k * channels
            out_ref[owner, :, at : at + channels] = normed_s[column, :].astype(BF16)
            at = (ncols + k) * channels
            out_ref[owner, :, at : at + channels] = cot_s[column, :].astype(BF16)


def bias_out_kernel(both_ref, out_ref):
    rows, wide = both_ref.shape
    width = out_ref.shape[2] // PARTS
    parts = both_ref[:, wide - 256 :].astype(F32)
    bias = parts[:, :width] + parts[:, width : 2 * width]
    high = rows // PARTS
    packed = jnp.concatenate([bias[k * high : (k + 1) * high] for k in range(PARTS)], axis=1)
    for c in range(out_ref.shape[0]):
        out_ref[c] = packed


def project_kernel(
    normed_ref, twin_normed_ref, cot_ref, twin_cot_ref, w_ref, wt_ref, w_out_ref,
    upright_ref, lying_ref, gates_ref,
):
    channels = w_ref.shape[-1]
    normed = jnp.concatenate([normed_ref[...], twin_normed_ref[...]], axis=1)
    cot = jnp.concatenate([cot_ref[...], twin_cot_ref[...]], axis=1)
    for m in range(3):
        at = slice(m * channels, (m + 1) * channels)
        upright_ref[0, :, at] = nn(normed, w_ref[m]).astype(BF16)
        lying_ref[0, at, :] = nt(wt_ref[m], normed).astype(BF16)
    gate_t = jax.nn.sigmoid(nt(wt_ref[3], normed))
    d_gated_t = nt(w_out_ref[...], cot)
    d_context_t = (d_gated_t * gate_t).astype(BF16)
    gates_ref[0, :channels, :] = gate_t
    gates_ref[0, channels:, :] = d_gated_t
    lying_ref[0, 3 * channels :, :] = d_context_t
    upright_ref[0, :, 3 * channels : 4 * channels] = turned(d_context_t)
    upright_ref[0, :, 4 * channels : 6 * channels] = normed
    upright_ref[0, :, 6 * channels :] = cot


def inner_specs(columns, rows, channels):
    sizes = ((rows, 8 * channels, BF16), (4 * channels, rows, BF16), (2 * channels, rows, F32))
    specs = [pl.BlockSpec((1, high, wide), lambda j: (j, 0, 0)) for high, wide, _ in sizes]
    shapes = [jax.ShapeDtypeStruct((columns, high, wide), kind) for high, wide, kind in sizes]
    return specs, shapes


def project(both, twin, w, wt, w_out, columns):
    rows = both.shape[0]
    channels = w.shape[-1]
    normed = pl.BlockSpec((rows, channels), lambda j: (0, j))
    cot = pl.BlockSpec((rows, channels), lambda j: (0, columns + j))
    specs, shapes = inner_specs(columns, rows, channels)
    return pl.pallas_call(
        project_kernel,
        grid=(columns,),
        in_specs=[
            normed, normed, cot, cot,
            pl.BlockSpec(w.shape, lambda j: (0, 0, 0)),
            pl.BlockSpec(wt.shape, lambda j: (0, 0, 0)),
            pl.BlockSpec(w_out.shape, lambda j: (0, 0)),
        ],
        out_specs=specs,
        out_shape=shapes,
        compiler_params=pltpu.CompilerParams(vmem_limit_bytes=24 << 20),
        name="project",
    )(both, twin, both, twin, w, wt, w_out)


def attention_kernel(
    valid_ref, got_ref, upright_at, lying_at, gates_at,
    acts_ref, sent_ref, upright_ref, lying_ref, gates_ref, sem, bias_s, total, grads_s, d_scores_s, weights_s, right_s,
):
    step = pl.program_id(0)
    steps = pl.num_programs(0)
    blocks, high, lanes = got_ref.shape
    rows = lying_ref.shape[2]
    channels = lying_ref.shape[1] // 4
    slots = 4
    width = channels // slots
    half = channels // 2
    cols = rows // blocks
    scale = width ** (-0.5)

    sources = (upright_at, lying_at, gates_at)
    targets = (upright_ref, lying_ref, gates_ref)

    def block(m, j):
        return pltpu.make_async_copy(sources[m].at[j], targets[m].at[j], sem.at[m, j])

    @pl.when(step == 0)
    def _():
        for j in range(upright_ref.shape[0]):
            for m in range(3):
                block(m, j).start()
        for k in range(PARTS):
            for h in range(2):
                at = (2 * k + h) * cols
                pieces = [got_ref[c, :, at : at + cols] for c in range(blocks)]
                bias_s[h, k * high : (k + 1) * high, :] = jnp.concatenate(pieces, axis=1) * LOG2E
        total[...] = jnp.zeros_like(total)
        grads_s[...] = jnp.zeros_like(grads_s)

    for m in range(3):
        block(m, step).wait()
    def attend_keys(limit):
        query = upright_ref[step, :, :channels]
        d_context = upright_ref[step, :, 3 * channels : 4 * channels]
        key = upright_ref[step, :limit, channels : 2 * channels]
        value = upright_ref[step, :limit, 2 * channels : 3 * channels]
        lane = lax.broadcasted_iota(jnp.int32, (rows, channels), 1)
        sure = rows // 2
        keep = lax.broadcasted_iota(jnp.int32, (limit - sure, rows), 0) + sure < valid_ref[0]
        zero = jnp.zeros((rows, channels), BF16)
        for slot in range(slots):
            mine = (lane >= slot * width) & (lane < (slot + 1) * width)
            here = slice(slot * rows, (slot + 1) * rows)
            part = slice(slot * width, (slot + 1) * width)
            right_s[here, :channels] = jnp.where(mine, query, zero)
            right_s[here, channels:] = jnp.where(mine, d_context, zero)
            scores = nn(key[:, part], lying_ref[step, part]) * (scale * LOG2E) + bias_s[slot % 2, :limit]
            masked = jnp.where(keep, scores[sure:], MASKED * LOG2E)
            scores = jnp.concatenate([scores[:sure], masked], axis=0)
            top = jnp.max(scores, axis=0, keepdims=True)
            grown = jnp.exp2(scores - top)
            inverse = 1.0 / jnp.sum(grown, axis=0, keepdims=True)
            probs = grown * inverse
            weights_s[:limit, here] = probs.astype(BF16)
            d_probs = nn(value[:, part], lying_ref[step, 3 * channels + slot * width : 3 * channels + (slot + 1) * width])
            delta = jnp.sum(grown * d_probs, axis=0, keepdims=True) * inverse
            d_scores = probs * (d_probs - delta)
            total[slot % 2, :limit] += d_scores
            d_scores_s[:limit, here] = d_scores.astype(BF16)
        blocks_t = [
            (nn(lying_ref[step, 2 * channels + s * width : 2 * channels + (s + 1) * width, :limit], weights_s[:limit, s * rows : (s + 1) * rows]),
             nn(lying_ref[step, channels + s * width : channels + (s + 1) * width, :limit], d_scores_s[:limit, s * rows : (s + 1) * rows]))
            for s in range(slots)
        ]
        context_t = jnp.concatenate([one for one, _ in blocks_t], axis=0).astype(BF16).astype(F32)
        d_query_t = (jnp.concatenate([two for _, two in blocks_t], axis=0) * scale).astype(BF16)
        d_key = (nn(d_scores_s[:limit], right_s[:, :channels]) * scale).astype(BF16)
        d_value = nn(weights_s[:limit], right_s[:, channels:]).astype(BF16)
        if limit < rows:
            rest = jnp.zeros((rows - limit, channels), BF16)
            d_key = jnp.concatenate([d_key, rest], axis=0)
            d_value = jnp.concatenate([d_value, rest], axis=0)
        gate_t = gates_ref[step, :channels]
        gated_t = (gate_t * context_t).astype(BF16)
        d_gate_t = (gates_ref[step, channels:] * context_t * gate_t * (1.0 - gate_t)).astype(BF16)
        acts = [turned(gated_t), turned(d_query_t), d_key, d_value, turned(d_gate_t)]
        for m in range(5):
            acts_ref[0, :, m * channels : (m + 1) * channels] = acts[m]
        left = jnp.concatenate([d_query_t, turned(d_key), turned(d_value), d_gate_t], axis=0)
        products = nn(left, upright_ref[step, :, 4 * channels : 6 * channels])
        for m in range(4):
            near = products[m * channels : m * channels + half, :channels]
            far = products[m * channels + half : (m + 1) * channels, channels:]
            grads_s[m * half : (m + 1) * half, :] += near + far
        last = nn(gated_t[:half], upright_ref[step, :, 6 * channels : 7 * channels])
        last = last + nn(gated_t[half:], upright_ref[step, :, 7 * channels :])
        grads_s[4 * half :, :] += last

    below = 0
    for limit in (2 * rows // 3, 5 * rows // 6, rows):
        fits = (valid_ref[0] > below) & (valid_ref[0] <= limit)
        pl.when(fits)(functools.partial(attend_keys, limit))
        below = limit

    @pl.when(step == steps - 1)
    def _():
        for c in range(blocks):
            pieces = [
                total[h, k * high : (k + 1) * high, c * cols : (c + 1) * cols]
                for k in range(PARTS)
                for h in range(2)
            ]
            sent_ref[c, :high, :] = jnp.concatenate(pieces, axis=1).astype(BF16)
        grads = grads_s[...]
        share = grads.shape[0] // blocks
        rest = sent_ref.shape[1] - high
        spare = jnp.zeros((3 * rest - share, channels), F32)
        for c in range(blocks):
            mine = jnp.concatenate([grads[c * share : (c + 1) * share], spare], axis=0)
            pieces = [mine[k * rest : (k + 1) * rest] for k in range(3)]
            sent_ref[c, high:, :] = jnp.concatenate(pieces, axis=1).astype(BF16)


def attend(valid_len, got, inner, columns):
    rows = inner[1].shape[2]
    channels = inner[1].shape[1] // 4
    blocks, high, lanes = got.shape
    return pl.pallas_call(
        attention_kernel,
        grid=(columns,),
        in_specs=[pl.BlockSpec(memory_space=pltpu.SMEM), pl.BlockSpec(memory_space=pltpu.VMEM)]
        + [pl.BlockSpec(memory_space=pl.ANY)] * 3,
        out_specs=[
            pl.BlockSpec((1, rows, 5 * channels), lambda j: (j, 0, 0)),
            pl.BlockSpec((blocks, high + 16, lanes), lambda j: (0, 0, 0)),
        ],
        out_shape=[
            jax.ShapeDtypeStruct((columns, rows, 5 * channels), BF16),
            jax.ShapeDtypeStruct((blocks, high + 16, lanes), BF16),
        ],
        scratch_shapes=[
            *[pltpu.VMEM(one.shape, one.dtype) for one in inner],
            pltpu.SemaphoreType.DMA((3, columns)),
            pltpu.VMEM((2, rows, rows), F32),
            pltpu.VMEM((2, rows, rows), F32),
            pltpu.VMEM((5 * channels // 2, channels), F32),
            pltpu.VMEM((rows, 4 * rows), BF16),
            pltpu.VMEM((rows, 4 * rows), BF16),
            pltpu.VMEM((4 * rows, 2 * channels), BF16),
        ],
        compiler_params=pltpu.CompilerParams(vmem_limit_bytes=24 << 20),
        name="attention",
    )(valid_len, got, *[distant(one) for one in inner])


def merge_kernel(acts_ref, came_ref, w_ref, out_ref):
    column = pl.program_id(0)
    columns = pl.num_programs(0)
    channels = w_ref.shape[-1]
    parts = []
    for m in range(5):
        at = slice(m * channels, (m + 1) * channels)
        parts.append(nn(jnp.concatenate([acts_ref[0, :, at], came_ref[0, :, at]], axis=1), w_ref[m]))
    d_normed = parts[1] + parts[2] + parts[3] + parts[4]
    out_ref[:, pl.ds(pl.multiple_of(column * channels, channels), channels)] = parts[0].astype(BF16)
    second = pl.multiple_of((columns + column) * channels, channels)
    out_ref[:, pl.ds(second, channels)] = d_normed.astype(BF16)


def merge(acts, came, w):
    columns, rows, lanes = acts.shape
    channels = w.shape[-1]
    block = pl.BlockSpec((1, rows, lanes), lambda j: (j, 0, 0))
    return pl.pallas_call(
        merge_kernel,
        grid=(columns,),
        in_specs=[block, block, pl.BlockSpec(w.shape, lambda j: (0, 0, 0))],
        out_specs=pl.BlockSpec((rows, 2 * columns * channels), lambda j: (0, 0)),
        out_shape=jax.ShapeDtypeStruct((rows, 2 * columns * channels + 256), BF16),
        compiler_params=pltpu.CompilerParams(vmem_limit_bytes=24 << 20),
        name="merge",
    )(acts, came, w)


def sum_kernel(got_ref, main_ref, out_ref):
    blocks, high, lanes = got_ref.shape
    owners, rows, wide = out_ref.shape
    part = lanes // PARTS
    total = got_ref[0].astype(F32)
    for c in range(1, blocks):
        total = total + got_ref[c].astype(F32)
    grads = jnp.concatenate([total[part:, k * 128 : (k + 1) * 128] for k in range(3)], axis=0)
    share = 5
    gap = jnp.zeros((rows - 4 * share, 64), F32)
    for owner in range(owners):
        across, down = divmod(owner, part // rows)
        block = total[down * rows : (down + 1) * rows, across * part : (across + 1) * part]
        coarse = block.astype(BF16).astype(F32)
        mine = grads[owner // 2 * share : (owner // 2 + 1) * share]
        near = mine.astype(BF16).astype(F32)
        far = mine - near
        stack = jnp.concatenate([near[:, :64], near[:, 64:], far[:, :64], far[:, 64:], gap], axis=0)
        out_ref[owner] = jnp.concatenate([coarse, block - coarse, stack], axis=1).astype(BF16)


def add_sums(got, main, n_row):
    rows, wide = main.shape
    blocked = main.reshape(n_row, rows // n_row, wide)
    spec = pl.BlockSpec((n_row, rows // n_row, 256), lambda i: (0, 0, wide // 256 - 1))
    return pl.pallas_call(
        sum_kernel,
        grid=(1,),
        in_specs=[pl.BlockSpec(memory_space=pltpu.VMEM), pl.BlockSpec(memory_space=pl.ANY)],
        out_specs=spec,
        out_shape=jax.ShapeDtypeStruct(blocked.shape, BF16),
        input_output_aliases={1: 0},
        compiler_params=pltpu.CompilerParams(vmem_limit_bytes=24 << 20),
        name="sum",
    )(got, blocked)


def finish_kernel(
    core_ref, got_ref, pair_at, gain_at, bias_weight_at,
    d_normed_ref, last_ref, pair_ref, gain_ref, bias_weight_ref, sem, d_bias_s,
):
    copies = fetched((pair_at, gain_at, bias_weight_at), (pair_ref, gain_ref, bias_weight_ref), sem)
    owners, rows, wide = got_ref.shape
    cols, channels = pair_ref.shape[1:]
    heads = bias_weight_ref.shape[0]
    ncols = cols // owners
    main = 2 * ncols * channels
    for owner in range(owners):
        for k in range(ncols):
            column = pl.ds(owner * ncols + k, rows, stride=cols)
            at = (ncols + k) * channels
            d_normed_ref[column, :] = got_ref[owner, :, at : at + channels].astype(F32)
    sums = [jnp.zeros((rows, 256), F32), jnp.zeros((rows, 256), F32)]
    for owner in range(owners):
        sums[owner % 2] = sums[owner % 2] + got_ref[owner, :, main:].astype(F32)
    for core in range(2):
        block = sums[core][:, : 2 * cols] + sums[core][:, 2 * cols : 4 * cols]
        block = block.astype(BF16).astype(F32)
        for h in range(2):
            at = pl.ds(2 * core + h, rows, stride=heads)
            d_bias_s[at, :] = block[:, h * cols : (h + 1) * cols]
    grads = jnp.where(core_ref[0] == 0, sums[0], sums[1])[:, 4 * cols :]
    grads = jnp.concatenate([grads[:5] + grads[10:15], grads[5:10] + grads[15:20]], axis=1)
    for copy in copies:
        copy.wait()
    xhat, inverse, normed = normalize(pair_ref, gain_ref)
    d_bias_t = jnp.transpose(d_bias_s[...]).astype(BF16)
    row = lax.broadcasted_iota(jnp.int32, (rows * heads, channels), 0)
    repeated = jnp.concatenate([bias_weight_ref[...].astype(F32)] * rows, axis=0).astype(BF16)
    weight_part = jnp.zeros((heads, channels), F32)
    for a in range(rows):
        here = slice(a * cols, (a + 1) * cols)
        mine = (row >= a * heads) & (row < (a + 1) * heads)
        weight = jnp.where(mine, repeated, jnp.zeros((rows * heads, channels), BF16))
        d_normed_ref[here, :] += nn(d_bias_t, weight)
        d_bias_a = d_bias_s[a * heads : (a + 1) * heads, :].astype(BF16)
        weight_part = weight_part + nn(d_bias_a, normed[here])
    gain_part = jnp.sum(d_normed_ref[...] * xhat, axis=0, keepdims=True)
    small = jnp.concatenate([weight_part, gain_part], axis=0)
    for t in range(5):
        pair = jnp.concatenate([grads[t : t + 1], small[t : t + 1]], axis=0)
        last_ref[:, t] = jnp.broadcast_to(pair[None], (last_ref.shape[0], 2, channels))


def output_kernel(got_ref, d_normed_ref, pair_ref, gain_ref, attended_ref, gradient_ref, moved_s):
    owners, rows, wide = got_ref.shape
    cols, channels = pair_ref.shape[1:]
    ncols = cols // owners
    xhat, inverse, normed = normalize(pair_ref, gain_ref)
    for owner in range(owners):
        for k in range(ncols):
            column = pl.ds(owner * ncols + k, rows, stride=cols)
            moved_s[column, :] = got_ref[owner, :, k * channels : (k + 1) * channels].astype(F32)
    attended_ref[...] = moved_s[...].astype(BF16).reshape(attended_ref.shape)
    scaled = d_normed_ref[...] * gain_ref[...]
    gradient = inverse * (
        scaled
        - jnp.mean(scaled, axis=-1, keepdims=True)
        - xhat * jnp.mean(scaled * xhat, axis=-1, keepdims=True)
    )
    gradient_ref[...] = gradient.reshape(gradient_ref.shape)


def gather_kernel(n_row, n_col, got_ref, grad_ref, weight_ref, gain_ref, halves_s):
    channels = got_ref.shape[-1]
    share = got_ref.shape[1]
    half = channels // 2
    for r in range(n_row):
        for c in range(n_col):
            at = (c * (n_row // 2) + r // 2) * share
            halves_s[r % 2, at : at + share, :] = got_ref[r * n_col + c, :, 0, :]
    small = jnp.sum(got_ref[:, :, 1, :], axis=0)
    heads = weight_ref.shape[0]
    weight_ref[...] = small[:heads]
    gain_ref[...] = small[heads : heads + 1]
    for m in range(5):
        both = [halves_s[core, m * half : (m + 1) * half, :] for core in range(2)]
        both = jnp.concatenate(both, axis=0)
        grad_ref[m] = jnp.transpose(both) if m < 4 else both


def shards(pair, gain, projections, bias_weight, valid_len, out_cotangent):
    n_row = lax.axis_size(ROW)
    n_col = lax.axis_size(COL)
    n_all = n_row * n_col
    tile_rows, tile_cols, channels = pair.shape
    rows = tile_rows * n_row
    heads = bias_weight.shape[1]
    ncols = tile_cols // n_row
    tile = tile_rows * tile_cols
    main = 2 * ncols * channels
    half = channels // 2
    shape = jax.ShapeDtypeStruct
    gain_row = gain[None, :]
    weight_t = bias_weight.T
    swap = [(0, 1), (1, 0)]
    core = lax.axis_index(CORE).astype(jnp.int32)
    halves = projections[:4].reshape(4, channels, 2, half)
    rows_out = projections[4].reshape(2, half, channels)
    own = lax.dynamic_index_in_dim(halves, core, 2, keepdims=False)
    other = lax.dynamic_index_in_dim(halves, 1 - core, 2, keepdims=False)
    own_out = lax.dynamic_index_in_dim(rows_out, core, 0, keepdims=False)
    other_out = lax.dynamic_index_in_dim(rows_out, 1 - core, 0, keepdims=False)
    zero = jnp.zeros_like(own)
    w = jnp.concatenate(
        [jnp.concatenate([own, zero], axis=2), jnp.concatenate([zero, own], axis=2)], axis=1
    )
    zero_out = jnp.zeros_like(own_out)
    w_out = jnp.concatenate(
        [jnp.concatenate([own_out, zero_out], axis=1), jnp.concatenate([zero_out, own_out], axis=1)],
        axis=0,
    )
    mine = jnp.concatenate([own_out[None], jnp.swapaxes(own, 1, 2)], axis=0)
    theirs = jnp.concatenate([other_out[None], jnp.swapaxes(other, 1, 2)], axis=0)
    gap = jnp.zeros((5, channels, channels), BF16)
    w_merge = jnp.concatenate([mine, gap, theirs], axis=1)

    anywhere = pl.BlockSpec(memory_space=pl.ANY)
    inputs = [pltpu.VMEM(pair.shape, BF16), pltpu.VMEM(gain_row.shape, F32), pltpu.VMEM(weight_t.shape, BF16)]
    packed = pl.pallas_call(
        pack_kernel,
        in_specs=[anywhere] * 4,
        out_shape=shape((n_row, tile_rows, main + 256), BF16),
        scratch_shapes=[
            inputs[0], *inputs, pltpu.SemaphoreType.DMA((4,)),
            pltpu.VMEM((tile, channels), F32), pltpu.VMEM((tile, channels), F32),
            pltpu.VMEM((heads * tile_rows, tile_cols), F32),
        ],
        compiler_params=pltpu.CompilerParams(vmem_limit_bytes=24 << 20),
        name="pack",
    )(distant(pair), distant(out_cotangent), distant(gain_row), distant(weight_t))
    both = exchange(packed, ROW).reshape(rows, main + 256)
    high = rows // PARTS
    lanes = PARTS * 2 * tile_cols
    smem = pl.BlockSpec(memory_space=pltpu.SMEM)
    vmem = pl.BlockSpec(memory_space=pltpu.VMEM)
    spread = pl.pallas_call(
        bias_out_kernel,
        in_specs=[vmem],
        out_shape=shape((n_col, high, lanes), F32),
        name="bias_out",
    )(resident(both))
    got = pltpu.with_memory_space_constraint(exchange(spread, COL), pltpu.VMEM)
    twin = lax.ppermute(both, CORE, swap)
    inner = project(both, twin, w, jnp.swapaxes(w, 1, 2), w_out, ncols)
    acts, sent = attend(valid_len, got, inner, ncols)
    summed = pltpu.with_memory_space_constraint(exchange(sent, COL), pltpu.VMEM)
    out = merge(acts, lax.ppermute(acts, CORE, swap), w_merge)
    back = pltpu.with_memory_space_constraint(exchange(add_sums(summed, out, n_row), ROW), pltpu.VMEM)
    d_normed, last = pl.pallas_call(
        finish_kernel,
        in_specs=[smem, vmem] + [anywhere] * 3,
        out_shape=[shape((tile, channels), F32), shape((n_all, 5, 2, channels), F32)],
        scratch_shapes=[*inputs, pltpu.SemaphoreType.DMA((3,)), pltpu.VMEM((heads * tile_rows, tile_cols), F32)],
        compiler_params=pltpu.CompilerParams(vmem_limit_bytes=24 << 20),
        name="finish",
    )(core[None], back, pair, gain_row, weight_t)
    everyone = pltpu.with_memory_space_constraint(exchange(last, ALL), pltpu.VMEM)
    attended, pair_gradient = pl.pallas_call(
        output_kernel,
        in_specs=[vmem] * 4,
        out_shape=[shape(pair.shape, BF16), shape(pair.shape, F32)],
        scratch_shapes=[pltpu.VMEM((tile, channels), F32)],
        compiler_params=pltpu.CompilerParams(vmem_limit_bytes=24 << 20),
        name="output",
    )(back, d_normed, pair, gain_row)
    projection_grad, bias_weight_grad, gain_gradient = pl.pallas_call(
        functools.partial(gather_kernel, n_row, n_col),
        in_specs=[vmem],
        out_shape=[shape(projections.shape, F32), shape((heads, channels), F32), shape((1, channels), F32)],
        scratch_shapes=[pltpu.VMEM((2, 5 * half, channels), F32)],
        name="gather",
    )(everyone)
    return (attended, pair_gradient, projection_grad, bias_weight_grad.T, gain_gradient[0])


def solution(mesh):
    torus = Mesh(mesh.devices.reshape(2, 4, 2, 2, 4), ALL)
    in_specs = (P(ROW, COL, None), P(), P(), P(), P(), P(ROW, COL, None))
    out_specs = (P(ROW, COL, None), P(ROW, COL, None), P(), P(), P())
    return jax.shard_map(
        shards, mesh=torus, in_specs=in_specs, out_specs=out_specs, check_vma=False
    )
```

```python
import functools

import jax
import jax.numpy as jnp
from jax import lax
from jax.experimental import pallas as pl
from jax.experimental.pallas import tpu as pltpu
from jax.sharding import Mesh
from jax.sharding import PartitionSpec as P

ROW = ("row_0", "row_1", "row_2")
COL = ("col_0", "col_1")
ALL = ROW + COL
CORE = "row_2"
EPS = 1e-05
MASKED = -1000000000.0
LOG2E = 1.4426950408889634
PARTS = 4
F32 = jnp.float32
BF16 = jnp.bfloat16


def nn(left, right):
    return lax.dot_general(left, right, (((1,), (0,)), ((), ())), preferred_element_type=F32)


def nt(left, right):
    return lax.dot_general(left, right, (((1,), (1,)), ((), ())), preferred_element_type=F32)


def turned(value):
    return jnp.transpose(value.astype(F32)).astype(value.dtype)


def exchange(value, axes):
    return lax.all_to_all(value, axes, split_axis=0, concat_axis=0, tiled=True)


def call(kernel, out_shape, scratch, name, *operands):
    return pl.pallas_call(
        kernel,
        out_shape=out_shape,
        scratch_shapes=scratch,
        compiler_params=pltpu.CompilerParams(vmem_limit_bytes=24 << 20),
        name=name,
    )(*operands)


def resident(value):
    return pltpu.with_memory_space_constraint(value, pltpu.VMEM)


def distant(value):
    return pltpu.with_memory_space_constraint(value, pltpu.HBM)


def fetched(sources, targets, sem):
    copies = [pltpu.make_async_copy(a, b, sem.at[k]) for k, (a, b) in enumerate(zip(sources, targets))]
    for copy in copies:
        copy.start()
    return copies


def coarse_fine(value):
    coarse = value.astype(BF16)
    return coarse, (value - coarse.astype(F32)).astype(BF16)


def normalize(pair_ref, gain_ref):
    rows, cols, channels = pair_ref.shape
    pair = pair_ref[...].astype(F32).reshape(rows * cols, channels)
    average = jnp.mean(pair, axis=-1, keepdims=True)
    var = jnp.mean((pair - average) ** 2, axis=-1, keepdims=True)
    inverse = lax.rsqrt(var + EPS)
    xhat = (pair - average) * inverse
    return xhat, inverse, (xhat * gain_ref[...]).astype(BF16)


def pack_kernel(
    pair_at, cot_at, gain_at, bias_weight_at,
    out_ref, pair_ref, cot_ref, gain_ref, bias_weight_ref, sem, normed_s, cot_s, bias_s,
):
    copies = fetched(
        (pair_at, gain_at, bias_weight_at, cot_at), (pair_ref, gain_ref, bias_weight_ref, cot_ref), sem
    )
    for copy in copies[:3]:
        copy.wait()
    rows, cols, channels = pair_ref.shape
    owners = out_ref.shape[0]
    ncols = cols // owners
    heads = bias_weight_ref.shape[0]
    normed = normalize(pair_ref, gain_ref)[2]
    normed_s[...] = normed.astype(F32)
    copies[3].wait()
    cot_s[...] = cot_ref[...].astype(F32).reshape(rows * cols, channels)
    for a in range(rows):
        bias = nt(bias_weight_ref[...], normed[a * cols : (a + 1) * cols])
        bias_s[pl.ds(a, heads, stride=rows), :] = bias
    pad = jnp.zeros((rows, 384 - 6 * cols), BF16)
    for core in range(2):
        first = 2 * core * rows
        bias = jnp.concatenate([bias_s[first : first + rows], bias_s[first + rows : first + 2 * rows]], axis=1)
        coarse, fine = coarse_fine(bias)
        finest = (bias - coarse.astype(F32) - fine.astype(F32)).astype(BF16)
        bias = jnp.concatenate([coarse, fine, finest, pad], axis=1)
        for owner in range(core, owners, 2):
            out_ref[owner, :, 2 * ncols * channels :] = bias
    for owner in range(owners):
        for k in range(ncols):
            column = pl.ds(owner * ncols + k, rows, stride=cols)
            at = k * channels
            out_ref[owner, :, at : at + channels] = normed_s[column, :].astype(BF16)
            at = (ncols + k) * channels
            out_ref[owner, :, at : at + channels] = cot_s[column, :].astype(BF16)


def bias_out_kernel(both_ref, out_ref):
    rows, wide = both_ref.shape
    width = out_ref.shape[2] // PARTS
    parts = both_ref[:, wide - 384 :].astype(F32)
    bias = parts[:, :width] + (parts[:, width : 2 * width] + parts[:, 2 * width : 3 * width])
    high = rows // PARTS
    packed = jnp.concatenate([bias[k * high : (k + 1) * high] for k in range(PARTS)], axis=1)
    for c in range(out_ref.shape[0]):
        out_ref[c] = packed


def project_kernel(
    normed_ref, twin_normed_ref, cot_ref, twin_cot_ref, w_ref, wt_ref, w_out_ref,
    upright_ref, lying_ref, gates_ref,
):
    channels = w_ref.shape[-1]
    normed = jnp.concatenate([normed_ref[...], twin_normed_ref[...]], axis=1)
    cot = jnp.concatenate([cot_ref[...], twin_cot_ref[...]], axis=1)
    for m in range(3):
        at = slice(m * channels, (m + 1) * channels)
        upright_ref[0, :, at] = nn(normed, w_ref[m]).astype(BF16)
        lying_ref[0, at, :] = nt(wt_ref[m], normed).astype(BF16)
    gate_t = jax.nn.sigmoid(nt(wt_ref[3], normed))
    d_gated_t = nt(w_out_ref[...], cot)
    d_context_t = (d_gated_t * gate_t).astype(BF16)
    gates_ref[0, :channels, :] = gate_t
    gates_ref[0, channels:, :] = d_gated_t
    lying_ref[0, 3 * channels :, :] = d_context_t
    upright_ref[0, :, 3 * channels : 4 * channels] = turned(d_context_t)
    upright_ref[0, :, 4 * channels : 6 * channels] = normed
    upright_ref[0, :, 6 * channels :] = cot


def inner_specs(columns, rows, channels):
    sizes = ((rows, 8 * channels, BF16), (4 * channels, rows, BF16), (2 * channels, rows, F32))
    specs = [pl.BlockSpec((1, high, wide), lambda j: (j, 0, 0)) for high, wide, _ in sizes]
    shapes = [jax.ShapeDtypeStruct((columns, high, wide), kind) for high, wide, kind in sizes]
    return specs, shapes


def project(both, twin, w, wt, w_out, columns):
    rows = both.shape[0]
    channels = w.shape[-1]
    normed = pl.BlockSpec((rows, channels), lambda j: (0, j))
    cot = pl.BlockSpec((rows, channels), lambda j: (0, columns + j))
    specs, shapes = inner_specs(columns, rows, channels)
    return pl.pallas_call(
        project_kernel,
        grid=(columns,),
        in_specs=[
            normed, normed, cot, cot,
            pl.BlockSpec(w.shape, lambda j: (0, 0, 0)),
            pl.BlockSpec(wt.shape, lambda j: (0, 0, 0)),
            pl.BlockSpec(w_out.shape, lambda j: (0, 0)),
        ],
        out_specs=specs,
        out_shape=shapes,
        compiler_params=pltpu.CompilerParams(vmem_limit_bytes=24 << 20),
        name="project",
    )(both, twin, both, twin, w, wt, w_out)


def attention_kernel(
    valid_ref, got_ref, upright_at, lying_at, gates_at,
    acts_ref, sent_ref, upright_ref, lying_ref, gates_ref, sem, bias_s, total, grads_s, d_scores_s, weights_s, right_s,
):
    step = pl.program_id(0)
    steps = pl.num_programs(0)
    blocks, high, lanes = got_ref.shape
    rows = lying_ref.shape[2]
    channels = lying_ref.shape[1] // 4
    slots = 4
    width = channels // slots
    half = channels // 2
    cols = rows // blocks
    scale = width ** (-0.5)

    sources = (upright_at, lying_at, gates_at)
    targets = (upright_ref, lying_ref, gates_ref)

    def block(m, j):
        return pltpu.make_async_copy(sources[m].at[j], targets[m].at[j], sem.at[m, j])

    @pl.when(step == 0)
    def _():
        for j in range(upright_ref.shape[0]):
            for m in range(3):
                block(m, j).start()
        for k in range(PARTS):
            for h in range(2):
                at = (2 * k + h) * cols
                pieces = [got_ref[c, :, at : at + cols] for c in range(blocks)]
                bias_s[h, k * high : (k + 1) * high, :] = jnp.concatenate(pieces, axis=1) * LOG2E
        total[...] = jnp.zeros_like(total)
        grads_s[...] = jnp.zeros_like(grads_s)

    for m in range(3):
        block(m, step).wait()
    def attend_keys(limit):
        query = upright_ref[step, :, :channels]
        d_context = upright_ref[step, :, 3 * channels : 4 * channels]
        key = upright_ref[step, :limit, channels : 2 * channels]
        value = upright_ref[step, :limit, 2 * channels : 3 * channels]
        lane = lax.broadcasted_iota(jnp.int32, (rows, channels), 1)
        sure = rows // 2
        keep = lax.broadcasted_iota(jnp.int32, (limit - sure, rows), 0) + sure < valid_ref[0]
        zero = jnp.zeros((rows, channels), BF16)
        for slot in range(slots):
            mine = (lane >= slot * width) & (lane < (slot + 1) * width)
            here = slice(slot * rows, (slot + 1) * rows)
            part = slice(slot * width, (slot + 1) * width)
            right_s[here, :channels] = jnp.where(mine, query, zero)
            right_s[here, channels:] = jnp.where(mine, d_context, zero)
            scores = nn(key[:, part], lying_ref[step, part]) * (scale * LOG2E) + bias_s[slot % 2, :limit]
            masked = jnp.where(keep, scores[sure:], MASKED * LOG2E)
            scores = jnp.concatenate([scores[:sure], masked], axis=0)
            top = jnp.max(scores, axis=0, keepdims=True)
            grown = jnp.exp2(scores - top)
            inverse = 1.0 / jnp.sum(grown, axis=0, keepdims=True)
            probs = grown * inverse
            weights_s[:limit, here] = probs.astype(BF16)
            d_probs = nn(value[:, part], lying_ref[step, 3 * channels + slot * width : 3 * channels + (slot + 1) * width])
            delta = jnp.sum(grown * d_probs, axis=0, keepdims=True) * inverse
            d_scores = probs * (d_probs - delta)
            total[slot % 2, :limit] += d_scores
            d_scores_s[:limit, here] = d_scores.astype(BF16)
        blocks_t = [
            (nn(lying_ref[step, 2 * channels + s * width : 2 * channels + (s + 1) * width, :limit], weights_s[:limit, s * rows : (s + 1) * rows]),
             nn(lying_ref[step, channels + s * width : channels + (s + 1) * width, :limit], d_scores_s[:limit, s * rows : (s + 1) * rows]))
            for s in range(slots)
        ]
        context_t = jnp.concatenate([one for one, _ in blocks_t], axis=0).astype(BF16).astype(F32)
        d_query_t = (jnp.concatenate([two for _, two in blocks_t], axis=0) * scale).astype(BF16)
        d_key = (nn(d_scores_s[:limit], right_s[:, :channels]) * scale).astype(BF16)
        d_value = nn(weights_s[:limit], right_s[:, channels:]).astype(BF16)
        if limit < rows:
            rest = jnp.zeros((rows - limit, channels), BF16)
            d_key = jnp.concatenate([d_key, rest], axis=0)
            d_value = jnp.concatenate([d_value, rest], axis=0)
        gate_t = gates_ref[step, :channels]
        gated_t = (gate_t * context_t).astype(BF16)
        d_gate_t = (gates_ref[step, channels:] * context_t * gate_t * (1.0 - gate_t)).astype(BF16)
        acts = [turned(gated_t), turned(d_query_t), d_key, d_value, turned(d_gate_t)]
        for m in range(5):
            acts_ref[0, :, m * channels : (m + 1) * channels] = acts[m]
        left = jnp.concatenate([d_query_t, turned(d_key), turned(d_value), d_gate_t], axis=0)
        products = nn(left, upright_ref[step, :, 4 * channels : 6 * channels])
        for m in range(4):
            near = products[m * channels : m * channels + half, :channels]
            far = products[m * channels + half : (m + 1) * channels, channels:]
            grads_s[m * half : (m + 1) * half, :] += near + far
        last = nn(gated_t[:half], upright_ref[step, :, 6 * channels : 7 * channels])
        last = last + nn(gated_t[half:], upright_ref[step, :, 7 * channels :])
        grads_s[4 * half :, :] += last

    below = 0
    for limit in (2 * rows // 3, 5 * rows // 6, rows):
        fits = (valid_ref[0] > below) & (valid_ref[0] <= limit)
        pl.when(fits)(functools.partial(attend_keys, limit))
        below = limit

    @pl.when(step == steps - 1)
    def _():
        for c in range(blocks):
            pieces = [
                total[h, k * high : (k + 1) * high, c * cols : (c + 1) * cols]
                for k in range(PARTS)
                for h in range(2)
            ]
            sent_ref[c, :high, :] = jnp.concatenate(pieces, axis=1).astype(BF16)
        grads = grads_s[...]
        share = grads.shape[0] // blocks
        rest = sent_ref.shape[1] - high
        spare = jnp.zeros((3 * rest - share, channels), F32)
        for c in range(blocks):
            mine = jnp.concatenate([grads[c * share : (c + 1) * share], spare], axis=0)
            pieces = [mine[k * rest : (k + 1) * rest] for k in range(3)]
            sent_ref[c, high:, :] = jnp.concatenate(pieces, axis=1).astype(BF16)


def attend(valid_len, got, inner, columns):
    rows = inner[1].shape[2]
    channels = inner[1].shape[1] // 4
    blocks, high, lanes = got.shape
    return pl.pallas_call(
        attention_kernel,
        grid=(columns,),
        in_specs=[pl.BlockSpec(memory_space=pltpu.SMEM), pl.BlockSpec(memory_space=pltpu.VMEM)]
        + [pl.BlockSpec(memory_space=pl.ANY)] * 3,
        out_specs=[
            pl.BlockSpec((1, rows, 5 * channels), lambda j: (j, 0, 0)),
            pl.BlockSpec((blocks, high + 16, lanes), lambda j: (0, 0, 0)),
        ],
        out_shape=[
            jax.ShapeDtypeStruct((columns, rows, 5 * channels), BF16),
            jax.ShapeDtypeStruct((blocks, high + 16, lanes), BF16),
        ],
        scratch_shapes=[
            *[pltpu.VMEM(one.shape, one.dtype) for one in inner],
            pltpu.SemaphoreType.DMA((3, columns)),
            pltpu.VMEM((2, rows, rows), F32),
            pltpu.VMEM((2, rows, rows), F32),
            pltpu.VMEM((5 * channels // 2, channels), F32),
            pltpu.VMEM((rows, 4 * rows), BF16),
            pltpu.VMEM((rows, 4 * rows), BF16),
            pltpu.VMEM((4 * rows, 2 * channels), BF16),
        ],
        compiler_params=pltpu.CompilerParams(vmem_limit_bytes=24 << 20),
        name="attention",
    )(valid_len, got, *[distant(one) for one in inner])


def merge_kernel(acts_ref, came_ref, w_ref, out_ref):
    column = pl.program_id(0)
    columns = pl.num_programs(0)
    channels = w_ref.shape[-1]
    parts = []
    for m in range(5):
        at = slice(m * channels, (m + 1) * channels)
        parts.append(nn(jnp.concatenate([acts_ref[0, :, at], came_ref[0, :, at]], axis=1), w_ref[m]))
    d_normed = parts[1] + parts[2] + parts[3] + parts[4]
    out_ref[:, pl.ds(pl.multiple_of(column * channels, channels), channels)] = parts[0].astype(BF16)
    second = pl.multiple_of((columns + column) * channels, channels)
    out_ref[:, pl.ds(second, channels)] = d_normed.astype(BF16)


def merge(acts, came, w):
    columns, rows, lanes = acts.shape
    channels = w.shape[-1]
    block = pl.BlockSpec((1, rows, lanes), lambda j: (j, 0, 0))
    return pl.pallas_call(
        merge_kernel,
        grid=(columns,),
        in_specs=[block, block, pl.BlockSpec(w.shape, lambda j: (0, 0, 0))],
        out_specs=pl.BlockSpec((rows, 2 * columns * channels), lambda j: (0, 0)),
        out_shape=jax.ShapeDtypeStruct((rows, 2 * columns * channels + 256), BF16),
        compiler_params=pltpu.CompilerParams(vmem_limit_bytes=24 << 20),
        name="merge",
    )(acts, came, w)


def sum_kernel(got_ref, main_ref, out_ref):
    blocks, high, lanes = got_ref.shape
    owners, rows, wide = out_ref.shape
    part = lanes // PARTS
    total = got_ref[0].astype(F32)
    for c in range(1, blocks):
        total = total + got_ref[c].astype(F32)
    grads = jnp.concatenate([total[part:, k * 128 : (k + 1) * 128] for k in range(3)], axis=0)
    share = 5
    gap = jnp.zeros((rows - 4 * share, 64), F32)
    for owner in range(owners):
        across, down = divmod(owner, part // rows)
        block = total[down * rows : (down + 1) * rows, across * part : (across + 1) * part]
        coarse = block.astype(BF16).astype(F32)
        mine = grads[owner // 2 * share : (owner // 2 + 1) * share]
        near = mine.astype(BF16).astype(F32)
        far = mine - near
        stack = jnp.concatenate([near[:, :64], near[:, 64:], far[:, :64], far[:, 64:], gap], axis=0)
        out_ref[owner] = jnp.concatenate([coarse, block - coarse, stack], axis=1).astype(BF16)


def add_sums(got, main, n_row):
    rows, wide = main.shape
    blocked = main.reshape(n_row, rows // n_row, wide)
    spec = pl.BlockSpec((n_row, rows // n_row, 256), lambda i: (0, 0, wide // 256 - 1))
    return pl.pallas_call(
        sum_kernel,
        grid=(1,),
        in_specs=[pl.BlockSpec(memory_space=pltpu.VMEM), pl.BlockSpec(memory_space=pl.ANY)],
        out_specs=spec,
        out_shape=jax.ShapeDtypeStruct(blocked.shape, BF16),
        input_output_aliases={1: 0},
        compiler_params=pltpu.CompilerParams(vmem_limit_bytes=24 << 20),
        name="sum",
    )(got, blocked)


def finish_kernel(
    core_ref, got_ref, pair_at, gain_at, bias_weight_at,
    d_normed_ref, last_ref, pair_ref, gain_ref, bias_weight_ref, sem, d_bias_s,
):
    copies = fetched((pair_at, gain_at, bias_weight_at), (pair_ref, gain_ref, bias_weight_ref), sem)
    owners, rows, wide = got_ref.shape
    cols, channels = pair_ref.shape[1:]
    heads = bias_weight_ref.shape[0]
    ncols = cols // owners
    main = 2 * ncols * channels
    for owner in range(owners):
        for k in range(ncols):
            column = pl.ds(owner * ncols + k, rows, stride=cols)
            at = (ncols + k) * channels
            d_normed_ref[column, :] = got_ref[owner, :, at : at + channels].astype(F32)
    sums = [jnp.zeros((rows, 256), F32), jnp.zeros((rows, 256), F32)]
    for owner in range(owners):
        sums[owner % 2] = sums[owner % 2] + got_ref[owner, :, main:].astype(F32)
    for core in range(2):
        block = sums[core][:, : 2 * cols] + sums[core][:, 2 * cols : 4 * cols]
        block = block.astype(BF16).astype(F32)
        for h in range(2):
            at = pl.ds(2 * core + h, rows, stride=heads)
            d_bias_s[at, :] = block[:, h * cols : (h + 1) * cols]
    grads = jnp.where(core_ref[0] == 0, sums[0], sums[1])[:, 4 * cols :]
    grads = jnp.concatenate([grads[:5] + grads[10:15], grads[5:10] + grads[15:20]], axis=1)
    for copy in copies:
        copy.wait()
    xhat, inverse, normed = normalize(pair_ref, gain_ref)
    d_bias_t = jnp.transpose(d_bias_s[...]).astype(BF16)
    row = lax.broadcasted_iota(jnp.int32, (rows * heads, channels), 0)
    repeated = jnp.concatenate([bias_weight_ref[...].astype(F32)] * rows, axis=0).astype(BF16)
    weight_part = jnp.zeros((heads, channels), F32)
    for a in range(rows):
        here = slice(a * cols, (a + 1) * cols)
        mine = (row >= a * heads) & (row < (a + 1) * heads)
        weight = jnp.where(mine, repeated, jnp.zeros((rows * heads, channels), BF16))
        d_normed_ref[here, :] += nn(d_bias_t, weight)
        d_bias_a = d_bias_s[a * heads : (a + 1) * heads, :].astype(BF16)
        weight_part = weight_part + nn(d_bias_a, normed[here])
    gain_part = jnp.sum(d_normed_ref[...] * xhat, axis=0, keepdims=True)
    small = jnp.concatenate([weight_part, gain_part], axis=0)
    for t in range(5):
        pair = jnp.concatenate([grads[t : t + 1], small[t : t + 1]], axis=0)
        last_ref[:, t] = jnp.broadcast_to(pair[None], (last_ref.shape[0], 2, channels))


def output_kernel(got_ref, d_normed_ref, pair_ref, gain_ref, attended_ref, gradient_ref, moved_s):
    owners, rows, wide = got_ref.shape
    cols, channels = pair_ref.shape[1:]
    ncols = cols // owners
    xhat, inverse, normed = normalize(pair_ref, gain_ref)
    for owner in range(owners):
        for k in range(ncols):
            column = pl.ds(owner * ncols + k, rows, stride=cols)
            moved_s[column, :] = got_ref[owner, :, k * channels : (k + 1) * channels].astype(F32)
    attended_ref[...] = moved_s[...].astype(BF16).reshape(attended_ref.shape)
    scaled = d_normed_ref[...] * gain_ref[...]
    gradient = inverse * (
        scaled
        - jnp.mean(scaled, axis=-1, keepdims=True)
        - xhat * jnp.mean(scaled * xhat, axis=-1, keepdims=True)
    )
    gradient_ref[...] = gradient.reshape(gradient_ref.shape)


def gather_kernel(n_row, n_col, got_ref, grad_ref, weight_ref, gain_ref, halves_s):
    channels = got_ref.shape[-1]
    share = got_ref.shape[1]
    half = channels // 2
    for r in range(n_row):
        for c in range(n_col):
            at = (c * (n_row // 2) + r // 2) * share
            halves_s[r % 2, at : at + share, :] = got_ref[r * n_col + c, :, 0, :]
    small = jnp.sum(got_ref[:, :, 1, :], axis=0)
    heads = weight_ref.shape[0]
    weight_ref[...] = small[:heads]
    gain_ref[...] = small[heads : heads + 1]
    for m in range(5):
        both = [halves_s[core, m * half : (m + 1) * half, :] for core in range(2)]
        both = jnp.concatenate(both, axis=0)
        grad_ref[m] = jnp.transpose(both) if m < 4 else both


def shards(pair, gain, projections, bias_weight, valid_len, out_cotangent):
    n_row = lax.axis_size(ROW)
    n_col = lax.axis_size(COL)
    n_all = n_row * n_col
    tile_rows, tile_cols, channels = pair.shape
    rows = tile_rows * n_row
    heads = bias_weight.shape[1]
    ncols = tile_cols // n_row
    tile = tile_rows * tile_cols
    main = 2 * ncols * channels
    half = channels // 2
    shape = jax.ShapeDtypeStruct
    gain_row = gain[None, :]
    weight_t = bias_weight.T
    swap = [(0, 1), (1, 0)]
    core = lax.axis_index(CORE).astype(jnp.int32)
    halves = projections[:4].reshape(4, channels, 2, half)
    rows_out = projections[4].reshape(2, half, channels)
    own = lax.dynamic_index_in_dim(halves, core, 2, keepdims=False)
    other = lax.dynamic_index_in_dim(halves, 1 - core, 2, keepdims=False)
    own_out = lax.dynamic_index_in_dim(rows_out, core, 0, keepdims=False)
    other_out = lax.dynamic_index_in_dim(rows_out, 1 - core, 0, keepdims=False)
    zero = jnp.zeros_like(own)
    w = jnp.concatenate(
        [jnp.concatenate([own, zero], axis=2), jnp.concatenate([zero, own], axis=2)], axis=1
    )
    zero_out = jnp.zeros_like(own_out)
    w_out = jnp.concatenate(
        [jnp.concatenate([own_out, zero_out], axis=1), jnp.concatenate([zero_out, own_out], axis=1)],
        axis=0,
    )
    mine = jnp.concatenate([own_out[None], jnp.swapaxes(own, 1, 2)], axis=0)
    theirs = jnp.concatenate([other_out[None], jnp.swapaxes(other, 1, 2)], axis=0)
    gap = jnp.zeros((5, channels, channels), BF16)
    w_merge = jnp.concatenate([mine, gap, theirs], axis=1)

    anywhere = pl.BlockSpec(memory_space=pl.ANY)
    inputs = [pltpu.VMEM(pair.shape, BF16), pltpu.VMEM(gain_row.shape, F32), pltpu.VMEM(weight_t.shape, BF16)]
    packed = pl.pallas_call(
        pack_kernel,
        in_specs=[anywhere] * 4,
        out_shape=shape((n_row, tile_rows, main + 384), BF16),
        scratch_shapes=[
            inputs[0], *inputs, pltpu.SemaphoreType.DMA((4,)),
            pltpu.VMEM((tile, channels), F32), pltpu.VMEM((tile, channels), F32),
            pltpu.VMEM((heads * tile_rows, tile_cols), F32),
        ],
        compiler_params=pltpu.CompilerParams(vmem_limit_bytes=24 << 20),
        name="pack",
    )(distant(pair), distant(out_cotangent), distant(gain_row), distant(weight_t))
    both = exchange(packed, ROW).reshape(rows, main + 384)
    high = rows // PARTS
    lanes = PARTS * 2 * tile_cols
    smem = pl.BlockSpec(memory_space=pltpu.SMEM)
    vmem = pl.BlockSpec(memory_space=pltpu.VMEM)
    spread = pl.pallas_call(
        bias_out_kernel,
        in_specs=[vmem],
        out_shape=shape((n_col, high, lanes), F32),
        name="bias_out",
    )(resident(both))
    got = pltpu.with_memory_space_constraint(exchange(spread, COL), pltpu.VMEM)
    twin = lax.ppermute(both, CORE, swap)
    inner = project(both, twin, w, jnp.swapaxes(w, 1, 2), w_out, ncols)
    acts, sent = attend(valid_len, got, inner, ncols)
    summed = pltpu.with_memory_space_constraint(exchange(sent, COL), pltpu.VMEM)
    out = merge(acts, lax.ppermute(acts, CORE, swap), w_merge)
    back = pltpu.with_memory_space_constraint(exchange(add_sums(summed, out, n_row), ROW), pltpu.VMEM)
    d_normed, last = pl.pallas_call(
        finish_kernel,
        in_specs=[smem, vmem] + [anywhere] * 3,
        out_shape=[shape((tile, channels), F32), shape((n_all, 5, 2, channels), F32)],
        scratch_shapes=[*inputs, pltpu.SemaphoreType.DMA((3,)), pltpu.VMEM((heads * tile_rows, tile_cols), F32)],
        compiler_params=pltpu.CompilerParams(vmem_limit_bytes=24 << 20),
        name="finish",
    )(core[None], back, pair, gain_row, weight_t)
    everyone = pltpu.with_memory_space_constraint(exchange(last, ALL), pltpu.VMEM)
    attended, pair_gradient = pl.pallas_call(
        output_kernel,
        in_specs=[vmem] * 4,
        out_shape=[shape(pair.shape, BF16), shape(pair.shape, F32)],
        scratch_shapes=[pltpu.VMEM((tile, channels), F32)],
        compiler_params=pltpu.CompilerParams(vmem_limit_bytes=24 << 20),
        name="output",
    )(back, d_normed, pair, gain_row)
    projection_grad, bias_weight_grad, gain_gradient = pl.pallas_call(
        functools.partial(gather_kernel, n_row, n_col),
        in_specs=[vmem],
        out_shape=[shape(projections.shape, F32), shape((heads, channels), F32), shape((1, channels), F32)],
        scratch_shapes=[pltpu.VMEM((2, 5 * half, channels), F32)],
        name="gather",
    )(everyone)
    return (attended, pair_gradient, projection_grad, bias_weight_grad.T, gain_gradient[0])


def solution(mesh):
    torus = Mesh(mesh.devices.reshape(2, 4, 2, 2, 4), ALL)
    in_specs = (P(ROW, COL, None), P(), P(), P(), P(), P(ROW, COL, None))
    out_specs = (P(ROW, COL, None), P(ROW, COL, None), P(), P(), P())
    return jax.shard_map(
        shards, mesh=torus, in_specs=in_specs, out_specs=out_specs, check_vma=False
    )
```

```python
import functools

import jax
import jax.numpy as jnp
from jax import lax
from jax.experimental import pallas as pl
from jax.experimental.pallas import tpu as pltpu
from jax.sharding import Mesh
from jax.sharding import PartitionSpec as P

ROW = ("row_0", "row_1", "row_2")
COL = ("col_0", "col_1")
ALL = ROW + COL
CORE = "row_2"
EPS = 1e-05
MASKED = -1000000000.0
LOG2E = 1.4426950408889634
PARTS = 4
F32 = jnp.float32
BF16 = jnp.bfloat16


def nn(left, right):
    return lax.dot_general(left, right, (((1,), (0,)), ((), ())), preferred_element_type=F32)


def nt(left, right):
    return lax.dot_general(left, right, (((1,), (1,)), ((), ())), preferred_element_type=F32)


def turned(value):
    return jnp.transpose(value.astype(F32)).astype(value.dtype)


def exchange(value, axes):
    return lax.all_to_all(value, axes, split_axis=0, concat_axis=0, tiled=True)


def call(kernel, out_shape, scratch, name, *operands):
    return pl.pallas_call(
        kernel,
        out_shape=out_shape,
        scratch_shapes=scratch,
        compiler_params=pltpu.CompilerParams(vmem_limit_bytes=24 << 20),
        name=name,
    )(*operands)


def resident(value):
    return pltpu.with_memory_space_constraint(value, pltpu.VMEM)


def distant(value):
    return pltpu.with_memory_space_constraint(value, pltpu.HBM)


def fetched(sources, targets, sem):
    copies = [pltpu.make_async_copy(a, b, sem.at[k]) for k, (a, b) in enumerate(zip(sources, targets))]
    for copy in copies:
        copy.start()
    return copies


def coarse_fine(value):
    coarse = value.astype(BF16)
    return coarse, (value - coarse.astype(F32)).astype(BF16)


def normalize(pair_ref, gain_ref):
    rows, cols, channels = pair_ref.shape
    pair = pair_ref[...].astype(F32).reshape(rows * cols, channels)
    average = jnp.mean(pair, axis=-1, keepdims=True)
    var = jnp.mean((pair - average) ** 2, axis=-1, keepdims=True)
    inverse = lax.rsqrt(var + EPS)
    xhat = (pair - average) * inverse
    return xhat, inverse, (xhat * gain_ref[...]).astype(BF16)


def pack_kernel(
    pair_at, cot_at, gain_at, bias_weight_at,
    out_ref, pair_ref, cot_ref, gain_ref, bias_weight_ref, sem, normed_s, cot_s, bias_s,
):
    copies = fetched(
        (pair_at, gain_at, bias_weight_at, cot_at), (pair_ref, gain_ref, bias_weight_ref, cot_ref), sem
    )
    for copy in copies[:3]:
        copy.wait()
    rows, cols, channels = pair_ref.shape
    owners = out_ref.shape[0]
    ncols = cols // owners
    heads = bias_weight_ref.shape[0]
    normed = normalize(pair_ref, gain_ref)[2]
    normed_s[...] = normed.astype(F32)
    copies[3].wait()
    cot_s[...] = cot_ref[...].astype(F32).reshape(rows * cols, channels)
    for a in range(rows):
        bias = nt(bias_weight_ref[...], normed[a * cols : (a + 1) * cols])
        bias_s[pl.ds(a, heads, stride=rows), :] = bias
    pad = jnp.zeros((rows, 384 - 6 * cols), BF16)
    for core in range(2):
        first = 2 * core * rows
        bias = jnp.concatenate([bias_s[first : first + rows], bias_s[first + rows : first + 2 * rows]], axis=1)
        coarse, fine = coarse_fine(bias)
        finest = (bias - coarse.astype(F32) - fine.astype(F32)).astype(BF16)
        bias = jnp.concatenate([coarse, fine, finest, pad], axis=1)
        for owner in range(core, owners, 2):
            out_ref[owner, :, 2 * ncols * channels :] = bias
    for owner in range(owners):
        for k in range(ncols):
            column = pl.ds(owner * ncols + k, rows, stride=cols)
            at = k * channels
            out_ref[owner, :, at : at + channels] = normed_s[column, :].astype(BF16)
            at = (ncols + k) * channels
            out_ref[owner, :, at : at + channels] = cot_s[column, :].astype(BF16)


def bias_out_kernel(both_ref, out_ref):
    rows, wide = both_ref.shape
    width = out_ref.shape[2] // PARTS
    parts = both_ref[:, wide - 384 :].astype(F32)
    bias = parts[:, :width] + (parts[:, width : 2 * width] + parts[:, 2 * width : 3 * width])
    high = rows // PARTS
    packed = jnp.concatenate([bias[k * high : (k + 1) * high] for k in range(PARTS)], axis=1)
    for c in range(out_ref.shape[0]):
        out_ref[c] = packed


def project_kernel(
    normed_ref, twin_normed_ref, cot_ref, twin_cot_ref, w_ref, wt_ref, w_out_ref,
    upright_ref, lying_ref, gates_ref,
):
    channels = w_ref.shape[-1]
    normed = jnp.concatenate([normed_ref[...], twin_normed_ref[...]], axis=1)
    cot = jnp.concatenate([cot_ref[...], twin_cot_ref[...]], axis=1)
    for m in range(3):
        at = slice(m * channels, (m + 1) * channels)
        upright_ref[0, :, at] = nn(normed, w_ref[m]).astype(BF16)
        lying_ref[0, at, :] = nt(wt_ref[m], normed).astype(BF16)
    gate_t = jax.nn.sigmoid(nt(wt_ref[3], normed))
    d_gated_t = nt(w_out_ref[...], cot)
    d_context_t = (d_gated_t * gate_t).astype(BF16)
    gates_ref[0, :channels, :] = gate_t
    gates_ref[0, channels:, :] = d_gated_t
    lying_ref[0, 3 * channels :, :] = d_context_t
    upright_ref[0, :, 3 * channels : 4 * channels] = turned(d_context_t)
    upright_ref[0, :, 4 * channels : 6 * channels] = normed
    upright_ref[0, :, 6 * channels :] = cot


def inner_specs(columns, rows, channels):
    sizes = ((rows, 8 * channels, BF16), (4 * channels, rows, BF16), (2 * channels, rows, F32))
    specs = [pl.BlockSpec((1, high, wide), lambda j: (j, 0, 0)) for high, wide, _ in sizes]
    shapes = [jax.ShapeDtypeStruct((columns, high, wide), kind) for high, wide, kind in sizes]
    return specs, shapes


def project(both, twin, w, wt, w_out, columns):
    rows = both.shape[0]
    channels = w.shape[-1]
    normed = pl.BlockSpec((rows, channels), lambda j: (0, j))
    cot = pl.BlockSpec((rows, channels), lambda j: (0, columns + j))
    specs, shapes = inner_specs(columns, rows, channels)
    return pl.pallas_call(
        project_kernel,
        grid=(columns,),
        in_specs=[
            normed, normed, cot, cot,
            pl.BlockSpec(w.shape, lambda j: (0, 0, 0)),
            pl.BlockSpec(wt.shape, lambda j: (0, 0, 0)),
            pl.BlockSpec(w_out.shape, lambda j: (0, 0)),
        ],
        out_specs=specs,
        out_shape=shapes,
        compiler_params=pltpu.CompilerParams(vmem_limit_bytes=24 << 20),
        name="project",
    )(both, twin, both, twin, w, wt, w_out)


def attention_kernel(
    valid_ref, got_ref, upright_at, lying_at, gates_at,
    acts_ref, sent_ref, upright_ref, lying_ref, gates_ref, sem, bias_s, total, grads_s, d_scores_s, weights_s, right_s,
):
    step = pl.program_id(0)
    steps = pl.num_programs(0)
    blocks, high, lanes = got_ref.shape
    rows = lying_ref.shape[2]
    channels = lying_ref.shape[1] // 4
    slots = 4
    width = channels // slots
    half = channels // 2
    cols = rows // blocks
    scale = width ** (-0.5)

    sources = (upright_at, lying_at, gates_at)
    targets = (upright_ref, lying_ref, gates_ref)

    def block(m, j):
        return pltpu.make_async_copy(sources[m].at[j], targets[m].at[j], sem.at[m, j])

    @pl.when(step == 0)
    def _():
        for j in range(upright_ref.shape[0]):
            for m in range(3):
                block(m, j).start()
        for k in range(PARTS):
            for h in range(2):
                at = (2 * k + h) * cols
                pieces = [got_ref[c, :, at : at + cols] for c in range(blocks)]
                bias_s[h, k * high : (k + 1) * high, :] = jnp.concatenate(pieces, axis=1) * LOG2E
        total[...] = jnp.zeros_like(total)
        grads_s[...] = jnp.zeros_like(grads_s)

    for m in range(3):
        block(m, step).wait()
    def attend_keys(limit):
        query = upright_ref[step, :, :channels]
        d_context = upright_ref[step, :, 3 * channels : 4 * channels]
        key = upright_ref[step, :limit, channels : 2 * channels]
        value = upright_ref[step, :limit, 2 * channels : 3 * channels]
        lane = lax.broadcasted_iota(jnp.int32, (rows, channels), 1)
        sure = rows // 2
        keep = lax.broadcasted_iota(jnp.int32, (limit - sure, rows), 0) + sure < valid_ref[0]
        zero = jnp.zeros((rows, channels), BF16)
        for slot in range(slots):
            mine = (lane >= slot * width) & (lane < (slot + 1) * width)
            here = slice(slot * rows, (slot + 1) * rows)
            part = slice(slot * width, (slot + 1) * width)
            right_s[here, :channels] = jnp.where(mine, query, zero)
            right_s[here, channels:] = jnp.where(mine, d_context, zero)
            scores = nn(key[:, part], lying_ref[step, part]) * (scale * LOG2E) + bias_s[slot % 2, :limit]
            masked = jnp.where(keep, scores[sure:], MASKED * LOG2E)
            scores = jnp.concatenate([scores[:sure], masked], axis=0)
            top = jnp.max(scores, axis=0, keepdims=True)
            grown = jnp.exp2(scores - top)
            inverse = 1.0 / jnp.sum(grown, axis=0, keepdims=True)
            probs = grown * inverse
            weights_s[:limit, here] = probs.astype(BF16)
            d_probs = nn(value[:, part], lying_ref[step, 3 * channels + slot * width : 3 * channels + (slot + 1) * width])
            delta = jnp.sum(grown * d_probs, axis=0, keepdims=True) * inverse
            d_scores = probs * (d_probs - delta)
            total[slot % 2, :limit] += d_scores
            d_scores_s[:limit, here] = d_scores.astype(BF16)
        blocks_t = [
            (nn(lying_ref[step, 2 * channels + s * width : 2 * channels + (s + 1) * width, :limit], weights_s[:limit, s * rows : (s + 1) * rows]),
             nn(lying_ref[step, channels + s * width : channels + (s + 1) * width, :limit], d_scores_s[:limit, s * rows : (s + 1) * rows]))
            for s in range(slots)
        ]
        context_t = jnp.concatenate([one for one, _ in blocks_t], axis=0).astype(BF16).astype(F32)
        d_query_t = (jnp.concatenate([two for _, two in blocks_t], axis=0) * scale).astype(BF16)
        d_key = (nn(d_scores_s[:limit], right_s[:, :channels]) * scale).astype(BF16)
        d_value = nn(weights_s[:limit], right_s[:, channels:]).astype(BF16)
        if limit < rows:
            rest = jnp.zeros((rows - limit, channels), BF16)
            d_key = jnp.concatenate([d_key, rest], axis=0)
            d_value = jnp.concatenate([d_value, rest], axis=0)
        gate_t = gates_ref[step, :channels]
        gated_t = (gate_t * context_t).astype(BF16)
        d_gate_t = (gates_ref[step, channels:] * context_t * gate_t * (1.0 - gate_t)).astype(BF16)
        acts = [turned(gated_t), turned(d_query_t), d_key, d_value, turned(d_gate_t)]
        for m in range(5):
            acts_ref[0, :, m * channels : (m + 1) * channels] = acts[m]
        left = jnp.concatenate([d_query_t, turned(d_key), turned(d_value), d_gate_t], axis=0)
        products = nn(left, upright_ref[step, :, 4 * channels : 6 * channels])
        for m in range(4):
            near = products[m * channels : m * channels + half, :channels]
            far = products[m * channels + half : (m + 1) * channels, channels:]
            grads_s[m * half : (m + 1) * half, :] += near + far
        last = nn(gated_t[:half], upright_ref[step, :, 6 * channels : 7 * channels])
        last = last + nn(gated_t[half:], upright_ref[step, :, 7 * channels :])
        grads_s[4 * half :, :] += last

    below = 0
    for limit in (2 * rows // 3, 5 * rows // 6, rows):
        fits = (valid_ref[0] > below) & (valid_ref[0] <= limit)
        pl.when(fits)(functools.partial(attend_keys, limit))
        below = limit

    @pl.when(step == steps - 1)
    def _():
        for c in range(blocks):
            pieces = [
                total[h, k * high : (k + 1) * high, c * cols : (c + 1) * cols]
                for k in range(PARTS)
                for h in range(2)
            ]
            sent_ref[c, :high, :] = jnp.concatenate(pieces, axis=1).astype(BF16)
        grads = grads_s[...]
        share = grads.shape[0] // blocks
        rest = sent_ref.shape[1] - high
        spare = jnp.zeros((3 * rest - share, channels), F32)
        for c in range(blocks):
            mine = jnp.concatenate([grads[c * share : (c + 1) * share], spare], axis=0)
            pieces = [mine[k * rest : (k + 1) * rest] for k in range(3)]
            sent_ref[c, high:, :] = jnp.concatenate(pieces, axis=1).astype(BF16)


def attend(valid_len, got, inner, columns):
    rows = inner[1].shape[2]
    channels = inner[1].shape[1] // 4
    blocks, high, lanes = got.shape
    return pl.pallas_call(
        attention_kernel,
        grid=(columns,),
        in_specs=[pl.BlockSpec(memory_space=pltpu.SMEM), pl.BlockSpec(memory_space=pltpu.VMEM)]
        + [pl.BlockSpec(memory_space=pl.ANY)] * 3,
        out_specs=[
            pl.BlockSpec((1, rows, 5 * channels), lambda j: (j, 0, 0)),
            pl.BlockSpec((blocks, high + 16, lanes), lambda j: (0, 0, 0)),
        ],
        out_shape=[
            jax.ShapeDtypeStruct((columns, rows, 5 * channels), BF16),
            jax.ShapeDtypeStruct((blocks, high + 16, lanes), BF16),
        ],
        scratch_shapes=[
            *[pltpu.VMEM(one.shape, one.dtype) for one in inner],
            pltpu.SemaphoreType.DMA((3, columns)),
            pltpu.VMEM((2, rows, rows), F32),
            pltpu.VMEM((2, rows, rows), F32),
            pltpu.VMEM((5 * channels // 2, channels), F32),
            pltpu.VMEM((rows, 4 * rows), BF16),
            pltpu.VMEM((rows, 4 * rows), BF16),
            pltpu.VMEM((4 * rows, 2 * channels), BF16),
        ],
        compiler_params=pltpu.CompilerParams(vmem_limit_bytes=24 << 20),
        name="attention",
    )(valid_len, got, *[distant(one) for one in inner])


def merge_kernel(acts_ref, came_ref, w_ref, out_ref):
    column = pl.program_id(0)
    columns = pl.num_programs(0)
    channels = w_ref.shape[-1]
    parts = []
    for m in range(5):
        at = slice(m * channels, (m + 1) * channels)
        parts.append(nn(jnp.concatenate([acts_ref[0, :, at], came_ref[0, :, at]], axis=1), w_ref[m]))
    d_normed = parts[1] + parts[2] + parts[3] + parts[4]
    out_ref[:, pl.ds(pl.multiple_of(column * channels, channels), channels)] = parts[0].astype(BF16)
    second = pl.multiple_of((columns + column) * channels, channels)
    out_ref[:, pl.ds(second, channels)] = d_normed.astype(BF16)


def merge(acts, came, w):
    columns, rows, lanes = acts.shape
    channels = w.shape[-1]
    block = pl.BlockSpec((1, rows, lanes), lambda j: (j, 0, 0))
    return pl.pallas_call(
        merge_kernel,
        grid=(columns,),
        in_specs=[block, block, pl.BlockSpec(w.shape, lambda j: (0, 0, 0))],
        out_specs=pl.BlockSpec((rows, 2 * columns * channels), lambda j: (0, 0)),
        out_shape=jax.ShapeDtypeStruct((rows, 2 * columns * channels + 256), BF16),
        compiler_params=pltpu.CompilerParams(vmem_limit_bytes=24 << 20),
        name="merge",
    )(acts, came, w)


def sum_kernel(got_ref, main_ref, out_ref):
    blocks, high, lanes = got_ref.shape
    owners, rows, wide = out_ref.shape
    part = lanes // PARTS
    total = got_ref[0].astype(F32)
    for c in range(1, blocks):
        total = total + got_ref[c].astype(F32)
    grads = jnp.concatenate([total[part:, k * 128 : (k + 1) * 128] for k in range(3)], axis=0)
    share = 5
    gap = jnp.zeros((rows - 4 * share, 64), F32)
    for owner in range(owners):
        across, down = divmod(owner, part // rows)
        block = total[down * rows : (down + 1) * rows, across * part : (across + 1) * part]
        coarse = block.astype(BF16).astype(F32)
        mine = grads[owner // 2 * share : (owner // 2 + 1) * share]
        near = mine.astype(BF16).astype(F32)
        far = mine - near
        stack = jnp.concatenate([near[:, :64], near[:, 64:], far[:, :64], far[:, 64:], gap], axis=0)
        out_ref[owner] = jnp.concatenate([coarse, block - coarse, stack], axis=1).astype(BF16)


def add_sums(got, main, n_row):
    rows, wide = main.shape
    blocked = main.reshape(n_row, rows // n_row, wide)
    spec = pl.BlockSpec((n_row, rows // n_row, 256), lambda i: (0, 0, wide // 256 - 1))
    return pl.pallas_call(
        sum_kernel,
        grid=(1,),
        in_specs=[pl.BlockSpec(memory_space=pltpu.VMEM), pl.BlockSpec(memory_space=pl.ANY)],
        out_specs=spec,
        out_shape=jax.ShapeDtypeStruct(blocked.shape, BF16),
        input_output_aliases={1: 0},
        compiler_params=pltpu.CompilerParams(vmem_limit_bytes=24 << 20),
        name="sum",
    )(got, blocked)


def finish_kernel(
    core_ref, got_ref, pair_at, gain_at, bias_weight_at,
    d_normed_ref, last_ref, pair_ref, gain_ref, bias_weight_ref, sem, d_bias_s,
):
    copies = fetched((pair_at, gain_at, bias_weight_at), (pair_ref, gain_ref, bias_weight_ref), sem)
    owners, rows, wide = got_ref.shape
    cols, channels = pair_ref.shape[1:]
    heads = bias_weight_ref.shape[0]
    ncols = cols // owners
    main = 2 * ncols * channels
    for owner in range(owners):
        for k in range(ncols):
            column = pl.ds(owner * ncols + k, rows, stride=cols)
            at = (ncols + k) * channels
            d_normed_ref[column, :] = got_ref[owner, :, at : at + channels].astype(F32)
    sums = [jnp.zeros((rows, 256), F32), jnp.zeros((rows, 256), F32)]
    for owner in range(owners):
        sums[owner % 2] = sums[owner % 2] + got_ref[owner, :, main:].astype(F32)
    for core in range(2):
        block = sums[core][:, : 2 * cols] + sums[core][:, 2 * cols : 4 * cols]
        block = block.astype(BF16).astype(F32)
        for h in range(2):
            at = pl.ds(2 * core + h, rows, stride=heads)
            d_bias_s[at, :] = block[:, h * cols : (h + 1) * cols]
    grads = jnp.where(core_ref[0] == 0, sums[0], sums[1])[:, 4 * cols :]
    grads = jnp.concatenate([grads[:5] + grads[10:15], grads[5:10] + grads[15:20]], axis=1)
    for copy in copies:
        copy.wait()
    xhat, inverse, normed = normalize(pair_ref, gain_ref)
    d_bias_t = jnp.transpose(d_bias_s[...]).astype(BF16)
    row = lax.broadcasted_iota(jnp.int32, (rows * heads, channels), 0)
    repeated = jnp.concatenate([bias_weight_ref[...].astype(F32)] * rows, axis=0).astype(BF16)
    weight_part = jnp.zeros((heads, channels), F32)
    for a in range(rows):
        here = slice(a * cols, (a + 1) * cols)
        mine = (row >= a * heads) & (row < (a + 1) * heads)
        weight = jnp.where(mine, repeated, jnp.zeros((rows * heads, channels), BF16))
        d_normed_ref[here, :] += nn(d_bias_t, weight)
        d_bias_a = d_bias_s[a * heads : (a + 1) * heads, :].astype(BF16)
        weight_part = weight_part + nn(d_bias_a, normed[here])
    gain_part = jnp.sum(d_normed_ref[...] * xhat, axis=0, keepdims=True)
    small = jnp.concatenate([weight_part, gain_part], axis=0)
    for t in range(5):
        pair = jnp.concatenate([grads[t : t + 1], small[t : t + 1]], axis=0)
        last_ref[:, t] = jnp.broadcast_to(pair[None], (last_ref.shape[0], 2, channels))


def output_kernel(got_ref, d_normed_ref, pair_ref, gain_ref, attended_ref, gradient_ref, moved_s):
    owners, rows, wide = got_ref.shape
    cols, channels = pair_ref.shape[1:]
    ncols = cols // owners
    xhat, inverse, normed = normalize(pair_ref, gain_ref)
    for owner in range(owners):
        for k in range(ncols):
            column = pl.ds(owner * ncols + k, rows, stride=cols)
            moved_s[column, :] = got_ref[owner, :, k * channels : (k + 1) * channels].astype(F32)
    attended_ref[...] = moved_s[...].astype(BF16).reshape(attended_ref.shape)
    scaled = d_normed_ref[...] * gain_ref[...]
    gradient = inverse * (
        scaled
        - jnp.mean(scaled, axis=-1, keepdims=True)
        - xhat * jnp.mean(scaled * xhat, axis=-1, keepdims=True)
    )
    gradient_ref[...] = gradient.reshape(gradient_ref.shape)


def gather_kernel(n_row, n_col, got_ref, grad_ref, weight_ref, gain_ref, halves_s):
    channels = got_ref.shape[-1]
    share = got_ref.shape[1]
    half = channels // 2
    for r in range(n_row):
        for c in range(n_col):
            at = (c * (n_row // 2) + r // 2) * share
            halves_s[r % 2, at : at + share, :] = got_ref[r * n_col + c, :, 0, :]
    small = jnp.sum(got_ref[:, :, 1, :], axis=0)
    heads = weight_ref.shape[0]
    weight_ref[...] = small[:heads]
    gain_ref[...] = small[heads : heads + 1]
    for m in range(5):
        both = [halves_s[core, m * half : (m + 1) * half, :] for core in range(2)]
        both = jnp.concatenate(both, axis=0)
        grad_ref[m] = jnp.transpose(both) if m < 4 else both


def shards(pair, gain, projections, bias_weight, valid_len, out_cotangent):
    n_row = lax.axis_size(ROW)
    n_col = lax.axis_size(COL)
    n_all = n_row * n_col
    tile_rows, tile_cols, channels = pair.shape
    rows = tile_rows * n_row
    heads = bias_weight.shape[1]
    ncols = tile_cols // n_row
    tile = tile_rows * tile_cols
    main = 2 * ncols * channels
    half = channels // 2
    shape = jax.ShapeDtypeStruct
    gain_row = gain[None, :]
    weight_t = bias_weight.T
    swap = [(0, 1), (1, 0)]
    core = lax.axis_index(CORE).astype(jnp.int32)
    halves = projections[:4].reshape(4, channels, 2, half)
    rows_out = projections[4].reshape(2, half, channels)
    own = lax.dynamic_index_in_dim(halves, core, 2, keepdims=False)
    other = lax.dynamic_index_in_dim(halves, 1 - core, 2, keepdims=False)
    own_out = lax.dynamic_index_in_dim(rows_out, core, 0, keepdims=False)
    other_out = lax.dynamic_index_in_dim(rows_out, 1 - core, 0, keepdims=False)
    zero = jnp.zeros_like(own)
    w = jnp.concatenate(
        [jnp.concatenate([own, zero], axis=2), jnp.concatenate([zero, own], axis=2)], axis=1
    )
    zero_out = jnp.zeros_like(own_out)
    w_out = jnp.concatenate(
        [jnp.concatenate([own_out, zero_out], axis=1), jnp.concatenate([zero_out, own_out], axis=1)],
        axis=0,
    )
    mine = jnp.concatenate([own_out[None], jnp.swapaxes(own, 1, 2)], axis=0)
    theirs = jnp.concatenate([other_out[None], jnp.swapaxes(other, 1, 2)], axis=0)
    gap = jnp.zeros((5, channels, channels), BF16)
    w_merge = jnp.concatenate([mine, gap, theirs], axis=1)

    anywhere = pl.BlockSpec(memory_space=pl.ANY)
    inputs = [pltpu.VMEM(pair.shape, BF16), pltpu.VMEM(gain_row.shape, F32), pltpu.VMEM(weight_t.shape, BF16)]
    packed = pl.pallas_call(
        pack_kernel,
        in_specs=[anywhere] * 4,
        out_shape=shape((n_row, tile_rows, main + 384), BF16),
        scratch_shapes=[
            inputs[0], *inputs, pltpu.SemaphoreType.DMA((4,)),
            pltpu.VMEM((tile, channels), F32), pltpu.VMEM((tile, channels), F32),
            pltpu.VMEM((heads * tile_rows, tile_cols), F32),
        ],
        compiler_params=pltpu.CompilerParams(vmem_limit_bytes=24 << 20),
        name="pack",
    )(distant(pair), distant(out_cotangent), distant(gain_row), distant(weight_t))
    both = exchange(packed, ROW).reshape(rows, main + 384)
    high = rows // PARTS
    lanes = PARTS * 2 * tile_cols
    smem = pl.BlockSpec(memory_space=pltpu.SMEM)
    vmem = pl.BlockSpec(memory_space=pltpu.VMEM)
    spread = pl.pallas_call(
        bias_out_kernel,
        in_specs=[vmem],
        out_shape=shape((n_col, high, lanes), F32),
        compiler_params=pltpu.CompilerParams(vmem_limit_bytes=24 << 20),
        name="bias_out",
    )(resident(both))
    got = pltpu.with_memory_space_constraint(exchange(spread, COL), pltpu.VMEM)
    twin = lax.ppermute(both, CORE, swap)
    inner = project(both, twin, w, jnp.swapaxes(w, 1, 2), w_out, ncols)
    acts, sent = attend(valid_len, got, inner, ncols)
    summed = pltpu.with_memory_space_constraint(exchange(sent, COL), pltpu.VMEM)
    out = merge(acts, lax.ppermute(acts, CORE, swap), w_merge)
    back = pltpu.with_memory_space_constraint(exchange(add_sums(summed, out, n_row), ROW), pltpu.VMEM)
    d_normed, last = pl.pallas_call(
        finish_kernel,
        in_specs=[smem, vmem] + [anywhere] * 3,
        out_shape=[shape((tile, channels), F32), shape((n_all, 5, 2, channels), F32)],
        scratch_shapes=[*inputs, pltpu.SemaphoreType.DMA((3,)), pltpu.VMEM((heads * tile_rows, tile_cols), F32)],
        compiler_params=pltpu.CompilerParams(vmem_limit_bytes=24 << 20),
        name="finish",
    )(core[None], back, pair, gain_row, weight_t)
    everyone = pltpu.with_memory_space_constraint(exchange(last, ALL), pltpu.VMEM)
    attended, pair_gradient = pl.pallas_call(
        output_kernel,
        in_specs=[vmem] * 4,
        out_shape=[shape(pair.shape, BF16), shape(pair.shape, F32)],
        scratch_shapes=[pltpu.VMEM((tile, channels), F32)],
        compiler_params=pltpu.CompilerParams(vmem_limit_bytes=24 << 20),
        name="output",
    )(back, d_normed, pair, gain_row)
    projection_grad, bias_weight_grad, gain_gradient = pl.pallas_call(
        functools.partial(gather_kernel, n_row, n_col),
        in_specs=[vmem],
        out_shape=[shape(projections.shape, F32), shape((heads, channels), F32), shape((1, channels), F32)],
        scratch_shapes=[pltpu.VMEM((2, 5 * half, channels), F32)],
        compiler_params=pltpu.CompilerParams(vmem_limit_bytes=24 << 20),
        name="gather",
    )(everyone)
    return (attended, pair_gradient, projection_grad, bias_weight_grad.T, gain_gradient[0])


def solution(mesh):
    torus = Mesh(mesh.devices.reshape(2, 4, 2, 2, 4), ALL)
    in_specs = (P(ROW, COL, None), P(), P(), P(), P(), P(ROW, COL, None))
    out_specs = (P(ROW, COL, None), P(ROW, COL, None), P(), P(), P())
    return jax.shard_map(
        shards, mesh=torus, in_specs=in_specs, out_specs=out_specs, check_vma=False
    )
```
